32 devices in a mesh: dp: 8 (over z, y), seq: 4 (over x, core).
Axes of the slice: x: 2, y: 2, z: 4, core: 2. Of those that a mesh axis runs over, the one named last changes fastest.
Arguments:
- prompt_in: bfloat16 [16, 512, 768], P('dp', 'seq'), may hold values from -6 to 6
- cont_in: bfloat16 [16, 512, 768], P('dp', 'seq'), may hold values from -6 to 6
- enc_out: bfloat16 [16, 256, 768], P('dp', 'seq'), may hold values from -6 to 6
- prefix: int32 [16], P('dp'), may hold values from 128 to 512, as said below
- prompt_cot: bfloat16 [16, 512, 768], P('dp', 'seq'), may hold values from -6 to 6
- cont_cot: bfloat16 [16, 512, 768], P('dp', 'seq'), may hold values from -6 to 6
- self_query: bfloat16 [768, 768], P(('dp', 'seq')), may hold values from -0.21875 to 0.21875
- self_qbias: bfloat16 [768], P(('dp', 'seq')), may hold values from -1.75 to 1.75
- self_key: bfloat16 [768, 768], P(('dp', 'seq')), may hold values from -0.21875 to 0.21875
- self_value: bfloat16 [768, 768], P(('dp', 'seq')), may hold values from -0.21875 to 0.21875
- self_vbias: bfloat16 [768], P(('dp', 'seq')), may hold values from -1.75 to 1.75
- self_out: bfloat16 [768, 768], P(('dp', 'seq')), may hold values from -3.5 to 3.5
- self_obias: bfloat16 [768], P(('dp', 'seq')), may hold values from -1.75 to 1.75
- gain_one: bfloat16 [768], P(('dp', 'seq')), may hold values from 0.5 to 1.5
- shift_one: bfloat16 [768], P(('dp', 'seq')), may hold values from -1.75 to 1.75
- cross_query: bfloat16 [768, 768], P(('dp', 'seq')), may hold values from -0.21875 to 0.21875
- cross_qbias: bfloat16 [768], P(('dp', 'seq')), may hold values from -1.75 to 1.75
- cross_key: bfloat16 [768, 768], P(('dp', 'seq')), may hold values from -0.21875 to 0.21875
- cross_value: bfloat16 [768, 768], P(('dp', 'seq')), may hold values from -0.21875 to 0.21875
- cross_vbias: bfloat16 [768], P(('dp', 'seq')), may hold values from -1.75 to 1.75
- cross_out: bfloat16 [768, 768], P(('dp', 'seq')), may hold values from -3 to 3
- cross_obias: bfloat16 [768], P(('dp', 'seq')), may hold values from -1.75 to 1.75
- gain_two: bfloat16 [768], P(('dp', 'seq')), may hold values from 0.5 to 1.5
- shift_two: bfloat16 [768], P(('dp', 'seq')), may hold values from -1.75 to 1.75
- inner_mat: bfloat16 [768, 3072], P(('dp', 'seq')), may hold values from -0.21875 to 0.21875
- inner_bias: bfloat16 [3072], P(('dp', 'seq')), may hold values from -1.75 to 1.75
- outer_mat: bfloat16 [3072, 768], P(('dp', 'seq')), may hold values from -0.109375 to 0.109375
- outer_bias: bfloat16 [768], P(('dp', 'seq')), may hold values from -1.75 to 1.75
- gain_three: bfloat16 [768], P(('dp', 'seq')), may hold values from 0.5 to 1.5
- shift_three: bfloat16 [768], P(('dp', 'seq')), may hold values from -1.75 to 1.75
Outputs:
- prompt_out: bfloat16 [16, 512, 768], P('dp', 'seq')
- cont_out: bfloat16 [16, 512, 768], P('dp', 'seq')
- prompt_grad: bfloat16 [16, 512, 768], P('dp', 'seq')
- cont_grad: bfloat16 [16, 512, 768], P('dp', 'seq')
- enc_grad: bfloat16 [16, 256, 768], P('dp', 'seq')
- grad_self_query: float32 [768, 768], P(('dp', 'seq'))
- grad_self_qbias: float32 [768], P(('dp', 'seq'))
- grad_self_key: float32 [768, 768], P(('dp', 'seq'))
- grad_self_value: float32 [768, 768], P(('dp', 'seq'))
- grad_self_vbias: float32 [768], P(('dp', 'seq'))
- grad_self_out: float32 [768, 768], P(('dp', 'seq'))
- grad_self_obias: float32 [768], P(('dp', 'seq'))
- grad_gain_one: float32 [768], P(('dp', 'seq'))
- grad_shift_one: float32 [768], P(('dp', 'seq'))
- grad_cross_query: float32 [768, 768], P(('dp', 'seq'))
- grad_cross_qbias: float32 [768], P(('dp', 'seq'))
- grad_cross_key: float32 [768, 768], P(('dp', 'seq'))
- grad_cross_value: float32 [768, 768], P(('dp', 'seq'))
- grad_cross_vbias: float32 [768], P(('dp', 'seq'))
- grad_cross_out: float32 [768, 768], P(('dp', 'seq'))
- grad_cross_obias: float32 [768], P(('dp', 'seq'))
- grad_gain_two: float32 [768], P(('dp', 'seq'))
- grad_shift_two: float32 [768], P(('dp', 'seq'))
- grad_inner_mat: float32 [768, 3072], P(('dp', 'seq'))
- grad_inner_bias: float32 [3072], P(('dp', 'seq'))
- grad_outer_mat: float32 [3072, 768], P(('dp', 'seq'))
- grad_outer_bias: float32 [768], P(('dp', 'seq'))
- grad_gain_three: float32 [768], P(('dp', 'seq'))
- grad_shift_three: float32 [768], P(('dp', 'seq'))
The draws below stay inside these ranges and needn't reach their ends.
Inputs may be any that keep to these rules, and one draw needn't show every extreme that they name: `prefix`: some group's continuation follows the whole prompt and some other group's follows its first 128 positions.
All inputs are finite; a program needn't handle non-finite values.
Results may differ from the reference program's by a relative error of at most 0.025.
Values may be sent and summed in bfloat16 or wider, within the bound.
No kernel may reach another device: no remote copies, remote signals or barrier semaphores. Data moves between devices by JAX's collectives and lax.ppermute only.
A program may use at most 256 MiB of HBM per device.

```python
import jax
import jax.numpy as jnp
from jax import lax

D = 768
H = 12
DH = 64
FF = 3072
CONT = 512
ENC = 256
PROMPT = 512
GROUPS = 16


def draw_prefix(key, part):
    first_key, second_key, third_key = jax.random.split(key, 3)
    values = jax.random.randint(first_key, (GROUPS,), PROMPT // 4, PROMPT + 1, dtype=jnp.int32)
    longest = jax.random.randint(second_key, (), 0, GROUPS, dtype=jnp.int32)
    shortest = (longest + jax.random.randint(third_key, (), 1, GROUPS, dtype=jnp.int32)) % GROUPS
    values = values.at[longest].set(PROMPT).at[shortest].set(PROMPT // 4)
    return values.astype(jnp.int32)


def spiked(values, own_key, source, target, blocks, factor):
    def block_of(axis_at):
        return (jnp.arange(values.shape[axis_at]) // (values.shape[axis_at] // blocks)).reshape((-1,) + (1,) * (values.ndim - 1 - axis_at))

    one_side = jax.random.permutation(own_key, blocks)[block_of(target)]
    far = (block_of(target) + blocks // 2) % blocks
    return jnp.where((block_of(source) == one_side) | (block_of(source) == far), factor * values, values)


def shard_levels(rng, dims, shards, least, high):
    def one(dim, blocks):
        heights = jax.random.uniform(jax.random.fold_in(jax.random.fold_in(rng, 6), dim), (blocks,), jnp.float32, least / len(shards), high / len(shards))
        return jnp.repeat(jnp.exp(heights), dims[dim] // blocks).reshape((-1,) + (1,) * (len(dims) - dim - 1))

    loudness = one(*shards[0])
    for cut in shards[1:]:
        loudness = loudness * one(*cut)
    return loudness


def bell_draw(key, dims, deviation, most, cuts=(), kind=jnp.bfloat16):
    values = jax.random.normal(key, dims, jnp.float32) * deviation
    if len(cuts) > 0:
        values = shard_levels(key, dims, cuts, -0.22, 0.18) * values
    return jnp.clip(values, min=-most, max=most).astype(kind)


def noise_with(rng, dims, scale, most, cuts, heavy, kind=jnp.bfloat16):
    array = scale * jax.random.normal(rng, dims, jnp.float32)
    if cuts:
        array = array * shard_levels(rng, dims, cuts, -0.22, 0.18)
    return jnp.clip(spiked(array, jax.random.fold_in(rng, 3), *heavy), -most, most).astype(kind)


def setup_inputs(seed: int = 0) -> dict:
    streams_of = jax.random.split(jax.random.key(seed), 31)
    return {
        "prompt_in": noise_with(streams_of[0], (GROUPS, PROMPT, D), 1.0, 6.0, ((0, 8), (1, 4)), (0, 2, 8, 2.0)),
        "cont_in": bell_draw(streams_of[1], (GROUPS, CONT, D), 1.0, 6.0, ((0, 8), (1, 4))),
        "enc_out": bell_draw(streams_of[2], (GROUPS, ENC, D), 1.0, 6.0, ((0, 8), (1, 4))),
        "prefix": draw_prefix(jax.random.fold_in(streams_of[30], 71), 0),
        "prompt_cot": bell_draw(streams_of[4], (GROUPS, PROMPT, D), 1.0, 6.0, ((0, 8), (1, 4))),
        "cont_cot": bell_draw(streams_of[5], (GROUPS, CONT, D), 1.0, 6.0, ((0, 8), (1, 4))),
        "self_query": bell_draw(streams_of[6], (D, D), D ** -0.5, 0.21875, ((0, 32),)),
        "self_qbias": bell_draw(streams_of[7], (D,), 0.3, 1.75, ((0, 32),)),
        "self_key": bell_draw(streams_of[8], (D, D), D ** -0.5, 0.21875, ((0, 32),)),
        "self_value": bell_draw(streams_of[9], (D, D), D ** -0.5, 0.21875, ((0, 32),)),
        "self_vbias": bell_draw(streams_of[10], (D,), 0.3, 1.75, ((0, 32),)),
        "self_out": bell_draw(streams_of[11], (D, D), 3 ** -0.5, 3.5, ((0, 32),)),
        "self_obias": bell_draw(streams_of[12], (D,), 0.3, 1.75, ((0, 32),)),
        "gain_one": jnp.clip(1.0 + 0.1 * jax.random.normal(streams_of[13], (D,), jnp.float32), 0.5, 1.5).astype(jnp.bfloat16),
        "shift_one": bell_draw(streams_of[14], (D,), 0.3, 1.75, ((0, 32),)),
        "cross_query": bell_draw(streams_of[15], (D, D), D ** -0.5, 0.21875, ((0, 32),)),
        "cross_qbias": bell_draw(streams_of[16], (D,), 0.3, 1.75, ((0, 32),)),
        "cross_key": bell_draw(streams_of[17], (D, D), D ** -0.5, 0.21875, ((0, 32),)),
        "cross_value": bell_draw(streams_of[18], (D, D), D ** -0.5, 0.21875, ((0, 32),)),
        "cross_vbias": bell_draw(streams_of[19], (D,), 0.3, 1.75, ((0, 32),)),
        "cross_out": bell_draw(streams_of[20], (D, D), 4 ** -0.5, 3.0, ((0, 32),)),
        "cross_obias": bell_draw(streams_of[21], (D,), 0.3, 1.75, ((0, 32),)),
        "gain_two": jnp.clip(1.0 + 0.1 * jax.random.normal(streams_of[22], (D,), jnp.float32), 0.5, 1.5).astype(jnp.bfloat16),
        "shift_two": bell_draw(streams_of[23], (D,), 0.3, 1.75, ((0, 32),)),
        "inner_mat": bell_draw(streams_of[24], (D, FF), D ** -0.5, 0.21875, ((0, 32),)),
        "inner_bias": bell_draw(streams_of[25], (FF,), 0.3, 1.75, ((0, 32),)),
        "outer_mat": bell_draw(streams_of[26], (FF, D), FF ** -0.5, 0.109375, ((0, 32),)),
        "outer_bias": bell_draw(streams_of[27], (D,), 0.3, 1.75, ((0, 32),)),
        "gain_three": jnp.clip(1.0 + 0.1 * jax.random.normal(streams_of[28], (D,), jnp.float32), 0.5, 1.5).astype(jnp.bfloat16),
        "shift_three": bell_draw(streams_of[29], (D,), 0.3, 1.75, ((0, 32),)),
    }


highest = lax.Precision.HIGHEST

@jax.custom_vjp
def low(v):
    return lax.optimization_barrier(v.astype(jnp.bfloat16)).astype(jnp.float32)

@jax.custom_vjp
def low_back(v):
    return v

def low_keep(v):
    return (low(v), None)

def low_pass(kept, grad):
    return (grad,)

def back_keep(v):
    return (v, None)

def back_low(kept, grad):
    return (low(grad),)
low.defvjp(low_keep, low_pass)
low_back.defvjp(back_keep, back_low)

def rounded(value):
    return low(low_back(value))

def matmul(left, right):
    return jnp.dot(left, right, precision=highest)

def normalize(values, gain, shift):
    centred = values - lax.optimization_barrier(jnp.mean(values, axis=-1, keepdims=True))
    scale = lax.rsqrt(lax.optimization_barrier(jnp.mean(centred * centred, axis=-1, keepdims=True)) + 1e-05)
    return centred * scale * gain + shift

def attend(queries, keys, values, allowed):
    count = queries.shape[0]
    length = keys.shape[0]
    query_heads = queries.reshape(count, H, DH)
    key_heads = keys.reshape(length, H, DH)
    value_heads = values.reshape(length, H, DH)
    scores = low_back(jnp.einsum('qhd,khd->hqk', query_heads, key_heads, precision=highest))
    scores = jnp.where(allowed[None], scores, -1e+30)
    top = lax.optimization_barrier(jnp.max(scores, axis=-1, keepdims=True))
    expd = jnp.exp(scores - top)
    probs = low(expd / lax.optimization_barrier(jnp.sum(expd, axis=-1, keepdims=True)))
    mixed = jnp.einsum('hqk,khd->qhd', probs, value_heads, precision=highest)
    return rounded(mixed.reshape(count, H * DH))

def layer(weights, prompt_x, cont_x, encoder, offset):
    self_query, self_qbias, self_key, self_value, self_vbias, self_out, self_obias, gain_one, shift_one, cross_query, cross_qbias, cross_key, cross_value, cross_vbias, cross_out, cross_obias, gain_two, shift_two, inner_mat, inner_bias, outer_mat, outer_bias, gain_three, shift_three = weights
    tokens = jnp.concatenate([prompt_x, cont_x], axis=0)
    total = PROMPT + CONT
    row_ids = jnp.arange(total, dtype=jnp.int32)[:, None]
    col_ids = jnp.arange(total, dtype=jnp.int32)[None, :]
    causal = col_ids <= row_ids
    prompt_side = (row_ids < PROMPT) & causal
    cont_side = (row_ids >= PROMPT) & ((col_ids < offset) | (col_ids >= PROMPT) & causal)
    allowed = prompt_side | cont_side
    queries = rounded((matmul(tokens, self_query) + self_qbias) * 0.125)
    keys = low(matmul(tokens, self_key))
    values = low(matmul(tokens, self_value) + self_vbias)
    mixed = attend(queries, keys, values, allowed)
    first = normalize(tokens + low_back(matmul(mixed, self_out) + self_obias), gain_one, shift_one)
    cross_queries = rounded((matmul(low(first), cross_query) + cross_qbias) * 0.125)
    cross_keys = low(matmul(encoder, cross_key))
    cross_values = low(matmul(encoder, cross_value) + cross_vbias)
    everywhere = jnp.ones((total, encoder.shape[0]), dtype=jnp.bool_)
    cross_mixed = attend(cross_queries, cross_keys, cross_values, everywhere)
    second = normalize(first + low_back(matmul(cross_mixed, cross_out) + cross_obias), gain_two, shift_two)
    inner = low_back(matmul(low(second), inner_mat) + inner_bias)
    active = low(jax.nn.gelu(inner, approximate=False))
    result = normalize(second + low_back(matmul(active, outer_mat) + outer_bias), gain_three, shift_three)
    return (result[:PROMPT], result[PROMPT:])

def reference(prompt_in, cont_in, enc_out, prefix, prompt_cot, cont_cot, self_query, self_qbias, self_key, self_value, self_vbias, self_out, self_obias, gain_one, shift_one, cross_query, cross_qbias, cross_key, cross_value, cross_vbias, cross_out, cross_obias, gain_two, shift_two, inner_mat, inner_bias, outer_mat, outer_bias, gain_three, shift_three):
    params = tuple((item.astype(jnp.float32) for item in (self_query, self_qbias, self_key, self_value, self_vbias, self_out, self_obias, gain_one, shift_one, cross_query, cross_qbias, cross_key, cross_value, cross_vbias, cross_out, cross_obias, gain_two, shift_two, inner_mat, inner_bias, outer_mat, outer_bias, gain_three, shift_three)))

    def one_group(totals, items):
        prompt_x, cont_x, enc_x, offset, prompt_dy, cont_dy = items

        def forward(weights, prompt_f, cont_f, enc_f):
            return layer(weights, prompt_f, cont_f, enc_f, offset)
        outputs, pullback = jax.vjp(forward, params, prompt_x.astype(jnp.float32), cont_x.astype(jnp.float32), enc_x.astype(jnp.float32))
        grads, prompt_back, cont_back, enc_back = pullback((prompt_dy.astype(jnp.float32), cont_dy.astype(jnp.float32)))
        totals = tuple((first + second for first, second in zip(totals, grads)))
        return (totals, (outputs[0].astype(jnp.bfloat16), outputs[1].astype(jnp.bfloat16), prompt_back.astype(jnp.bfloat16), cont_back.astype(jnp.bfloat16), enc_back.astype(jnp.bfloat16)))
    zeros = tuple((jnp.zeros_like(item) for item in params))
    totals, results = lax.scan(one_group, zeros, (prompt_in, cont_in, enc_out, prefix, prompt_cot, cont_cot))
    return (results[0], results[1], results[2], results[3], results[4], totals[0], totals[1], totals[2], totals[3], totals[4], totals[5], totals[6], totals[7], totals[8], totals[9], totals[10], totals[11], totals[12], totals[13], totals[14], totals[15], totals[16], totals[17], totals[18], totals[19], totals[20], totals[21], totals[22], totals[23])
```

```python
import jax
import jax.numpy as jnp
from jax import lax
from jax.experimental import pallas as pl
from jax.experimental.pallas import tpu as pltpu
from jax.sharding import PartitionSpec as P

HEADS = 12
VMEM_LIMIT = 60 * 1024 * 1024
NEG = -1e30


def matmul(left, right):
    return jnp.dot(left, right, preferred_element_type=jnp.float32)


def contract_rows(left, right):
    return lax.dot_general(
        left, right, (((0,), (0,)), ((), ())), preferred_element_type=jnp.float32
    )


def times_transpose(left, right):
    return lax.dot_general(
        left, right, (((1,), (1,)), ((), ())), preferred_element_type=jnp.float32
    )


def widen(values):
    return values.astype(jnp.float32)


def low(values):
    return values.astype(jnp.bfloat16)


def normalize(values, gain, shift):
    centred = values - jnp.mean(values, axis=-1, keepdims=True)
    scale = lax.rsqrt(jnp.mean(centred * centred, axis=-1, keepdims=True) + 1e-05)
    return centred * scale * gain + shift


def norm_backward(values, gain, upstream):
    centred = values - jnp.mean(values, axis=-1, keepdims=True)
    scale = lax.rsqrt(jnp.mean(centred * centred, axis=-1, keepdims=True) + 1e-05)
    normed = centred * scale
    scaled = upstream * gain
    result = scale * (
        scaled
        - jnp.mean(scaled, axis=-1, keepdims=True)
        - normed * jnp.mean(scaled * normed, axis=-1, keepdims=True)
    )
    return (
        result,
        jnp.sum(upstream * normed, axis=0, keepdims=True),
        jnp.sum(upstream, axis=0, keepdims=True),
    )


(
    SELF_Q,
    SELF_V,
    SELF_O,
    GAIN_ONE,
    SHIFT_ONE,
    CROSS_Q,
    CROSS_V,
    CROSS_O,
    GAIN_TWO,
    SHIFT_TWO,
    OUTER_B,
    GAIN_THREE,
    SHIFT_THREE,
    INNER_B,
) = range(14)


def pack_vectors(vectors, width):
    def kernel(*refs):
        out_ref = refs[-1]
        out_ref[...] = jnp.zeros_like(out_ref)
        for i, ref in enumerate(refs[:-1]):
            size = ref.shape[1]
            at = 128 * (i // 8)
            out_ref[i % 8 : i % 8 + 1, at : at + size] = ref[...]

    return pl.pallas_call(
        kernel,
        out_shape=jax.ShapeDtypeStruct((8, width), vectors[0].dtype),
        name="pack_vectors",
    )(*[v[None, :] for v in vectors])


class Call:
    def __init__(self, name, grid):
        self.name, self.grid = name, grid
        self.ins, self.in_specs, self.out_shapes, self.out_specs = [], [], [], []
        self.flops, self.bytes, self.exps = 0, 0, 0

    def whole(self, array):
        zeros = (0,) * array.ndim
        self.blocked(array, array.shape, lambda *g: zeros, buffers=1)

    def blocked(self, array, block, index, buffers=2):
        mode = {} if buffers == 2 else {"pipeline_mode": pl.Buffered(buffers)}
        self.ins.append(array)
        self.in_specs.append(pl.BlockSpec(block, index, **mode))
        self.bytes += array.size * array.dtype.itemsize

    def scalars(self, array):
        self.ins.append(array)
        self.in_specs.append(pl.BlockSpec(memory_space=pltpu.SMEM))

    def weight(self, weight):
        array, block, index = weight
        self.ins.append(array)
        self.in_specs.append(pl.BlockSpec(block, lambda *g: index, pipeline_mode=pl.Buffered(1)))
        self.bytes += array.shape[-1] ** 2 * 2

    def out(self, shape, dtype, block=None, index=None):
        zeros = (0,) * len(shape)
        self.out_shapes.append(jax.ShapeDtypeStruct(shape, dtype))
        self.out_specs.append(pl.BlockSpec(block or shape, index or (lambda *g: zeros)))
        size = 1
        for n in shape:
            size *= n
        self.bytes += size * jnp.dtype(dtype).itemsize

    def run(self, kernel, scratch=()):
        return pl.pallas_call(
            kernel,
            grid=self.grid,
            in_specs=self.in_specs,
            out_specs=self.out_specs,
            out_shape=self.out_shapes,
            scratch_shapes=list(scratch),
            compiler_params=pltpu.CompilerParams(vmem_limit_bytes=VMEM_LIMIT),
            cost_estimate=pl.CostEstimate(
                flops=int(self.flops), bytes_accessed=int(self.bytes), transcendentals=int(self.exps)
            ),
            name=self.name,
        )(*self.ins)


class Halves:
    def __init__(self, call, count, owners, owned_rows, width, heads=None, index=None):
        self.owned_rows = owned_rows
        self.even = owned_rows % 8 == 0
        if self.even:
            shape, outs = (owners // 2, count, owned_rows, width), 2
            block = (heads or owners // 2, 1 if index else count, owned_rows, width)
        else:
            shape, outs = (count, owners * owned_rows, width), 1
            block = (1 if index else count, 2 * (heads or owners // 2) * owned_rows, width)
        for _ in range(outs):
            if index is None:
                call.out(shape, jnp.bfloat16)
            elif self.even:
                call.out(shape, jnp.bfloat16, block, lambda *g: index(*g) + (0, 0))
            else:
                call.out(shape, jnp.bfloat16, block, lambda *g: index(*g)[::-1] + (0,))
        self.outs = outs

    def store(self, refs, at, value, mine):
        if not self.even:
            refs[0][at] = low(value)
            return
        parts = value.reshape(-1, 2, self.owned_rows, value.shape[-1])
        first, second = low(parts[:, 0]), low(parts[:, 1])
        refs[0][:, at] = jnp.where(mine == 0, first, second)
        refs[1][:, at] = jnp.where(mine == 0, second, first)

    def pair(self, results, mine):
        if self.even:
            return tuple(results)
        whole = results[0]
        parts = whole.reshape(whole.shape[0], -1, 2, self.owned_rows, whole.shape[-1])
        return tuple(
            lax.dynamic_index_in_dim(parts, which, 2, keepdims=False).transpose(1, 0, 2, 3)
            for which in (mine, 1 - mine)
        )


def load(ref):
    value = ref[...]
    return value.reshape(-1, value.shape[-1])


def row(vecs_ref, index):
    return vecs_ref[index : index + 1, :]


def fill_bias(bias_ref, chunk, rows, ids_ref):
    half, block = rows // 2, rows // 4
    key = lax.broadcasted_iota(jnp.int32, (rows, rows), 0)
    query = lax.broadcasted_iota(jnp.int32, (rows, rows), 1)
    key_block = jnp.where(
        lax.rem(key, half) < block, ids_ref[2 * chunk], ids_ref[2 * chunk + 1]
    )
    query_block = jnp.where(lax.rem(query, half) < block, ids_ref[0], ids_ref[1])
    key_place = key_block * block + lax.rem(key, block)
    query_place = query_block * block + lax.rem(query, block)
    causal = key_place <= query_place
    prompt_key = key < half
    prompt_query = query < half
    allowed = (prompt_key & prompt_query & causal) | (
        jnp.logical_not(prompt_query)
        & ((prompt_key & (key_place < ids_ref[4])) | (jnp.logical_not(prompt_key) & causal))
    )
    bias_ref[chunk] = jnp.where(allowed, 0.0, NEG)


def lane_masks(values):
    lane = lax.broadcasted_iota(jnp.int32, values.shape, 1)
    zero = jnp.zeros_like(values)
    first = lane < values.shape[1] // 2
    return jnp.where(first, values, zero), jnp.where(first, zero, values)


def attend_pair(queries, keys, values, bias_ref, log_ref):
    queries = lane_masks(queries)
    outs = []
    for head in range(2):
        scores = []
        for chunk in range(2):
            part = times_transpose(keys[chunk], queries[head])
            scores.append(part if bias_ref is None else part + bias_ref[chunk])
        top = jnp.maximum(
            scores[0].max(axis=0, keepdims=True), scores[1].max(axis=0, keepdims=True)
        )
        total, mixed = 0.0, 0.0
        for chunk in range(2):
            weights = jnp.exp(scores[chunk] - top)
            total = total + weights.sum(axis=0, keepdims=True)
            mixed = mixed + contract_rows(values[chunk], low(weights))
        outs.append(mixed * (1.0 / total))
        log_ref[0, head : head + 1, :] = top + jnp.log(total)
    lane = lax.broadcasted_iota(jnp.int32, outs[0].shape, 0)
    return low(jnp.where(lane < outs[0].shape[0] // 2, outs[0], outs[1]).T)


def attend_pair_backward(queries, keys, values, bias_ref, log_ref, mixed, upstream):
    queries = lane_masks(queries)
    ups = lane_masks(upstream)
    product = widen(mixed) * widen(upstream)
    high = low(product)
    rest = low(product - widen(high))
    pair = product.shape[1]
    lane = lax.broadcasted_iota(jnp.int32, (8, pair), 1)
    line = lax.broadcasted_iota(jnp.int32, (8, pair), 0)
    pick = jnp.where(
        ((lane < pair // 2) & (line == 0)) | ((lane >= pair // 2) & (line == 1)), 1.0, 0.0
    ).astype(jnp.bfloat16)
    delta = times_transpose(pick, high) + times_transpose(pick, rest)
    dq = 0.0
    dk = [0.0, 0.0]
    dv = [0.0, 0.0]
    for head in range(2):
        for chunk in range(2):
            part = times_transpose(keys[chunk], queries[head])
            if bias_ref is not None:
                part = part + bias_ref[chunk]
            probs = jnp.exp(part - log_ref[0, head : head + 1, :])
            prob_grad = times_transpose(values[chunk], ups[head])
            score_grad = low(probs * (prob_grad - delta[head : head + 1, :]))
            dv[chunk] = dv[chunk] + matmul(low(probs), ups[head])
            dk[chunk] = dk[chunk] + matmul(score_grad, queries[head])
            dq = dq + contract_rows(lane_masks(keys[chunk])[head], score_grad)
    return low(dq.T), dk, dv


def project_kernel(scaled, x_ref, *refs):
    vecs_ref = refs[-3] if scaled else refs[-2]
    values = x_ref[...]
    if scaled:
        wq_ref, wk_ref, wv_ref = refs[:3]
        q_ref, kv_ref = refs[-2:]
        q_ref[...] = low((matmul(values, load(wq_ref)) + row(vecs_ref, SELF_Q)) * 0.125)
        bias = row(vecs_ref, SELF_V)
    else:
        wk_ref, wv_ref = refs[:2]
        kv_ref = refs[-1]
        bias = row(vecs_ref, CROSS_V)
    kv_ref[0] = low(matmul(values, load(wk_ref)))
    kv_ref[1] = low(matmul(values, load(wv_ref)) + bias)


def project(tokens, weights, vecs):
    rows, width = tokens.shape
    scaled = len(weights) == 3
    call = Call("project", (1,))
    call.whole(tokens)
    for weight in weights:
        call.weight(weight)
    call.whole(vecs)
    if scaled:
        call.out((rows, width), jnp.bfloat16)
    call.out((2, rows, width), jnp.bfloat16)
    call.flops = 2 * len(weights) * rows * width * width

    def kernel(*refs):
        project_kernel(scaled, *refs)

    return call.run(kernel)


def lanes_of(width):
    lanes = 2 * (width // HEADS)

    def at(h):
        return pl.ds(pl.multiple_of(h * lanes, lanes), lanes)

    return lanes, at


def self_attend(ids, queries, own, other):
    rows, width = queries.shape
    pairs = HEADS // 2
    lanes, _ = lanes_of(width)
    call = Call("self_attend", (pairs,))
    call.scalars(ids)
    call.blocked(queries, (rows, lanes), lambda h: (0, h))
    for array in (own, other):
        call.blocked(array, (2, rows, lanes), lambda h: (0, 0, h))
    call.out((rows, width), jnp.bfloat16, (rows, lanes), lambda h: (0, h))
    call.out((pairs, 2, rows), jnp.float32, (1, 2, rows), lambda h: (h, 0, 0))
    call.flops = 16 * rows * rows * width
    call.exps = 2 * rows * rows * HEADS

    def kernel(ids_ref, q_ref, own_ref, other_ref, mixed_ref, log_ref, bias_ref):
        @pl.when(pl.program_id(0) == 0)
        def _():
            for chunk in range(2):
                fill_bias(bias_ref, chunk, rows, ids_ref)

        keys, values = (own_ref[0], other_ref[0]), (own_ref[1], other_ref[1])
        mixed_ref[...] = attend_pair(q_ref[...], keys, values, bias_ref, log_ref)

    return call.run(kernel, [pltpu.VMEM((2, rows, rows), jnp.float32)])


def self_finish(tokens, mixed, out_weight, query_weight, vecs):
    rows, width = tokens.shape
    call = Call("self_finish", (1,))
    call.whole(tokens)
    call.whole(mixed)
    call.weight(out_weight)
    call.weight(query_weight)
    call.whole(vecs)
    call.out((rows, width), jnp.float32)
    call.out((rows, width), jnp.bfloat16)
    call.out((rows, width), jnp.bfloat16)
    call.flops = 4 * rows * width * width

    def kernel(x_ref, mixed_ref, wo_ref, wq_ref, vecs_ref, pre_ref, low_ref, next_ref):
        pre = widen(x_ref[...]) + matmul(mixed_ref[...], load(wo_ref)) + row(vecs_ref, SELF_O)
        pre_ref[...] = pre
        first = low(normalize(pre, row(vecs_ref, GAIN_ONE), row(vecs_ref, SHIFT_ONE)))
        low_ref[...] = first
        next_ref[...] = low((matmul(first, load(wq_ref)) + row(vecs_ref, CROSS_Q)) * 0.125)

    return call.run(kernel)


def cross_attend(queries, own, other, first_pre, out_weight, vecs):
    rows, width = queries.shape
    key_rows = own.shape[1]
    pairs = HEADS // 2
    lanes, at = lanes_of(width)
    call = Call("cross_attend", (pairs,))
    call.blocked(queries, (rows, lanes), lambda h: (0, h))
    for array in (own, other):
        call.blocked(array, (2, key_rows, lanes), lambda h: (0, 0, h))
    call.whole(first_pre)
    call.weight(out_weight)
    call.whole(vecs)
    call.out((rows, width), jnp.bfloat16)
    call.out((pairs, 2, rows), jnp.float32, (1, 2, rows), lambda h: (h, 0, 0))
    call.out((rows, width), jnp.float32)
    call.out((rows, width), jnp.bfloat16)
    call.flops = 16 * rows * key_rows * width + 2 * rows * width * width
    call.exps = 2 * rows * key_rows * HEADS

    def kernel(
        q_ref, own_ref, other_ref, first_ref, wo_ref, vecs_ref, mixed_ref, log_ref, pre_ref, low_ref
    ):
        step = pl.program_id(0)
        keys, values = (own_ref[0], other_ref[0]), (own_ref[1], other_ref[1])
        mixed_ref[:, at(step)] = attend_pair(q_ref[...], keys, values, None, log_ref)

        @pl.when(step == pairs - 1)
        def _():
            first = normalize(first_ref[...], row(vecs_ref, GAIN_ONE), row(vecs_ref, SHIFT_ONE))
            pre = first + matmul(mixed_ref[...], load(wo_ref)) + row(vecs_ref, CROSS_O)
            pre_ref[...] = pre
            low_ref[...] = low(normalize(pre, row(vecs_ref, GAIN_TWO), row(vecs_ref, SHIFT_TWO)))

    return call.run(kernel)


def feed_blocks(call, feed, width, chunks, owned_rows):
    owners = feed.shape[0]
    hidden_rows = chunks * owned_rows
    if owned_rows % 8 == 0:
        call.blocked(feed, (owners, owned_rows, width), lambda i: (0, chunks + i, 0))
        call.blocked(feed, (owners // chunks, hidden_rows, width), lambda i: (i, 0, 0))
    else:
        parts = [
            feed[:, hidden_rows + i * owned_rows : hidden_rows + (i + 1) * owned_rows]
            for i in range(chunks)
        ]
        parts = [p.reshape(-1, width) for p in parts]
        call.blocked(jnp.concatenate(parts, axis=1), (width, width), lambda i: (0, i))
        call.blocked(feed[:, :hidden_rows].reshape(-1, width), (width, width), lambda i: (i, 0))


def feed_forward(second_pre, second_low, feed, vecs, chunks, owned_rows):
    rows, width = second_low.shape
    hidden = chunks * width
    call = Call("feed_forward", (chunks,))
    call.whole(second_pre)
    call.whole(second_low)
    feed_blocks(call, feed, width, chunks, owned_rows)
    call.whole(vecs)
    call.out((rows, hidden), jnp.bfloat16, (rows, width), lambda i: (0, i))
    call.out((rows, hidden), jnp.bfloat16, (rows, width), lambda i: (0, i))
    call.out((rows, width), jnp.float32)
    call.out((rows, width), jnp.bfloat16)
    call.flops = 4 * rows * hidden * width
    call.exps = 2 * rows * hidden

    def kernel(
        pre_ref, low_ref, inner_ref, outer_ref, vecs_ref, active_ref, slope_ref, third_ref, out_ref
    ):
        step = pl.program_id(0)

        @pl.when(step == 0)
        def _():
            second = normalize(pre_ref[...], row(vecs_ref, GAIN_TWO), row(vecs_ref, SHIFT_TWO))
            third_ref[...] = second + row(vecs_ref, OUTER_B)

        inner = matmul(low_ref[...], load(inner_ref)) + vecs_ref[pl.ds(INNER_B + step, 1), :]
        bell = 0.5 * (1.0 + lax.erf(inner * 0.7071067811865476))
        active = low(inner * bell)
        active_ref[...] = active
        density = jnp.exp(-0.5 * inner * inner) * 0.3989422804014327
        slope_ref[...] = low(bell + inner * density)
        third_ref[...] += matmul(active, load(outer_ref))

        @pl.when(step == chunks - 1)
        def _():
            out_ref[...] = low(
                normalize(third_ref[...], row(vecs_ref, GAIN_THREE), row(vecs_ref, SHIFT_THREE))
            )

    return call.run(kernel)


def feed_backward(
    ids, upstream, third_pre, second_pre, second_low, active, slope, cross_mixed, feed, out_weight, vecs,
    chunks, owned_rows,
):
    rows, width = second_low.shape
    hidden = chunks * width
    owners = width // owned_rows
    call = Call("feed_backward", (chunks,))
    call.scalars(ids)
    call.whole(upstream)
    call.whole(third_pre)
    call.whole(second_pre)
    call.whole(second_low)
    call.blocked(active, (rows, width), lambda i: (0, i))
    call.blocked(slope, (rows, width), lambda i: (0, i))
    call.whole(cross_mixed)
    feed_blocks(call, feed, width, chunks, owned_rows)
    call.weight(out_weight)
    call.whole(vecs)
    inner_half = Halves(
        call, chunks, owners, owned_rows, width, owners // 2, lambda i: (0, i)
    )
    outer_half = Halves(
        call, 1, owners, chunks * owned_rows, width, owners // 2 // chunks, lambda i: (i, 0)
    )
    out_half = Halves(call, 1, owners, owned_rows, width)
    call.out((rows, width), jnp.float32)
    call.out((rows, width), jnp.bfloat16)
    call.out((16, width), jnp.float32)
    n_in, n_half, n_outer = len(call.ins), inner_half.outs, outer_half.outs
    call.flops = 8 * rows * hidden * width + 4 * rows * width * width

    def kernel(*refs):
        (
            ids_ref, up_ref, third_ref, second_ref, low_ref, active_ref, slope_ref, mixed_ref, inner_ref,
            outer_ref, wo_ref, vecs_ref,
        ) = refs[:n_in]
        inner_grads = refs[n_in : n_in + n_half]
        outer_grads = refs[n_in + n_half : n_in + n_half + n_outer]
        out_grads = refs[n_in + n_half + n_outer : -5]
        second_grad_ref, mix_ref, sums_ref, third_low_ref, total_ref = refs[-5:]
        step = pl.program_id(0)
        mine = ids_ref[5]

        @pl.when(step == 0)
        def _():
            grad, gain_sum, shift_sum = norm_backward(
                third_ref[...], row(vecs_ref, GAIN_THREE), widen(up_ref[...])
            )
            total_ref[...] = grad
            third_low_ref[...] = low(grad)
            sums_ref[0:1, :] = gain_sum
            sums_ref[1:2, :] = shift_sum
            sums_ref[2:3, :] = jnp.sum(widen(low(grad)), axis=0, keepdims=True)

        third_low = third_low_ref[...]
        inner_low = low(times_transpose(third_low, load(outer_ref)) * widen(slope_ref[...]))
        total_ref[...] += times_transpose(inner_low, load(inner_ref))
        outer_half.store(outer_grads, 0, contract_rows(active_ref[...], third_low), mine)
        inner_half.store(inner_grads, 0, contract_rows(low_ref[...], inner_low), mine)
        sums_ref[pl.ds(8 + step, 1), :] = jnp.sum(widen(inner_low), axis=0, keepdims=True)

        @pl.when(step == chunks - 1)
        def _():
            grad, gain_sum, shift_sum = norm_backward(
                second_ref[...], row(vecs_ref, GAIN_TWO), total_ref[...]
            )
            second_grad_ref[...] = grad
            cross_low = low(grad)
            sums_ref[3:4, :] = gain_sum
            sums_ref[4:5, :] = shift_sum
            sums_ref[5:6, :] = jnp.sum(widen(cross_low), axis=0, keepdims=True)
            mix_ref[...] = low(times_transpose(cross_low, load(wo_ref)))
            out_half.store(out_grads, 0, contract_rows(mixed_ref[...], cross_low), mine)

    results = call.run(
        kernel, [pltpu.VMEM((rows, width), jnp.bfloat16), pltpu.VMEM((rows, width), jnp.float32)]
    )
    core = ids[5]
    return (
        inner_half.pair(results[:n_half], core),
        outer_half.pair(results[n_half : n_half + n_outer], core),
        out_half.pair(results[n_half + n_outer : -3], core),
    ) + tuple(results[-3:])


def cross_backward(
    ids, queries, own, other, mixed, upstream, logsum, first_low, first_pre, second_grad, self_mixed,
    query_weight, out_weight, vecs, owned_rows,
):
    rows, width = queries.shape
    key_rows = own.shape[1]
    pairs = HEADS // 2
    lanes, at = lanes_of(width)
    call = Call("cross_backward", (pairs,))
    call.scalars(ids)
    for array in (queries, mixed, upstream):
        call.blocked(array, (rows, lanes), lambda h: (0, h))
    call.blocked(logsum, (1, 2, rows), lambda h: (h, 0, 0))
    for array in (own, other):
        call.blocked(array, (2, key_rows, lanes), lambda h: (0, 0, h))
    for array in (first_low, first_pre, second_grad, self_mixed):
        call.whole(array)
    call.weight(query_weight)
    call.weight(out_weight)
    call.whole(vecs)
    for _ in range(2):
        call.out((2, key_rows, width), jnp.bfloat16, (2, key_rows, lanes), lambda h: (0, 0, h))
    call.out((rows, width), jnp.float32)
    call.out((rows, width), jnp.bfloat16)
    call.out((8, width), jnp.float32)
    half = Halves(call, 2, width // owned_rows, owned_rows, width)
    call.flops = 40 * rows * key_rows * width + 8 * rows * width * width
    call.exps = 2 * rows * key_rows * HEADS

    def kernel(
        ids_ref, q_ref, mixed_ref, up_ref, log_ref, own_ref, other_ref, low_ref, pre_ref, grad_ref,
        self_mixed_ref, wq_ref, wo_ref, vecs_ref, own_out_ref, other_out_ref, first_ref, mix_ref,
        sums_ref, *rest,
    ):
        step = pl.program_id(0)
        weights_refs, dq_ref = rest[:-1], rest[-1]
        keys, values = (own_ref[0], other_ref[0]), (own_ref[1], other_ref[1])
        dq, dk, dv = attend_pair_backward(
            q_ref[...], keys, values, None, log_ref, mixed_ref[...], up_ref[...]
        )
        dq_ref[:, at(step)] = dq
        for chunk, out in enumerate((own_out_ref, other_out_ref)):
            out[0] = low(dk[chunk])
            out[1] = low(dv[chunk])

        @pl.when(step == pairs - 1)
        def _():
            query_low = dq_ref[...]
            half.store(weights_refs, 0, contract_rows(low_ref[...], query_low) * 0.125, ids_ref[5])
            total = grad_ref[...] + times_transpose(query_low, load(wq_ref)) * 0.125
            grad, gain_sum, shift_sum = norm_backward(pre_ref[...], row(vecs_ref, GAIN_ONE), total)
            first_ref[...] = grad
            self_low = low(grad)
            mix_ref[...] = low(times_transpose(self_low, load(wo_ref)))
            half.store(weights_refs, 1, contract_rows(self_mixed_ref[...], self_low), ids_ref[5])
            sums_ref[0:1, :] = gain_sum
            sums_ref[1:2, :] = shift_sum
            sums_ref[2:3, :] = jnp.sum(widen(self_low), axis=0, keepdims=True)
            sums_ref[3:4, :] = jnp.sum(widen(query_low), axis=0, keepdims=True) * 0.125

    results = call.run(kernel, [pltpu.VMEM((rows, width), jnp.bfloat16)])
    return tuple(results[:5]) + (half.pair(results[5:], ids[5]),)


def self_backward(
    ids, queries, own, other, mixed, upstream, logsum, tokens, first_grad, query_weight, owned_rows
):
    rows, width = queries.shape
    pairs = HEADS // 2
    lanes, at = lanes_of(width)
    call = Call("self_backward", (pairs,))
    call.scalars(ids)
    for array in (queries, mixed, upstream):
        call.blocked(array, (rows, lanes), lambda h: (0, h))
    call.blocked(logsum, (1, 2, rows), lambda h: (h, 0, 0))
    for array in (own, other):
        call.blocked(array, (2, rows, lanes), lambda h: (0, 0, h))
    for array in (tokens, first_grad):
        call.whole(array)
    call.weight(query_weight)
    for _ in range(2):
        call.out((2, rows, width), jnp.bfloat16, (2, rows, lanes), lambda h: (0, 0, h))
    call.out((rows, width), jnp.float32)
    call.out((8, width), jnp.float32)
    half = Halves(call, 1, width // owned_rows, owned_rows, width)
    call.flops = 40 * rows * rows * width + 4 * rows * width * width
    call.exps = 2 * rows * rows * HEADS

    def kernel(
        ids_ref, q_ref, mixed_ref, up_ref, log_ref, own_ref, other_ref, x_ref, grad_ref, wq_ref,
        own_out_ref, other_out_ref, part_ref, sums_ref, *rest,
    ):
        weights_refs, (bias_ref, dq_ref) = rest[:-2], rest[-2:]
        step = pl.program_id(0)

        @pl.when(step == 0)
        def _():
            for chunk in range(2):
                fill_bias(bias_ref, chunk, rows, ids_ref)

        keys, values = (own_ref[0], other_ref[0]), (own_ref[1], other_ref[1])
        dq, dk, dv = attend_pair_backward(
            q_ref[...], keys, values, bias_ref, log_ref, mixed_ref[...], up_ref[...]
        )
        dq_ref[:, at(step)] = dq
        for chunk, out in enumerate((own_out_ref, other_out_ref)):
            out[0] = low(dk[chunk])
            out[1] = low(dv[chunk])

        @pl.when(step == pairs - 1)
        def _():
            query_low = dq_ref[...]
            half.store(weights_refs, 0, contract_rows(x_ref[...], query_low) * 0.125, ids_ref[5])
            part_ref[...] = grad_ref[...] + times_transpose(query_low, load(wq_ref)) * 0.125
            sums_ref[0:1, :] = jnp.sum(widen(query_low), axis=0, keepdims=True) * 0.125

    results = call.run(
        kernel,
        [pltpu.VMEM((2, rows, rows), jnp.float32), pltpu.VMEM((rows, width), jnp.bfloat16)],
    )
    return tuple(results[:4]) + (half.pair(results[4:], ids[5]),)


def key_backward(ids, tokens, mine, got, part, key_weight, value_weight, owned_rows):
    rows, width = tokens.shape
    call = Call("key_backward", (1,))
    call.scalars(ids)
    for array in (tokens, mine, got) + (() if part is None else (part,)):
        call.whole(array)
    call.weight(key_weight)
    call.weight(value_weight)
    call.out((rows, width), jnp.bfloat16)
    call.out((8, width), jnp.float32)
    half = Halves(call, 2, width // owned_rows, owned_rows, width)
    call.flops = 8 * rows * width * width

    def kernel(ids_ref, x_ref, mine_ref, got_ref, *refs):
        if part is not None:
            total, refs = refs[0][...], refs[1:]
        else:
            total = 0.0
        wk_ref, wv_ref, out_ref, sums_ref = refs[:4]
        weights_refs = refs[4:]
        values = x_ref[...]
        dk = low(widen(mine_ref[0]) + widen(got_ref[0]))
        dv = low(widen(mine_ref[1]) + widen(got_ref[1]))
        half.store(weights_refs, 0, contract_rows(values, dk), ids_ref[5])
        half.store(weights_refs, 1, contract_rows(values, dv), ids_ref[5])
        out_ref[...] = low(
            total + times_transpose(dk, load(wk_ref)) + times_transpose(dv, load(wv_ref))
        )
        sums_ref[0:1, :] = jnp.sum(widen(dv), axis=0, keepdims=True)

    results = call.run(kernel)
    return tuple(results[:2]) + (half.pair(results[2:], ids[5]),)


def flip(size, bit):
    return [(i, i ^ bit) for i in range(size)]


def swap_seq(values, bits):
    return lax.ppermute(values, "seq", flip(lax.axis_size("seq"), bits))


def tie(*values):
    return lax.optimization_barrier(values)


def bit_order(dp_size, seq_size):
    return [("dp", b) for b in range(dp_size.bit_length() - 1)][::-1] + [
        ("seq", b) for b in range(seq_size.bit_length() - 1)
    ][::-1]


class Moves:
    def __init__(self):
        self.spots = {name: lax.axis_index(name) for name in ("dp", "seq")}
        self.sizes = {name: lax.axis_size(name) for name in ("dp", "seq")}
        self.canonical = bit_order(self.sizes["dp"], self.sizes["seq"])

    def mine(self, step):
        return (self.spots[step[0]] >> step[1]) & 1

    def send(self, values, step):
        name, bit = step
        return lax.ppermute(values, name, flip(self.sizes[name], 1 << bit))


def split_sum(keep, got, at, mine):
    total = low(widen(keep) + widen(got))
    return [
        lax.dynamic_index_in_dim(total, which, at, keepdims=False) for which in (mine, 1 - mine)
    ]


def merge(keep, got, at, mine):
    shape = keep.shape
    before, after = 1, shape[-2]
    for n in shape[:at]:
        before *= n
    for n in shape[at + 1 : -2]:
        after *= n
    width = shape[-1]
    left = tuple(shape[:at] + shape[at + 1 :])
    if shape[-2] % 8:
        return split_sum(keep, got, at, mine)
    view = (before, 2, after, width)
    rows, heads = after, 1
    while rows > 256 and rows % 16 == 0:
        rows //= 2
    while heads * rows < 128 and before % (2 * heads) == 0:
        heads *= 2
    block = (heads, None, rows, width)

    def stay(i, j, mine_ref):
        return (i, mine_ref[0], j, 0)

    def go(i, j, mine_ref):
        return (i, 1 - mine_ref[0], j, 0)

    def kernel(mine_ref, keep_a, keep_b, got_a, got_b, stay_ref, go_ref):
        stay_ref[...] = low(widen(keep_a[...]) + widen(got_a[...]))
        go_ref[...] = low(widen(keep_b[...]) + widen(got_b[...]))

    size = before * after * width
    out = pl.BlockSpec((heads, rows, width), lambda i, j, mine_ref: (i, j, 0))
    keep, got = keep.reshape(view), got.reshape(view)
    results = pl.pallas_call(
        kernel,
        grid_spec=pltpu.PrefetchScalarGridSpec(
            num_scalar_prefetch=1,
            grid=(before // heads, after // rows),
            in_specs=[pl.BlockSpec(block, m) for m in (stay, go, stay, go)],
            out_specs=[out, out],
        ),
        out_shape=[jax.ShapeDtypeStruct((before, after, width), jnp.bfloat16)] * 2,
        compiler_params=pltpu.CompilerParams(vmem_limit_bytes=VMEM_LIMIT),
        cost_estimate=pl.CostEstimate(flops=2 * size, bytes_accessed=12 * size, transcendentals=0),
        name="merge",
    )(mine.reshape(1).astype(jnp.int32), keep, keep, got, got)
    return [r.reshape(left) for r in results]


class Scatter:
    def __init__(self, moves, pairs, order):
        self.moves = moves
        self.dims = [step for step in moves.canonical if step != order[0]]
        self.order = list(order)
        pieces = (2,) * len(self.dims)

        def join(arrays):
            arrays = [a.reshape(pieces + (-1, a.shape[-1])) for a in arrays]
            return arrays[0] if len(arrays) == 1 else jnp.concatenate(arrays, axis=-2)

        self.keep = join([k for k, _ in pairs])
        self.away = join([a for _, a in pairs])
        self.got = None

    def ship(self):
        self.got = self.moves.send(self.away, self.order.pop(0))
        self.away = None

    def take(self):
        got, self.got = self.got, None
        if self.order:
            step = self.order[0]
            at = self.dims.index(step)
            split = merge if self.keep.size > 2**18 else split_sum
            self.keep, self.away = split(self.keep, got, at, self.moves.mine(step))
            self.dims.pop(at)
        else:
            self.held = widen(self.keep) + widen(got)

    def total(self):
        return low(widen(self.keep) + widen(self.got))


def joined(chains):
    first = chains[0]
    chain = object.__new__(Scatter)
    chain.moves, chain.dims, chain.order, chain.got = first.moves, first.dims, first.order, None
    chain.keep = jnp.concatenate([c.keep for c in chains], axis=-2)
    chain.away = jnp.concatenate([c.away for c in chains], axis=-2)
    return chain


def receive(chains, *values):
    tied = tie(*[c.got for c in chains], *values)
    for chain, got in zip(chains, tied):
        chain.got = got
        chain.take()
    values = tied[len(chains) :]
    return values[0] if len(values) == 1 else values


def depart(chains, *values):
    tied = tie(*[c.away for c in chains], *values)
    for chain, away in zip(chains, tied):
        chain.away = away
        chain.ship()
    values = tied[len(chains) :]
    return values[0] if len(values) == 1 else values


def advance(chains, *values):
    values = receive(chains, *values)
    return depart(chains, *(values if isinstance(values, (list, tuple)) else (values,)))


class Gather:
    def __init__(self, moves, held, order, dims=()):
        self.moves, self.held, self.order, self.dims = moves, held, list(order), list(dims)

    def ship(self):
        self.got = self.moves.send(self.held, self.order[0])

    def take(self):
        step = self.order.pop(0)
        mine = self.moves.mine(step)
        first = jnp.where(mine == 0, self.held, self.got)
        second = jnp.where(mine == 0, self.got, self.held)
        self.held = jnp.stack([first, second], axis=0)
        self.dims.insert(0, step)

    def part(self, first, last, order):
        return Gather(self.moves, self.held[..., first:last, :], order, self.dims)

    def result(self):
        order = [self.dims.index(step) for step in self.moves.canonical]
        count = len(order)
        held = self.held.transpose(order + [count, count + 1])
        return held.reshape((-1,) + held.shape[-2:])


def pump(taking, shipping, *values):
    tied = tie(*[g.got for g in taking], *values)
    for gather, got in zip(taking, tied):
        gather.got = got
        gather.take()
    tied = tie(*[g.held for g in shipping], *tied[len(taking) :])
    for gather, held in zip(shipping, tied):
        gather.held = held
        gather.ship()
    values = tied[len(shipping) :]
    return values[0] if len(values) == 1 else values


def body(
    prompt_in,
    cont_in,
    enc_out,
    prefix,
    prompt_cot,
    cont_cot,
    self_query,
    self_qbias,
    self_key,
    self_value,
    self_vbias,
    self_out,
    self_obias,
    gain_one,
    shift_one,
    cross_query,
    cross_qbias,
    cross_key,
    cross_value,
    cross_vbias,
    cross_out,
    cross_obias,
    gain_two,
    shift_two,
    inner_mat,
    inner_bias,
    outer_mat,
    outer_bias,
    gain_three,
    shift_three,
):
    seq = lax.axis_index("seq")
    parts, blocks = lax.axis_size("seq"), lax.axis_size("dp")
    rows = prompt_in.shape[1]
    width = prompt_in.shape[2]
    owned_rows = self_query.shape[0]
    group = seq // 2
    ids = jnp.stack([seq, 3 - seq, seq ^ 1, 3 - (seq ^ 1), prefix[group], seq & 1]).astype(jnp.int32)

    def pick(array, index):
        return lax.dynamic_index_in_dim(array, index, 0, keepdims=False)

    vectors = [
        self_qbias,
        self_vbias,
        self_obias,
        gain_one,
        shift_one,
        cross_qbias,
        cross_vbias,
        cross_obias,
        gain_two,
        shift_two,
        outer_bias,
        gain_three,
        shift_three,
    ]
    hidden_rows = outer_mat.shape[0]
    chunks = hidden_rows // owned_rows
    tail = pack_vectors(vectors + [inner_bias], width)
    moves = Moves()
    bits = moves.canonical
    dp_bits, hi, lo = bits[:-2], bits[-2], bits[-1]
    line, near = dp_bits[:-1], dp_bits[-1]
    cut = 2 * owned_rows
    first_part = jnp.concatenate([self_query, self_key, self_value, tail], axis=0)
    feed = jnp.concatenate(
        [outer_mat]
        + [inner_mat[:, i * width : (i + 1) * width] for i in range(chunks)]
        + [self_out, cross_query, cross_key, cross_value, cross_out],
        axis=0,
    )
    one = Gather(moves, first_part, line)
    one.ship()
    first_part, feed, sent = tie(
        first_part,
        feed,
        jnp.concatenate([pick(v, 1 - group) for v in (prompt_in, cont_in, enc_out)], axis=0),
    )
    feed = lax.all_gather(feed, ("dp", "seq"), axis=0, tiled=False)
    got = swap_seq(sent, 3)
    pump([one], [one])
    while len(one.order) > 1:
        pump([one], [one])
    got = pump([one], [], got)
    one_parts = [
        one.part(0, cut, [near, hi, lo]),
        one.part(cut, first_part.shape[0], [hi, near, lo]),
    ]
    got = pump([], one_parts, got)
    got = pump(one_parts, one_parts, got)
    got = pump(one_parts, one_parts, got)
    got = pump(one_parts, [], got)

    tokens = jnp.concatenate(
        [pick(prompt_in, group), got[:rows], pick(cont_in, group), got[rows : 2 * rows]], axis=0
    )
    encoder = jnp.concatenate([pick(enc_out, group), got[2 * rows :]], axis=0)

    def square(array, index):
        if owned_rows % 8 == 0:
            return array, (array.shape[0], owned_rows, width), (0, index, 0)
        part = array[:, index * owned_rows : (index + 1) * owned_rows].reshape(-1, width)
        return part, part.shape, (0, 0)

    front, back = [g.result() for g in one_parts]
    self_query, self_key, self_value = square(front, 0), square(front, 1), square(back, 0)
    tail = back[:, owned_rows:]
    owners = parts * blocks
    slots = tail.reshape(owners, 8, -1, 128)[:, :, :2, :owned_rows]
    vecs = slots.transpose(2, 1, 0, 3).reshape(16, width)[:13]
    biases = tail[:, 5, 128 : 128 + hidden_rows].reshape(chunks, width)
    vecs = widen(jnp.concatenate([vecs, biases], axis=0))

    queries, own = project(tokens, [self_query, self_key, self_value], vecs)
    other = swap_seq(own, 1)
    cot_sent = jnp.concatenate([pick(v, 1 - group) for v in (prompt_cot, cont_cot)], axis=0)
    cot_sent, other = tie(cot_sent, other)
    cot_got = swap_seq(cot_sent, 3)
    mixed, logsum = self_attend(ids, queries, own, other)
    mixed, cot_got = tie(mixed, cot_got)
    base = 2 * chunks
    self_out, cross_query, cross_key, cross_value, cross_out = [
        square(feed, base + i) for i in range(5)
    ]
    (cross_own,) = project(encoder, [cross_key, cross_value], vecs)
    cross_other = swap_seq(cross_own, 1)
    first_pre, first_low, cross_queries = self_finish(tokens, mixed, self_out, cross_query, vecs)
    cross_mixed, cross_logsum, second_pre, second_low = cross_attend(
        cross_queries, cross_own, cross_other, first_pre, cross_out, vecs
    )
    upstream = jnp.concatenate(
        [pick(prompt_cot, group), cot_got[:rows], pick(cont_cot, group), cot_got[rows:]], axis=0
    )
    active, slope, third_pre, result = feed_forward(
        second_pre, second_low, feed, vecs, chunks, owned_rows
    )

    def send_back(own, *values):
        away = jnp.concatenate([own[rows : 2 * rows], own[3 * rows :]], axis=0)
        tied = tie(away, *values)
        return (own, swap_seq(tied[0], 3)) + tuple(tied[1:])

    def place(own, back):
        kept = (own[:rows], own[2 * rows : 3 * rows])
        back = (back[:rows], back[rows:])
        return [
            jnp.where(group == 0, jnp.stack([a, b]), jnp.stack([b, a])) for a, b in zip(kept, back)
        ]

    result, result_back, third_pre = send_back(result, third_pre)

    bits = dp_bits[::-1]
    x_first = [lo, hi] + bits
    y_first = [lo, bits[0], hi] + bits[1:]
    inner_pair, outer_pair, cross_out_pair, second_grad, cross_mix, feed_sums = feed_backward(
        ids, upstream, third_pre, second_pre, second_low, active, slope, cross_mixed, feed, cross_out,
        vecs, chunks, owned_rows,
    )
    cross_mix, result_back = tie(cross_mix, result_back)
    prompt_out, cont_out = place(result, result_back)
    outer_chain = Scatter(moves, [outer_pair], x_first)
    inner_chain = Scatter(moves, [inner_pair], y_first)
    feed_chains = [outer_chain, inner_chain]
    cross_mix = depart(feed_chains, cross_mix)
    cross_mix = advance(feed_chains, cross_mix)
    own_back, other_back, first_grad, mix, cross_sums, query_pair = cross_backward(
        ids, cross_queries, cross_own, cross_other, cross_mixed, cross_mix, cross_logsum, first_low,
        first_pre, second_grad, mixed, cross_query, self_out, vecs, owned_rows,
    )
    mix, other_back = receive(feed_chains, mix, other_back)
    got_back = swap_seq(other_back, 1)
    got_back = depart(feed_chains, got_back)
    enc_back, key_sums, key_pair = key_backward(
        ids, encoder, own_back, got_back, None, cross_key, cross_value, owned_rows
    )
    cross_chains = [
        Scatter(moves, [query_pair, cross_out_pair], x_first),
        Scatter(moves, [key_pair], y_first),
    ]
    outer_chain.got, inner_chain.got, enc_back, mix = tie(
        outer_chain.got, inner_chain.got, enc_back, mix
    )
    mix = depart(cross_chains, mix)
    rest = jnp.concatenate([c.total() for c in feed_chains], axis=-2)
    rest, mix = tie(rest, mix)
    rest = rest.reshape((-1,) + rest.shape[-2:])
    lines = [[i for i in range(blocks) if i % 2 == side] for side in range(2)]
    rest = lax.psum_scatter(
        rest, "dp", scatter_dimension=0, axis_index_groups=lines, tiled=True
    )[0]
    mix = advance(cross_chains, mix)
    self_own, self_other, part, self_sums, self_query_pair = self_backward(
        ids, queries, own, other, mixed, mix, logsum, tokens, first_grad, self_query, owned_rows
    )
    self_other = receive(cross_chains, self_other)
    self_got = swap_seq(self_other, 1)
    self_got = depart(cross_chains, self_got)
    token_grad, self_key_sums, self_key_pair = key_backward(
        ids, tokens, self_own, self_got, part, self_key, self_value, owned_rows
    )
    token_grad = receive(cross_chains, token_grad)
    sums = jnp.concatenate(
        [
            self_sums[0:1],
            self_key_sums[0:1],
            cross_sums[2:3],
            cross_sums[0:2],
            cross_sums[3:4],
            key_sums[0:1],
            feed_sums[5:6],
            feed_sums[3:5],
            feed_sums[2:3],
            feed_sums[0:2],
        ],
        axis=0,
    )
    slots = jnp.pad(sums.reshape(13, owners, owned_rows), ((0, 3), (0, 0), (0, 128 - owned_rows)))
    slots = slots.reshape(2, 8, owners, 128).transpose(2, 1, 0, 3)
    bias_sums = feed_sums[8 : 8 + chunks].reshape(owners, hidden_rows)
    slots = slots.at[:, 5, 1, :hidden_rows].set(bias_sums)
    sums = jnp.pad(low(slots).reshape(owners, 8, 256), ((0, 0), (0, 0), (0, width - 256)))
    sums = sums.reshape(-1, 2, 8, width)
    sums_pair = (
        lax.dynamic_index_in_dim(sums, seq & 1, 1, keepdims=False),
        lax.dynamic_index_in_dim(sums, 1 - (seq & 1), 1, keepdims=False),
    )
    even_chain = Scatter(moves, [self_key_pair], x_first)
    odd_chain = Scatter(moves, [self_query_pair, sums_pair], y_first)
    last = [even_chain, odd_chain]
    token_grad, token_back = send_back(token_grad)
    depart(last)
    advance(last)
    advance(last)
    receive(last)
    tail_chain = joined(last + cross_chains)
    tail_chain.ship()
    while tail_chain.got is not None:
        receive([tail_chain])
        if tail_chain.order and tail_chain.away is not None:
            tail_chain.ship()
    ends, at = [], 0
    for size, extra in ((2, 0), (1, 8), (3, 0), (2, 0)):
        ends.append((at, at + size * owned_rows))
        at += size * owned_rows + extra
    self_key_grads, self_query_grad, cross_grads, cross_key_grads = [
        tail_chain.held[a:b].reshape(-1, owned_rows, width) for a, b in ends
    ]
    vec = tail_chain.held[ends[1][1] : ends[1][1] + 8].reshape(8, -1, 128)
    prompt_grad, cont_grad = place(token_grad, token_back)
    enc_rows = enc_out.shape[1]
    enc_got = swap_seq(enc_back[enc_rows:], 3)
    enc_grad = jnp.where(
        group == 0,
        jnp.stack([enc_back[:enc_rows], enc_got]),
        jnp.stack([enc_got, enc_back[:enc_rows]]),
    )

    rest = widen(rest)
    outer_mat_grad = rest[:hidden_rows]
    inner_mat_grad = jnp.concatenate(
        [rest[hidden_rows + i * owned_rows : hidden_rows + (i + 1) * owned_rows] for i in range(chunks)],
        axis=1,
    )
    vec_out = [vec[i % 8, i // 8, :owned_rows] for i in range(13)]
    inner_bias_out = vec[5, 1, :hidden_rows]
    return (
        prompt_out,
        cont_out,
        prompt_grad,
        cont_grad,
        enc_grad,
        self_query_grad[0],
        vec_out[0],
        self_key_grads[0],
        self_key_grads[1],
        vec_out[1],
        cross_grads[1],
        vec_out[2],
        vec_out[3],
        vec_out[4],
        cross_grads[0],
        vec_out[5],
        cross_key_grads[0],
        cross_key_grads[1],
        vec_out[6],
        cross_grads[2],
        vec_out[7],
        vec_out[8],
        vec_out[9],
        inner_mat_grad,
        inner_bias_out,
        outer_mat_grad,
        vec_out[10],
        vec_out[11],
        vec_out[12],
    )


def solution(mesh):
    rows_spec = P("dp", "seq", None)
    mat, vec = P(("dp", "seq"), None), P(("dp", "seq"))
    weights = (
        mat,
        vec,
        mat,
        mat,
        vec,
        mat,
        vec,
        vec,
        vec,
        mat,
        vec,
        mat,
        mat,
        vec,
        mat,
        vec,
        vec,
        vec,
        mat,
        vec,
        mat,
        vec,
        vec,
        vec,
    )
    in_specs = (rows_spec, rows_spec, rows_spec, P("dp"), rows_spec, rows_spec) + weights
    out_specs = (rows_spec,) * 5 + weights
    return jax.shard_map(body, mesh=mesh, in_specs=in_specs, out_specs=out_specs, check_vma=False)
```

```python
import jax
import jax.numpy as jnp
from jax import lax
from jax.experimental import pallas as pl
from jax.experimental.pallas import tpu as pltpu
from jax.sharding import PartitionSpec as P

HEADS = 12
VMEM_LIMIT = 60 * 1024 * 1024
NEG = -1e30


def matmul(left, right):
    return jnp.dot(left, right, preferred_element_type=jnp.float32)


def contract_rows(left, right):
    return lax.dot_general(
        left, right, (((0,), (0,)), ((), ())), preferred_element_type=jnp.float32
    )


def times_transpose(left, right):
    return lax.dot_general(
        left, right, (((1,), (1,)), ((), ())), preferred_element_type=jnp.float32
    )


def widen(values):
    return values.astype(jnp.float32)


def low(values):
    return values.astype(jnp.bfloat16)


def normalize(values, gain, shift):
    centred = values - jnp.mean(values, axis=-1, keepdims=True)
    scale = lax.rsqrt(jnp.mean(centred * centred, axis=-1, keepdims=True) + 1e-05)
    return centred * scale * gain + shift


def norm_backward(values, gain, upstream):
    centred = values - jnp.mean(values, axis=-1, keepdims=True)
    scale = lax.rsqrt(jnp.mean(centred * centred, axis=-1, keepdims=True) + 1e-05)
    normed = centred * scale
    scaled = upstream * gain
    result = scale * (
        scaled
        - jnp.mean(scaled, axis=-1, keepdims=True)
        - normed * jnp.mean(scaled * normed, axis=-1, keepdims=True)
    )
    return (
        result,
        jnp.sum(upstream * normed, axis=0, keepdims=True),
        jnp.sum(upstream, axis=0, keepdims=True),
    )


(
    SELF_Q,
    SELF_V,
    SELF_O,
    GAIN_ONE,
    SHIFT_ONE,
    CROSS_Q,
    CROSS_V,
    CROSS_O,
    GAIN_TWO,
    SHIFT_TWO,
    OUTER_B,
    GAIN_THREE,
    SHIFT_THREE,
    INNER_B,
) = range(14)


def pack_vectors(vectors, width):
    def kernel(*refs):
        out_ref = refs[-1]
        out_ref[...] = jnp.zeros_like(out_ref)
        for i, ref in enumerate(refs[:-1]):
            size = ref.shape[1]
            at = 128 * (i // 8)
            out_ref[i % 8 : i % 8 + 1, at : at + size] = ref[...]

    return pl.pallas_call(
        kernel,
        out_shape=jax.ShapeDtypeStruct((8, width), vectors[0].dtype),
        name="pack_vectors",
    )(*[v[None, :] for v in vectors])


class Call:
    def __init__(self, name, grid):
        self.name, self.grid = name, grid
        self.ins, self.in_specs, self.out_shapes, self.out_specs = [], [], [], []
        self.flops, self.bytes, self.exps = 0, 0, 0

    def whole(self, array):
        zeros = (0,) * array.ndim
        self.blocked(array, array.shape, lambda *g: zeros, buffers=1)

    def blocked(self, array, block, index, buffers=2):
        mode = {} if buffers == 2 else {"pipeline_mode": pl.Buffered(buffers)}
        self.ins.append(array)
        self.in_specs.append(pl.BlockSpec(block, index, **mode))
        self.bytes += array.size * array.dtype.itemsize

    def scalars(self, array):
        self.ins.append(array)
        self.in_specs.append(pl.BlockSpec(memory_space=pltpu.SMEM))

    def weight(self, weight):
        array, block, index = weight
        self.ins.append(array)
        self.in_specs.append(pl.BlockSpec(block, lambda *g: index, pipeline_mode=pl.Buffered(1)))
        self.bytes += array.shape[-1] ** 2 * 2

    def out(self, shape, dtype, block=None, index=None):
        zeros = (0,) * len(shape)
        self.out_shapes.append(jax.ShapeDtypeStruct(shape, dtype))
        self.out_specs.append(pl.BlockSpec(block or shape, index or (lambda *g: zeros)))
        size = 1
        for n in shape:
            size *= n
        self.bytes += size * jnp.dtype(dtype).itemsize

    def run(self, kernel, scratch=()):
        return pl.pallas_call(
            kernel,
            grid=self.grid,
            in_specs=self.in_specs,
            out_specs=self.out_specs,
            out_shape=self.out_shapes,
            scratch_shapes=list(scratch),
            compiler_params=pltpu.CompilerParams(vmem_limit_bytes=VMEM_LIMIT),
            cost_estimate=pl.CostEstimate(
                flops=int(self.flops), bytes_accessed=int(self.bytes), transcendentals=int(self.exps)
            ),
            name=self.name,
        )(*self.ins)


class Halves:
    def __init__(self, call, count, owners, owned_rows, width, heads=None, index=None):
        self.owned_rows = owned_rows
        self.even = owned_rows % 8 == 0
        if self.even:
            shape, outs = (owners // 2, count, owned_rows, width), 2
            block = (heads or owners // 2, 1 if index else count, owned_rows, width)
        else:
            shape, outs = (count, owners * owned_rows, width), 1
            block = (1 if index else count, 2 * (heads or owners // 2) * owned_rows, width)
        for _ in range(outs):
            if index is None:
                call.out(shape, jnp.bfloat16)
            elif self.even:
                call.out(shape, jnp.bfloat16, block, lambda *g: index(*g) + (0, 0))
            else:
                call.out(shape, jnp.bfloat16, block, lambda *g: index(*g)[::-1] + (0,))
        self.outs = outs

    def store(self, refs, at, value, mine):
        if not self.even:
            refs[0][at] = low(value)
            return
        parts = value.reshape(-1, 2, self.owned_rows, value.shape[-1])
        first, second = low(parts[:, 0]), low(parts[:, 1])
        refs[0][:, at] = jnp.where(mine == 0, first, second)
        refs[1][:, at] = jnp.where(mine == 0, second, first)

    def pair(self, results, mine):
        if self.even:
            return tuple(results)
        whole = results[0]
        parts = whole.reshape(whole.shape[0], -1, 2, self.owned_rows, whole.shape[-1])
        return tuple(
            lax.dynamic_index_in_dim(parts, which, 2, keepdims=False).transpose(1, 0, 2, 3)
            for which in (mine, 1 - mine)
        )


def load(ref):
    value = ref[...]
    return value.reshape(-1, value.shape[-1])


def row(vecs_ref, index):
    return vecs_ref[index : index + 1, :]


def fill_bias(bias_ref, chunk, rows, ids_ref):
    half, block = rows // 2, rows // 4
    key = lax.broadcasted_iota(jnp.int32, (rows, rows), 0)
    query = lax.broadcasted_iota(jnp.int32, (rows, rows), 1)
    key_block = jnp.where(
        lax.rem(key, half) < block, ids_ref[2 * chunk], ids_ref[2 * chunk + 1]
    )
    query_block = jnp.where(lax.rem(query, half) < block, ids_ref[0], ids_ref[1])
    key_place = key_block * block + lax.rem(key, block)
    query_place = query_block * block + lax.rem(query, block)
    causal = key_place <= query_place
    prompt_key = key < half
    prompt_query = query < half
    allowed = (prompt_key & prompt_query & causal) | (
        jnp.logical_not(prompt_query)
        & ((prompt_key & (key_place < ids_ref[4])) | (jnp.logical_not(prompt_key) & causal))
    )
    bias_ref[chunk] = jnp.where(allowed, 0.0, NEG)


def lane_masks(values):
    lane = lax.broadcasted_iota(jnp.int32, values.shape, 1)
    zero = jnp.zeros_like(values)
    first = lane < values.shape[1] // 2
    return jnp.where(first, values, zero), jnp.where(first, zero, values)


def attend_pair(queries, keys, values, bias_ref, log_ref):
    queries = lane_masks(queries)
    outs = []
    for head in range(2):
        scores = []
        for chunk in range(2):
            part = times_transpose(keys[chunk], queries[head])
            scores.append(part if bias_ref is None else part + bias_ref[chunk])
        top = jnp.maximum(
            scores[0].max(axis=0, keepdims=True), scores[1].max(axis=0, keepdims=True)
        )
        total, mixed = 0.0, 0.0
        for chunk in range(2):
            weights = jnp.exp(scores[chunk] - top)
            total = total + weights.sum(axis=0, keepdims=True)
            mixed = mixed + contract_rows(values[chunk], low(weights))
        outs.append(mixed * (1.0 / total))
        log_ref[0, head : head + 1, :] = top + jnp.log(total)
    lane = lax.broadcasted_iota(jnp.int32, outs[0].shape, 0)
    return low(jnp.where(lane < outs[0].shape[0] // 2, outs[0], outs[1]).T)


def attend_pair_backward(queries, keys, values, bias_ref, log_ref, mixed, upstream):
    queries = lane_masks(queries)
    ups = lane_masks(upstream)
    product = widen(mixed) * widen(upstream)
    high = low(product)
    rest = low(product - widen(high))
    pair = product.shape[1]
    lane = lax.broadcasted_iota(jnp.int32, (8, pair), 1)
    line = lax.broadcasted_iota(jnp.int32, (8, pair), 0)
    pick = jnp.where(
        ((lane < pair // 2) & (line == 0)) | ((lane >= pair // 2) & (line == 1)), 1.0, 0.0
    ).astype(jnp.bfloat16)
    delta = times_transpose(pick, high) + times_transpose(pick, rest)
    dq = 0.0
    dk = [0.0, 0.0]
    dv = [0.0, 0.0]
    for head in range(2):
        for chunk in range(2):
            part = times_transpose(keys[chunk], queries[head])
            if bias_ref is not None:
                part = part + bias_ref[chunk]
            probs = jnp.exp(part - log_ref[0, head : head + 1, :])
            prob_grad = times_transpose(values[chunk], ups[head])
            score_grad = low(probs * (prob_grad - delta[head : head + 1, :]))
            dv[chunk] = dv[chunk] + matmul(low(probs), ups[head])
            dk[chunk] = dk[chunk] + matmul(score_grad, queries[head])
            dq = dq + contract_rows(lane_masks(keys[chunk])[head], score_grad)
    return low(dq.T), dk, dv


def project_kernel(scaled, x_ref, *refs):
    vecs_ref = refs[-3] if scaled else refs[-2]
    values = x_ref[...]
    if scaled:
        wq_ref, wk_ref, wv_ref = refs[:3]
        q_ref, kv_ref = refs[-2:]
        q_ref[...] = low((matmul(values, load(wq_ref)) + row(vecs_ref, SELF_Q)) * 0.125)
        bias = row(vecs_ref, SELF_V)
    else:
        wk_ref, wv_ref = refs[:2]
        kv_ref = refs[-1]
        bias = row(vecs_ref, CROSS_V)
    kv_ref[0] = low(matmul(values, load(wk_ref)))
    kv_ref[1] = low(matmul(values, load(wv_ref)) + bias)


def project(tokens, weights, vecs):
    rows, width = tokens.shape
    scaled = len(weights) == 3
    call = Call("project", (1,))
    call.whole(tokens)
    for weight in weights:
        call.weight(weight)
    call.whole(vecs)
    if scaled:
        call.out((rows, width), jnp.bfloat16)
    call.out((2, rows, width), jnp.bfloat16)
    call.flops = 2 * len(weights) * rows * width * width

    def kernel(*refs):
        project_kernel(scaled, *refs)

    return call.run(kernel)


def lanes_of(width):
    lanes = 2 * (width // HEADS)

    def at(h):
        return pl.ds(pl.multiple_of(h * lanes, lanes), lanes)

    return lanes, at


def self_attend(ids, queries, own, other):
    rows, width = queries.shape
    pairs = HEADS // 2
    lanes, _ = lanes_of(width)
    call = Call("self_attend", (pairs,))
    call.scalars(ids)
    call.blocked(queries, (rows, lanes), lambda h: (0, h))
    for array in (own, other):
        call.blocked(array, (2, rows, lanes), lambda h: (0, 0, h))
    call.out((rows, width), jnp.bfloat16, (rows, lanes), lambda h: (0, h))
    call.out((pairs, 2, rows), jnp.float32, (1, 2, rows), lambda h: (h, 0, 0))
    call.flops = 16 * rows * rows * width
    call.exps = 2 * rows * rows * HEADS

    def kernel(ids_ref, q_ref, own_ref, other_ref, mixed_ref, log_ref, bias_ref):
        @pl.when(pl.program_id(0) == 0)
        def _():
            for chunk in range(2):
                fill_bias(bias_ref, chunk, rows, ids_ref)

        keys, values = (own_ref[0], other_ref[0]), (own_ref[1], other_ref[1])
        mixed_ref[...] = attend_pair(q_ref[...], keys, values, bias_ref, log_ref)

    return call.run(kernel, [pltpu.VMEM((2, rows, rows), jnp.float32)])


def self_finish(tokens, mixed, out_weight, query_weight, vecs):
    rows, width = tokens.shape
    call = Call("self_finish", (1,))
    call.whole(tokens)
    call.whole(mixed)
    call.weight(out_weight)
    call.weight(query_weight)
    call.whole(vecs)
    call.out((rows, width), jnp.float32)
    call.out((rows, width), jnp.bfloat16)
    call.out((rows, width), jnp.bfloat16)
    call.flops = 4 * rows * width * width

    def kernel(x_ref, mixed_ref, wo_ref, wq_ref, vecs_ref, pre_ref, low_ref, next_ref):
        pre = widen(x_ref[...]) + matmul(mixed_ref[...], load(wo_ref)) + row(vecs_ref, SELF_O)
        pre_ref[...] = pre
        first = low(normalize(pre, row(vecs_ref, GAIN_ONE), row(vecs_ref, SHIFT_ONE)))
        low_ref[...] = first
        next_ref[...] = low((matmul(first, load(wq_ref)) + row(vecs_ref, CROSS_Q)) * 0.125)

    return call.run(kernel)


def cross_attend(queries, own, other, first_pre, out_weight, vecs):
    rows, width = queries.shape
    key_rows = own.shape[1]
    pairs = HEADS // 2
    lanes, at = lanes_of(width)
    call = Call("cross_attend", (pairs,))
    call.blocked(queries, (rows, lanes), lambda h: (0, h))
    for array in (own, other):
        call.blocked(array, (2, key_rows, lanes), lambda h: (0, 0, h))
    call.whole(first_pre)
    call.weight(out_weight)
    call.whole(vecs)
    call.out((rows, width), jnp.bfloat16)
    call.out((pairs, 2, rows), jnp.float32, (1, 2, rows), lambda h: (h, 0, 0))
    call.out((rows, width), jnp.float32)
    call.out((rows, width), jnp.bfloat16)
    call.flops = 16 * rows * key_rows * width + 2 * rows * width * width
    call.exps = 2 * rows * key_rows * HEADS

    def kernel(
        q_ref, own_ref, other_ref, first_ref, wo_ref, vecs_ref, mixed_ref, log_ref, pre_ref, low_ref
    ):
        step = pl.program_id(0)
        keys, values = (own_ref[0], other_ref[0]), (own_ref[1], other_ref[1])
        mixed_ref[:, at(step)] = attend_pair(q_ref[...], keys, values, None, log_ref)

        @pl.when(step == pairs - 1)
        def _():
            first = normalize(first_ref[...], row(vecs_ref, GAIN_ONE), row(vecs_ref, SHIFT_ONE))
            pre = first + matmul(mixed_ref[...], load(wo_ref)) + row(vecs_ref, CROSS_O)
            pre_ref[...] = pre
            low_ref[...] = low(normalize(pre, row(vecs_ref, GAIN_TWO), row(vecs_ref, SHIFT_TWO)))

    return call.run(kernel)


def feed_blocks(call, feed, width, chunks, owned_rows):
    owners = feed.shape[0]
    hidden_rows = chunks * owned_rows
    if owned_rows % 8 == 0:
        call.blocked(feed, (owners, owned_rows, width), lambda i: (0, chunks + i, 0))
        call.blocked(feed, (owners // chunks, hidden_rows, width), lambda i: (i, 0, 0))
    else:
        parts = [
            feed[:, hidden_rows + i * owned_rows : hidden_rows + (i + 1) * owned_rows]
            for i in range(chunks)
        ]
        parts = [p.reshape(-1, width) for p in parts]
        call.blocked(jnp.concatenate(parts, axis=1), (width, width), lambda i: (0, i))
        call.blocked(feed[:, :hidden_rows].reshape(-1, width), (width, width), lambda i: (i, 0))


def feed_forward(second_pre, second_low, feed, vecs, chunks, owned_rows):
    rows, width = second_low.shape
    hidden = chunks * width
    call = Call("feed_forward", (chunks,))
    call.whole(second_pre)
    call.whole(second_low)
    feed_blocks(call, feed, width, chunks, owned_rows)
    call.whole(vecs)
    call.out((rows, hidden), jnp.bfloat16, (rows, width), lambda i: (0, i))
    call.out((rows, hidden), jnp.bfloat16, (rows, width), lambda i: (0, i))
    call.out((rows, width), jnp.float32)
    call.out((rows, width), jnp.bfloat16)
    call.flops = 4 * rows * hidden * width
    call.exps = 2 * rows * hidden

    def kernel(
        pre_ref, low_ref, inner_ref, outer_ref, vecs_ref, active_ref, slope_ref, third_ref, out_ref
    ):
        step = pl.program_id(0)

        @pl.when(step == 0)
        def _():
            second = normalize(pre_ref[...], row(vecs_ref, GAIN_TWO), row(vecs_ref, SHIFT_TWO))
            third_ref[...] = second + row(vecs_ref, OUTER_B)

        inner = matmul(low_ref[...], load(inner_ref)) + vecs_ref[pl.ds(INNER_B + step, 1), :]
        bell = 0.5 * (1.0 + lax.erf(inner * 0.7071067811865476))
        active = low(inner * bell)
        active_ref[...] = active
        density = jnp.exp(-0.5 * inner * inner) * 0.3989422804014327
        slope_ref[...] = low(bell + inner * density)
        third_ref[...] += matmul(active, load(outer_ref))

        @pl.when(step == chunks - 1)
        def _():
            out_ref[...] = low(
                normalize(third_ref[...], row(vecs_ref, GAIN_THREE), row(vecs_ref, SHIFT_THREE))
            )

    return call.run(kernel)


def outer_backward(ids, upstream, third_pre, active, vecs, chunks, owned_rows):
    rows, width = third_pre.shape
    owners = width // owned_rows
    call = Call("outer_backward", (chunks,))
    call.scalars(ids)
    call.whole(upstream)
    call.whole(third_pre)
    call.blocked(active, (rows, width), lambda i: (0, i))
    call.whole(vecs)
    call.out((rows, width), jnp.float32)
    call.out((rows, width), jnp.bfloat16)
    call.out((24, width), jnp.float32)
    half = Halves(
        call, 1, owners, chunks * owned_rows, width, owners // 2 // chunks, lambda i: (i, 0)
    )
    call.flops = 2 * rows * chunks * width * width

    def kernel(ids_ref, up_ref, third_ref, active_ref, vecs_ref, grad_ref, low_ref, sums_ref, *grads):
        @pl.when(pl.program_id(0) == 0)
        def _():
            grad, gain_sum, shift_sum = norm_backward(
                third_ref[...], row(vecs_ref, GAIN_THREE), widen(up_ref[...])
            )
            grad_ref[...] = grad
            low_ref[...] = low(grad)
            sums_ref[...] = jnp.zeros_like(sums_ref)
            sums_ref[GAIN_THREE : GAIN_THREE + 1, :] = gain_sum
            sums_ref[SHIFT_THREE : SHIFT_THREE + 1, :] = shift_sum
            sums_ref[OUTER_B : OUTER_B + 1, :] = jnp.sum(widen(low(grad)), axis=0, keepdims=True)

        half.store(grads, 0, contract_rows(active_ref[...], low_ref[...]), ids_ref[5])

    results = call.run(kernel)
    return tuple(results[:3]) + (half.pair(results[3:], ids[5]),)


def inner_backward(
    ids, third_grad, third_low, sums, second_pre, second_low, slope, cross_mixed, feed, out_weight, vecs,
    chunks, owned_rows,
):
    rows, width = second_low.shape
    owners = width // owned_rows
    call = Call("inner_backward", (chunks,))
    call.scalars(ids)
    for array in (third_grad, third_low, sums, second_pre, second_low):
        call.whole(array)
    call.blocked(slope, (rows, width), lambda i: (0, i))
    call.whole(cross_mixed)
    feed_blocks(call, feed, width, chunks, owned_rows)
    call.weight(out_weight)
    call.whole(vecs)
    call.out((rows, width), jnp.float32)
    call.out((rows, width), jnp.bfloat16)
    call.out((24, width), jnp.float32)
    inner_half = Halves(call, chunks, owners, owned_rows, width, owners // 2, lambda i: (0, i))
    out_half = Halves(call, 1, owners, owned_rows, width)
    call.flops = 6 * rows * chunks * width * width + 4 * rows * width * width
    outs = inner_half.outs

    def kernel(
        ids_ref, third_ref, third_low_ref, sums_in_ref, second_ref, low_ref, slope_ref, mixed_ref, inner_ref, outer_ref,
        wo_ref, vecs_ref, second_grad_ref, mix_ref, sums_ref, *rest,
    ):
        inner_grads, out_grads, total_ref = rest[:outs], rest[outs:-1], rest[-1]
        step = pl.program_id(0)
        mine = ids_ref[5]

        @pl.when(step == 0)
        def _():
            total_ref[...] = third_ref[...]
            sums_ref[...] = sums_in_ref[...]

        inner_low = low(times_transpose(third_low_ref[...], load(outer_ref)) * widen(slope_ref[...]))
        total_ref[...] += times_transpose(inner_low, load(inner_ref))
        inner_half.store(inner_grads, 0, contract_rows(low_ref[...], inner_low), mine)
        sums_ref[pl.ds(INNER_B + step, 1), :] = jnp.sum(widen(inner_low), axis=0, keepdims=True)

        @pl.when(step == chunks - 1)
        def _():
            grad, gain_sum, shift_sum = norm_backward(
                second_ref[...], row(vecs_ref, GAIN_TWO), total_ref[...]
            )
            second_grad_ref[...] = grad
            cross_low = low(grad)
            sums_ref[GAIN_TWO : GAIN_TWO + 1, :] = gain_sum
            sums_ref[SHIFT_TWO : SHIFT_TWO + 1, :] = shift_sum
            sums_ref[CROSS_O : CROSS_O + 1, :] = jnp.sum(widen(cross_low), axis=0, keepdims=True)
            mix_ref[...] = low(times_transpose(cross_low, load(wo_ref)))
            out_half.store(out_grads, 0, contract_rows(mixed_ref[...], cross_low), mine)

    results = call.run(kernel, [pltpu.VMEM((rows, width), jnp.float32)])
    core = ids[5]
    return tuple(results[:3]) + (
        inner_half.pair(results[3 : 3 + outs], core),
        out_half.pair(results[3 + outs :], core),
    )


def cross_backward(
    ids, queries, own, other, mixed, upstream, logsum, first_low, first_pre, second_grad, self_mixed, sums,
    query_weight, out_weight, vecs, owned_rows,
):
    rows, width = queries.shape
    key_rows = own.shape[1]
    pairs = HEADS // 2
    lanes, at = lanes_of(width)
    call = Call("cross_backward", (pairs,))
    call.scalars(ids)
    for array in (queries, mixed, upstream):
        call.blocked(array, (rows, lanes), lambda h: (0, h))
    call.blocked(logsum, (1, 2, rows), lambda h: (h, 0, 0))
    for array in (own, other):
        call.blocked(array, (2, key_rows, lanes), lambda h: (0, 0, h))
    for array in (first_low, first_pre, second_grad, self_mixed, sums):
        call.whole(array)
    call.weight(query_weight)
    call.weight(out_weight)
    call.whole(vecs)
    for _ in range(2):
        call.out((2, key_rows, width), jnp.bfloat16, (2, key_rows, lanes), lambda h: (0, 0, h))
    call.out((rows, width), jnp.float32)
    call.out((rows, width), jnp.bfloat16)
    call.out((24, width), jnp.float32)
    half = Halves(call, 2, width // owned_rows, owned_rows, width)
    call.flops = 40 * rows * key_rows * width + 8 * rows * width * width
    call.exps = 2 * rows * key_rows * HEADS

    def kernel(
        ids_ref, q_ref, mixed_ref, up_ref, log_ref, own_ref, other_ref, low_ref, pre_ref, grad_ref,
        self_mixed_ref, sums_in_ref, wq_ref, wo_ref, vecs_ref, own_out_ref, other_out_ref, first_ref, mix_ref,
        sums_ref, *rest,
    ):
        step = pl.program_id(0)
        weights_refs, dq_ref = rest[:-1], rest[-1]

        @pl.when(step == 0)
        def _():
            sums_ref[...] = sums_in_ref[...]

        keys, values = (own_ref[0], other_ref[0]), (own_ref[1], other_ref[1])
        dq, dk, dv = attend_pair_backward(
            q_ref[...], keys, values, None, log_ref, mixed_ref[...], up_ref[...]
        )
        dq_ref[:, at(step)] = dq
        for chunk, out in enumerate((own_out_ref, other_out_ref)):
            out[0] = low(dk[chunk])
            out[1] = low(dv[chunk])
        sums_ref[CROSS_V : CROSS_V + 1, at(step)] = sum(jnp.sum(v, axis=0, keepdims=True) for v in dv)

        @pl.when(step == pairs - 1)
        def _():
            query_low = dq_ref[...]
            half.store(weights_refs, 0, contract_rows(low_ref[...], query_low) * 0.125, ids_ref[5])
            total = grad_ref[...] + times_transpose(query_low, load(wq_ref)) * 0.125
            grad, gain_sum, shift_sum = norm_backward(pre_ref[...], row(vecs_ref, GAIN_ONE), total)
            first_ref[...] = grad
            self_low = low(grad)
            mix_ref[...] = low(times_transpose(self_low, load(wo_ref)))
            half.store(weights_refs, 1, contract_rows(self_mixed_ref[...], self_low), ids_ref[5])
            sums_ref[GAIN_ONE : GAIN_ONE + 1, :] = gain_sum
            sums_ref[SHIFT_ONE : SHIFT_ONE + 1, :] = shift_sum
            sums_ref[SELF_O : SELF_O + 1, :] = jnp.sum(widen(self_low), axis=0, keepdims=True)
            sums_ref[CROSS_Q : CROSS_Q + 1, :] = jnp.sum(widen(query_low), axis=0, keepdims=True) * 0.125

    results = call.run(kernel, [pltpu.VMEM((rows, width), jnp.bfloat16)])
    return tuple(results[:5]) + (half.pair(results[5:], ids[5]),)


def self_backward(ids, queries, own, other, mixed, upstream, logsum, first, last):
    rows, width = queries.shape
    lanes, _ = lanes_of(width)
    count = last - first
    call = Call("self_backward", (count,))
    call.scalars(ids)
    for array in (queries, mixed, upstream):
        call.blocked(array, (rows, lanes), lambda h: (0, first + h))
    call.blocked(logsum, (1, 2, rows), lambda h: (first + h, 0, 0))
    for array in (own, other):
        call.blocked(array, (2, rows, lanes), lambda h: (0, 0, first + h))
    call.out((rows, count * lanes), jnp.bfloat16, (rows, lanes), lambda h: (0, h))
    for _ in range(2):
        call.out(
            (2, rows, count * lanes), jnp.bfloat16, (2, rows, lanes), lambda h: (0, 0, h)
        )
    call.out((8, count * lanes), jnp.float32, (8, lanes), lambda h: (0, h))
    call.flops = 40 * rows * rows * count * lanes
    call.exps = 4 * rows * rows * count

    def kernel(
        ids_ref, q_ref, mixed_ref, up_ref, log_ref, own_ref, other_ref, dq_ref, own_out_ref,
        other_out_ref, sums_ref, bias_ref,
    ):
        @pl.when(pl.program_id(0) == 0)
        def _():
            for chunk in range(2):
                fill_bias(bias_ref, chunk, rows, ids_ref)

        keys, values = (own_ref[0], other_ref[0]), (own_ref[1], other_ref[1])
        dq, dk, dv = attend_pair_backward(
            q_ref[...], keys, values, bias_ref, log_ref, mixed_ref[...], up_ref[...]
        )
        dq_ref[...] = dq
        for chunk, out in enumerate((own_out_ref, other_out_ref)):
            out[0] = low(dk[chunk])
            out[1] = low(dv[chunk])
        sums_ref[0:1, :] = sum(jnp.sum(v, axis=0, keepdims=True) for v in dv)
        sums_ref[1:2, :] = jnp.sum(widen(dq), axis=0, keepdims=True) * 0.125

    return call.run(kernel, [pltpu.VMEM((2, rows, rows), jnp.float32)])


def query_backward(ids, tokens, query_low, half_sums, sums, first_grad, query_weight, owned_rows):
    rows, width = tokens.shape
    call = Call("query_backward", (1,))
    call.scalars(ids)
    for array in (tokens, first_grad, sums) + tuple(query_low) + tuple(half_sums):
        call.whole(array)
    call.weight(query_weight)
    call.out((rows, width), jnp.float32)
    call.out((24, width), jnp.float32)
    half = Halves(call, 1, width // owned_rows, owned_rows, width)
    call.flops = 4 * rows * width * width

    def kernel(
        ids_ref, x_ref, grad_ref, sums_in_ref, first_ref, second_ref, first_sums_ref, second_sums_ref,
        wq_ref, part_ref, sums_ref, *weights_refs,
    ):
        sums_ref[...] = sums_in_ref[...]
        cut = first_ref.shape[1]
        for lanes, ref in ((slice(0, cut), first_sums_ref), (slice(cut, width), second_sums_ref)):
            sums_ref[SELF_V : SELF_V + 1, lanes] = ref[0:1, :]
            sums_ref[SELF_Q : SELF_Q + 1, lanes] = ref[1:2, :]
        query = jnp.concatenate([first_ref[...], second_ref[...]], axis=1)
        half.store(weights_refs, 0, contract_rows(x_ref[...], query) * 0.125, ids_ref[5])
        part_ref[...] = grad_ref[...] + times_transpose(query, load(wq_ref)) * 0.125

    results = call.run(kernel)
    return results[0], results[1], half.pair(results[2:], ids[5])


def key_weights(ids, tokens, mine, got, owned_rows):
    rows, width = tokens.shape
    call = Call("key_weights", (1,))
    call.scalars(ids)
    for array in (tokens,) + tuple(mine) + tuple(got):
        call.whole(array)
    call.out((2, rows, width), jnp.bfloat16)
    halves = [Halves(call, 1, width // owned_rows, owned_rows, width) for _ in range(2)]
    outs = halves[0].outs
    call.flops = 4 * rows * width * width

    def kernel(ids_ref, x_ref, mine_a, mine_b, got_a, got_b, total_ref, *weights_refs):
        values = x_ref[...]
        for i in range(2):
            total = low(
                jnp.concatenate(
                    [widen(m[i]) + widen(g[i]) for m, g in ((mine_a, got_a), (mine_b, got_b))], axis=1
                )
            )
            total_ref[i] = total
            refs = weights_refs[i * outs : (i + 1) * outs]
            halves[i].store(refs, 0, contract_rows(values, total), ids_ref[5])

    results = call.run(kernel)
    return (results[0],) + tuple(
        halves[i].pair(results[1 + i * outs : 1 + (i + 1) * outs], ids[5]) for i in range(2)
    )


def token_backward(total, part, key_weight, value_weight):
    rows, width = part.shape
    call = Call("token_backward", (1,))
    call.whole(total)
    call.whole(part)
    call.weight(key_weight)
    call.weight(value_weight)
    call.out((rows, width), jnp.bfloat16)
    call.flops = 4 * rows * width * width

    def kernel(total_ref, part_ref, wk_ref, wv_ref, out_ref):
        out_ref[...] = low(
            part_ref[...]
            + times_transpose(total_ref[0], load(wk_ref))
            + times_transpose(total_ref[1], load(wv_ref))
        )

    return call.run(kernel)[0]


def key_backward(ids, tokens, mine, got, key_weight, value_weight, owned_rows):
    rows, width = tokens.shape
    call = Call("key_backward", (1,))
    call.scalars(ids)
    for array in (tokens, mine, got):
        call.whole(array)
    call.weight(key_weight)
    call.weight(value_weight)
    call.out((rows, width), jnp.bfloat16)
    half = Halves(call, 2, width // owned_rows, owned_rows, width)
    call.flops = 8 * rows * width * width

    def kernel(ids_ref, x_ref, mine_ref, got_ref, wk_ref, wv_ref, out_ref, *weights_refs):
        values = x_ref[...]
        dk = low(widen(mine_ref[0]) + widen(got_ref[0]))
        dv = low(widen(mine_ref[1]) + widen(got_ref[1]))
        half.store(weights_refs, 0, contract_rows(values, dk), ids_ref[5])
        half.store(weights_refs, 1, contract_rows(values, dv), ids_ref[5])
        out_ref[...] = low(
            times_transpose(dk, load(wk_ref)) + times_transpose(dv, load(wv_ref))
        )

    results = call.run(kernel)
    return results[0], half.pair(results[1:], ids[5])


def flip(size, bit):
    return [(i, i ^ bit) for i in range(size)]


def swap_seq(values, bits):
    return lax.ppermute(values, "seq", flip(lax.axis_size("seq"), bits))


def tie(*values):
    return lax.optimization_barrier(values)


def bit_order(dp_size, seq_size):
    return [("dp", b) for b in range(dp_size.bit_length() - 1)][::-1] + [
        ("seq", b) for b in range(seq_size.bit_length() - 1)
    ][::-1]


class Moves:
    def __init__(self):
        self.spots = {name: lax.axis_index(name) for name in ("dp", "seq")}
        self.sizes = {name: lax.axis_size(name) for name in ("dp", "seq")}
        self.canonical = bit_order(self.sizes["dp"], self.sizes["seq"])

    def mine(self, step):
        return (self.spots[step[0]] >> step[1]) & 1

    def send(self, values, step):
        name, bit = step
        flat = values.reshape(-1, values.shape[-1])
        return lax.ppermute(flat, name, flip(self.sizes[name], 1 << bit)).reshape(values.shape)


def split_sum(keep, got, at, mine):
    def side(which):
        first, second = [
            lax.dynamic_index_in_dim(v, which, at, keepdims=False) for v in (keep, got)
        ]
        return low(widen(first) + widen(second))

    return side(mine), side(1 - mine)


class Scatter:
    def __init__(self, moves, pairs, order):
        self.moves = moves
        self.dims = [step for step in moves.canonical if step != order[0]]
        self.order = list(order)
        pieces = (2,) * len(self.dims)

        def join(arrays):
            arrays = [a.reshape(pieces + (-1, a.shape[-1])) for a in arrays]
            return arrays[0] if len(arrays) == 1 else jnp.concatenate(arrays, axis=-2)

        self.keep = join([k for k, _ in pairs])
        self.away = join([a for _, a in pairs])
        self.got = None

    def ship(self):
        self.got = self.moves.send(self.away, self.order.pop(0))
        self.away = None

    def take(self):
        got, self.got = self.got, None
        if self.order:
            step = self.order[0]
            at = self.dims.index(step)
            self.keep, self.away = split_sum(self.keep, got, at, self.moves.mine(step))
            self.dims.pop(at)
        else:
            self.held = widen(self.keep) + widen(got)

    def spread(self):
        steps, self.order = self.order, []
        name = steps[0][0]
        assert self.dims == sorted(steps, reverse=True) and self.got is not None
        self.keep = self.total()
        count = 1 << len(steps)
        first = steps[0][1]
        assert [bit for _, bit in steps] == list(range(first, first + len(steps)))
        held = self.keep.reshape((count,) + self.keep.shape[-2:])
        spot = (self.moves.spots[name] >> first) & (count - 1)
        self.keep = lax.dynamic_index_in_dim(held, spot, 0, keepdims=False)
        self.spreads = [
            (i, lax.dynamic_index_in_dim(held, spot ^ i, 0, keepdims=False)) for i in range(1, count)
        ]
        size = self.moves.sizes[name]
        self.gots = [lax.ppermute(v, name, flip(size, i << first)) for i, v in self.spreads]

    def collect(self):
        self.held = widen(self.keep)
        for got in self.gots:
            self.held = self.held + widen(got)

    def total(self):
        return low(widen(self.keep) + widen(self.got))


def joined(chains):
    first = chains[0]
    chain = object.__new__(Scatter)
    chain.moves, chain.dims, chain.order, chain.got = first.moves, first.dims, first.order, None
    chain.keep = jnp.concatenate([c.keep for c in chains], axis=-2)
    chain.away = jnp.concatenate([c.away for c in chains], axis=-2)
    return chain


def receive(chains, *values):
    tied = tie(*[c.got for c in chains], *values)
    for chain, got in zip(chains, tied):
        chain.got = got
        chain.take()
    values = tied[len(chains) :]
    return values[0] if len(values) == 1 else values


def depart(chains, *values):
    tied = tie(*[c.away for c in chains], *values)
    for chain, away in zip(chains, tied):
        chain.away = away
        chain.ship()
    values = tied[len(chains) :]
    return values[0] if len(values) == 1 else values


def advance(chains, *values):
    values = receive(chains, *values)
    return depart(chains, *(values if isinstance(values, (list, tuple)) else (values,)))


class Gather:
    def __init__(self, moves, held, order, dims=()):
        self.moves, self.held, self.order, self.dims = moves, held, list(order), list(dims)

    def ship(self):
        self.got = self.moves.send(self.held, self.order[0])

    def take(self):
        step = self.order.pop(0)
        mine = self.moves.mine(step)
        first = jnp.where(mine == 0, self.held, self.got)
        second = jnp.where(mine == 0, self.got, self.held)
        self.held = jnp.stack([first, second], axis=0)
        self.dims.insert(0, step)

    def part(self, first, last, order):
        return Gather(self.moves, self.held[..., first:last, :], order, self.dims)

    def result(self):
        order = [self.dims.index(step) for step in self.moves.canonical]
        count = len(order)
        held = self.held.transpose(order + [count, count + 1])
        return held.reshape((-1,) + held.shape[-2:])


def pump(taking, shipping, *values):
    tied = tie(*[g.got for g in taking], *values)
    for gather, got in zip(taking, tied):
        gather.got = got
        gather.take()
    tied = tie(*[g.held for g in shipping], *tied[len(taking) :])
    for gather, held in zip(shipping, tied):
        gather.held = held
        gather.ship()
    values = tied[len(shipping) :]
    return values[0] if len(values) == 1 else values


def body(
    prompt_in,
    cont_in,
    enc_out,
    prefix,
    prompt_cot,
    cont_cot,
    self_query,
    self_qbias,
    self_key,
    self_value,
    self_vbias,
    self_out,
    self_obias,
    gain_one,
    shift_one,
    cross_query,
    cross_qbias,
    cross_key,
    cross_value,
    cross_vbias,
    cross_out,
    cross_obias,
    gain_two,
    shift_two,
    inner_mat,
    inner_bias,
    outer_mat,
    outer_bias,
    gain_three,
    shift_three,
):
    seq = lax.axis_index("seq")
    parts, blocks = lax.axis_size("seq"), lax.axis_size("dp")
    rows = prompt_in.shape[1]
    width = prompt_in.shape[2]
    owned_rows = self_query.shape[0]
    group = seq // 2
    ids = jnp.stack([seq, 3 - seq, seq ^ 1, 3 - (seq ^ 1), prefix[group], seq & 1]).astype(jnp.int32)

    def pick(array, index):
        return lax.dynamic_index_in_dim(array, index, 0, keepdims=False)

    vectors = [
        self_qbias,
        self_vbias,
        self_obias,
        gain_one,
        shift_one,
        cross_qbias,
        cross_vbias,
        cross_obias,
        gain_two,
        shift_two,
        outer_bias,
        gain_three,
        shift_three,
    ]
    hidden_rows = outer_mat.shape[0]
    chunks = hidden_rows // owned_rows
    tail = pack_vectors(vectors + [inner_bias], width)
    moves = Moves()
    bits = moves.canonical
    dp_bits, hi, lo = bits[:-2], bits[-2], bits[-1]
    line, near = dp_bits[:-1], dp_bits[-1]
    cut = 2 * owned_rows
    first_part = jnp.concatenate([self_query, self_key, self_value, tail], axis=0)
    first_part, inner_mat, outer_mat, self_out, prompt_in, cont_in = tie(
        first_part, inner_mat, outer_mat, self_out, prompt_in, cont_in
    )
    one = Gather(moves, first_part, line)
    one.ship()
    prompt_got = swap_seq(pick(prompt_in, 1 - group), 3)
    sent = jnp.concatenate([pick(v, 1 - group) for v in (cont_in, enc_out)], axis=0)
    feed = jnp.concatenate(
        [outer_mat]
        + [inner_mat[:, i * width : (i + 1) * width] for i in range(chunks)]
        + [cross_key, cross_value, cross_out],
        axis=0,
    )
    second_part = jnp.concatenate([self_out, cross_query], axis=0)
    feed = lax.all_gather(feed, ("dp", "seq"), axis=0, tiled=False)
    prompt_got, sent, second_part = pump([one], [one], prompt_got, sent, second_part)
    two = Gather(moves, second_part, line)
    got = swap_seq(sent, 3)
    while len(one.order) > 1:
        pump([one], [one])
    got = pump([one], [], got)
    one_parts = [
        one.part(0, cut, [near, hi, lo]),
        one.part(cut, first_part.shape[0], [hi, near, lo]),
    ]
    got = pump([], one_parts + [two], got)
    got = pump(one_parts + [two], one_parts + [two], got)
    while len(two.order) > 1:
        got = pump([two], [two], got)
    got = pump(one_parts + [two], one_parts, got)
    two_parts = [
        two.part(0, owned_rows, [near, hi, lo]),
        two.part(owned_rows, second_part.shape[0], [hi, near, lo]),
    ]
    got = pump(one_parts, two_parts, got)

    tokens = jnp.concatenate(
        [pick(prompt_in, group), prompt_got, pick(cont_in, group), got[:rows]], axis=0
    )
    encoder = jnp.concatenate([pick(enc_out, group), got[rows:]], axis=0)

    def square(array, index):
        if owned_rows % 8 == 0:
            return array, (array.shape[0], owned_rows, width), (0, index, 0)
        part = array[:, index * owned_rows : (index + 1) * owned_rows].reshape(-1, width)
        return part, part.shape, (0, 0)

    front, back = [g.result() for g in one_parts]
    self_query, self_key, self_value = square(front, 0), square(front, 1), square(back, 0)
    tail = back[:, owned_rows:]
    owners = parts * blocks
    counts = 13 * owned_rows
    slots = tail.reshape(owners, 8, -1, 128)[:, :, :2, :owned_rows]
    vecs = slots.transpose(2, 1, 0, 3).reshape(16, width)[:13]
    biases = tail[:, 5, 128 : 128 + hidden_rows].reshape(chunks, width)
    vecs = widen(jnp.concatenate([vecs, biases], axis=0))

    queries, own = project(tokens, [self_query, self_key, self_value], vecs)
    own = pump(two_parts, two_parts, own)
    other = swap_seq(own, 1)
    mixed, logsum = self_attend(ids, queries, own, other)
    mixed = pump(two_parts, two_parts, mixed)
    mixed = pump(two_parts, [], mixed)
    front, back = [g.result() for g in two_parts]
    self_out, cross_query = square(front, 0), square(back, 0)
    cot_sent = jnp.concatenate([pick(v, 1 - group) for v in (prompt_cot, cont_cot)], axis=0)
    cot_sent, mixed = tie(cot_sent, mixed)
    cot_got = swap_seq(cot_sent, 3)
    first_pre, first_low, cross_queries = self_finish(tokens, mixed, self_out, cross_query, vecs)
    cross_queries, cot_got, feed = tie(cross_queries, cot_got, feed)
    cross_key, cross_value, cross_out = [square(feed, 2 * chunks + i) for i in range(3)]
    (cross_own,) = project(encoder, [cross_key, cross_value], vecs)
    cross_other = swap_seq(cross_own, 1)
    cross_mixed, cross_logsum, second_pre, second_low = cross_attend(
        cross_queries, cross_own, cross_other, first_pre, cross_out, vecs
    )
    upstream = jnp.concatenate(
        [pick(prompt_cot, group), cot_got[:rows], pick(cont_cot, group), cot_got[rows:]], axis=0
    )
    active, slope, third_pre, result = feed_forward(
        second_pre, second_low, feed, vecs, chunks, owned_rows
    )

    def send_back(own, *values):
        away = jnp.concatenate([own[rows : 2 * rows], own[3 * rows :]], axis=0)
        tied = tie(away, *values)
        return (own, swap_seq(tied[0], 3)) + tuple(tied[1:])

    def place(own, back):
        kept = (own[:rows], own[2 * rows : 3 * rows])
        back = (back[:rows], back[rows:])
        return [
            jnp.where(group == 0, jnp.stack([a, b]), jnp.stack([b, a])) for a, b in zip(kept, back)
        ]

    result, result_back, third_pre = send_back(result, third_pre)

    bits = dp_bits[::-1]
    x_first = [lo, hi] + bits
    y_first = [lo, bits[0], hi] + bits[1:]
    third_grad, third_low, sums, outer_pair = outer_backward(
        ids, upstream, third_pre, active, vecs, chunks, owned_rows
    )
    third_low, result_back = tie(third_low, result_back)
    prompt_out, cont_out = place(result, result_back)
    outer_chain = Scatter(moves, [outer_pair], x_first)
    third_low = depart([outer_chain], third_low)
    second_grad, cross_mix, sums, inner_pair, cross_out_pair = inner_backward(
        ids, third_grad, third_low, sums, second_pre, second_low, slope, cross_mixed, feed, cross_out,
        vecs, chunks, owned_rows,
    )
    inner_chain = Scatter(moves, [inner_pair], y_first)
    feed_chains = [outer_chain, inner_chain]
    cross_mix = receive([outer_chain], cross_mix)
    cross_mix = depart([inner_chain], cross_mix)
    cross_mix = depart([outer_chain], cross_mix)
    cross_mix = advance([inner_chain], cross_mix)
    own_back, other_back, first_grad, mix, sums, query_pair = cross_backward(
        ids, cross_queries, cross_own, cross_other, cross_mixed, cross_mix, cross_logsum, first_low,
        first_pre, second_grad, mixed, sums, cross_query, self_out, vecs, owned_rows,
    )
    mix, other_back = receive(feed_chains, mix, other_back)
    got_back = swap_seq(other_back, 1)
    enc_back, key_pair = key_backward(
        ids, encoder, own_back, got_back, cross_key, cross_value, owned_rows
    )
    cross_chains = [
        Scatter(moves, [query_pair, cross_out_pair], x_first),
        Scatter(moves, [key_pair], y_first),
    ]
    enc_rows = enc_out.shape[1]
    mix = depart(cross_chains + feed_chains, mix)
    enc_sent, mix = tie(enc_back[enc_rows:], mix)
    enc_got = swap_seq(enc_sent, 3)
    halfway = HEADS // 4
    one = self_backward(ids, queries, own, other, mixed, mix, logsum, 0, halfway)
    tied = receive(cross_chains, enc_got, outer_chain.got, inner_chain.got, mix, *one)
    enc_got, outer_chain.got, inner_chain.got, mix = tied[:4]
    one = tied[4:]
    rest = jnp.concatenate([c.total() for c in feed_chains], axis=-2)
    rest, mix = tie(rest, mix)
    rest = rest.reshape((-1,) + rest.shape[-2:])
    lines = [[i for i in range(blocks) if i % 2 == side] for side in range(2)]
    rest = lax.psum_scatter(
        rest, "dp", scatter_dimension=0, axis_index_groups=lines, tiled=True
    )[0]
    mix = depart(cross_chains, mix)
    two = self_backward(ids, queries, own, other, mixed, mix, logsum, halfway, HEADS // 2)
    two = receive(cross_chains, *two)
    sent = [tie(h[2], *[c.away for c in cross_chains])[0] for h in (one, two)]
    got_one, got_two = [swap_seq(v, 1) for v in sent]
    part, sums, self_query_pair = query_backward(
        ids, tokens, (one[0], two[0]), (one[3], two[3]), sums, first_grad, self_query, owned_rows
    )
    got_one, got_two, part = tie(got_one, got_two, part)
    bias_sums = sums[INNER_B : INNER_B + chunks].reshape(owners, hidden_rows)
    sums = sums[:13].reshape(13, owners, owned_rows).transpose(1, 0, 2).reshape(owners, counts)
    sums = low(jnp.concatenate([sums, bias_sums], axis=1))
    sums = jnp.pad(sums[:, None, :], ((0, 0), (0, 7), (0, width - counts - hidden_rows)))
    sums = sums.reshape(-1, 2, 8, width)
    sums_pair = (
        lax.dynamic_index_in_dim(sums, seq & 1, 1, keepdims=False),
        lax.dynamic_index_in_dim(sums, 1 - (seq & 1), 1, keepdims=False),
    )
    query_chain = Scatter(moves, [self_query_pair, sums_pair], y_first)
    got_one = depart(cross_chains + [query_chain], got_one)
    total, key_pair, value_pair = key_weights(
        ids, tokens, (one[1], two[1]), (got_one, got_two), owned_rows
    )
    key_chains = [Scatter(moves, [key_pair], x_first), Scatter(moves, [value_pair], y_first)]
    total = receive(cross_chains + [query_chain], total)
    cross_last = joined(cross_chains)
    total = depart(key_chains + [query_chain, cross_last], total)
    token_grad = token_backward(total, part, self_key, self_value)
    token_grad = receive(key_chains + [query_chain, cross_last], token_grad)
    depart(key_chains + [query_chain, cross_last])
    receive(key_chains + [query_chain])
    depart(key_chains)
    last_away = query_chain.away
    receive(key_chains)
    tail_chain = joined(key_chains)
    tail_chain.order = list(tail_chain.order)
    query_chain.away = last_away
    tail_chain.keep = jnp.concatenate([tail_chain.keep, query_chain.keep], axis=-2)
    tail_chain.away = jnp.concatenate([tail_chain.away, query_chain.away], axis=-2)
    token_grad, token_back, tail_chain.away = send_back(token_grad, tail_chain.away)
    tail_chain.ship()
    token_back = receive([tail_chain], token_back)
    while tail_chain.order:
        tail_chain.ship()
        receive([tail_chain])
    while cross_last.got is not None:
        receive([cross_last])
        if cross_last.order:
            cross_last.ship()

    def cut_rows(held, sizes):
        ends = [sum(sizes[: i + 1]) for i in range(len(sizes))]
        return [held[e - n : e] for e, n in zip(ends, sizes)]

    self_key_grad, self_value_grad, self_query_grad, vec = cut_rows(
        tail_chain.held, [owned_rows, owned_rows, owned_rows, 8]
    )
    cross_held = cross_last.held.reshape(-1, owned_rows, width)
    vec = vec[0]
    prompt_grad, cont_grad = place(token_grad, token_back)
    enc_grad = jnp.where(
        group == 0,
        jnp.stack([enc_back[:enc_rows], enc_got]),
        jnp.stack([enc_got, enc_back[:enc_rows]]),
    )

    rest = widen(rest)
    outer_mat_grad = rest[:hidden_rows]
    inner_mat_grad = jnp.concatenate(
        [rest[hidden_rows + i * owned_rows : hidden_rows + (i + 1) * owned_rows] for i in range(chunks)],
        axis=1,
    )
    vec_out = [vec[i * owned_rows : (i + 1) * owned_rows] for i in range(13)]
    inner_bias_out = vec[counts : counts + hidden_rows]
    return (
        prompt_out,
        cont_out,
        prompt_grad,
        cont_grad,
        enc_grad,
        self_query_grad,
        vec_out[0],
        self_key_grad,
        self_value_grad,
        vec_out[1],
        cross_held[1],
        vec_out[2],
        vec_out[3],
        vec_out[4],
        cross_held[0],
        vec_out[5],
        cross_held[3],
        cross_held[4],
        vec_out[6],
        cross_held[2],
        vec_out[7],
        vec_out[8],
        vec_out[9],
        inner_mat_grad,
        inner_bias_out,
        outer_mat_grad,
        vec_out[10],
        vec_out[11],
        vec_out[12],
    )


def solution(mesh):
    rows_spec = P("dp", "seq", None)
    mat, vec = P(("dp", "seq"), None), P(("dp", "seq"))
    weights = (
        mat,
        vec,
        mat,
        mat,
        vec,
        mat,
        vec,
        vec,
        vec,
        mat,
        vec,
        mat,
        mat,
        vec,
        mat,
        vec,
        vec,
        vec,
        mat,
        vec,
        mat,
        vec,
        vec,
        vec,
    )
    in_specs = (rows_spec, rows_spec, rows_spec, P("dp"), rows_spec, rows_spec) + weights
    out_specs = (rows_spec,) * 5 + weights
    return jax.shard_map(body, mesh=mesh, in_specs=in_specs, out_specs=out_specs, check_vma=False)
```

```python
import jax
import jax.numpy as jnp
from jax import lax
from jax.experimental import pallas as pl
from jax.experimental.pallas import tpu as pltpu
from jax.sharding import PartitionSpec as P

HEADS = 12
VMEM_LIMIT = 60 * 1024 * 1024
NEG = -1e30


def matmul(left, right):
    return jnp.dot(left, right, preferred_element_type=jnp.float32)


def contract_rows(left, right):
    return lax.dot_general(
        left, right, (((0,), (0,)), ((), ())), preferred_element_type=jnp.float32
    )


def times_transpose(left, right):
    return lax.dot_general(
        left, right, (((1,), (1,)), ((), ())), preferred_element_type=jnp.float32
    )


def widen(values):
    return values.astype(jnp.float32)


def low(values):
    return values.astype(jnp.bfloat16)


def normalize(values, gain, shift):
    centred = values - jnp.mean(values, axis=-1, keepdims=True)
    scale = lax.rsqrt(jnp.mean(centred * centred, axis=-1, keepdims=True) + 1e-05)
    return centred * scale * gain + shift


def norm_backward(values, gain, upstream):
    centred = values - jnp.mean(values, axis=-1, keepdims=True)
    scale = lax.rsqrt(jnp.mean(centred * centred, axis=-1, keepdims=True) + 1e-05)
    normed = centred * scale
    scaled = upstream * gain
    result = scale * (
        scaled
        - jnp.mean(scaled, axis=-1, keepdims=True)
        - normed * jnp.mean(scaled * normed, axis=-1, keepdims=True)
    )
    return (
        result,
        jnp.sum(upstream * normed, axis=0, keepdims=True),
        jnp.sum(upstream, axis=0, keepdims=True),
    )


(
    SELF_Q,
    SELF_V,
    SELF_O,
    GAIN_ONE,
    SHIFT_ONE,
    CROSS_Q,
    CROSS_V,
    CROSS_O,
    GAIN_TWO,
    SHIFT_TWO,
    OUTER_B,
    GAIN_THREE,
    SHIFT_THREE,
    INNER_B,
) = range(14)


def pack_vectors(vectors, out_ref, base):
    out_ref[base : base + 8, :] = jnp.zeros((8, out_ref.shape[1]), out_ref.dtype)
    for i, ref in enumerate(vectors):
        at = 128 * (i // 8)
        out_ref[base + i % 8 : base + i % 8 + 1, at : at + ref.shape[1]] = ref[...]


def pack(first, vectors, second, outer, inner, rest):
    rows, width = first[0].shape
    chunks = inner.shape[1] // width
    counts = (len(first), len(vectors), len(second), 1, 1, len(rest))

    def kernel(*refs):
        groups, at = [], 0
        for count in counts:
            groups.append(refs[at : at + count])
            at += count
        outs = refs[at:]
        if rows % 8 == 0:
            for i, ref in enumerate(groups[0]):
                outs[0][i * rows : (i + 1) * rows, :] = ref[...]
            for i, ref in enumerate(groups[2]):
                outs[1][i * rows : (i + 1) * rows, :] = ref[...]
            outs[2][: chunks * rows, :] = groups[3][0][...]
            for i in range(chunks):
                at = (chunks + i) * rows
                outs[2][at : at + rows, :] = groups[4][0][:, i * width : (i + 1) * width]
            for i, ref in enumerate(groups[5]):
                at = (2 * chunks + i) * rows
                outs[2][at : at + rows, :] = ref[...]
        pack_vectors(groups[1], outs[0], len(first) * rows if rows % 8 == 0 else 0)

    shapes = [len(first) * rows + 8, len(second) * rows, (2 * chunks + len(rest)) * rows]
    if rows % 8:
        shapes = [8, 8, 8]
    outs = pl.pallas_call(
        kernel,
        out_shape=[jax.ShapeDtypeStruct((n, width), outer.dtype) for n in shapes],
        name="pack",
    )(*first, *[v[None, :] for v in vectors], *second, outer, inner, *rest)
    if rows % 8 == 0:
        return outs
    inner = [inner[:, i * width : (i + 1) * width] for i in range(chunks)]
    return [
        jnp.concatenate(list(first) + [outs[0]], axis=0),
        jnp.concatenate(second, axis=0),
        jnp.concatenate([outer] + inner + list(rest), axis=0),
    ]


class Call:
    def __init__(self, name, grid):
        self.name, self.grid = name, grid
        self.ins, self.in_specs, self.out_shapes, self.out_specs = [], [], [], []
        self.flops, self.bytes, self.exps = 0, 0, 0
        self.lates = []

    def whole(self, array):
        zeros = (0,) * array.ndim
        self.blocked(array, array.shape, lambda *g: zeros, buffers=1)

    def blocked(self, array, block, index, buffers=2):
        mode = {} if buffers == 2 else {"pipeline_mode": pl.Buffered(buffers)}
        self.ins.append(array)
        self.in_specs.append(pl.BlockSpec(block, index, **mode))
        self.bytes += array.size * array.dtype.itemsize

    def scalars(self, array):
        self.ins.append(array)
        self.in_specs.append(pl.BlockSpec(memory_space=pltpu.SMEM))

    def late(self, array, block=None, index=None):
        self.ins.append(array)
        self.in_specs.append(pl.BlockSpec(memory_space=pl.ANY))
        block = block or array.shape
        self.bytes += array.dtype.itemsize * array.size
        self.lates.append((len(self.ins) - 1, block, index, array.dtype))

    def late_weight(self, weight):
        array, block, index = weight
        self.late(array, block, tuple(i * n for i, n in zip(index, block)))

    def late_copies(self, refs, late_refs):
        count = len(self.lates)
        copies = []
        for i, (place, block, start, _) in enumerate(self.lates):
            source = refs[place]
            if start is not None:
                source = source.at[tuple(pl.ds(a, n) for a, n in zip(start, block))]
            copies.append(pltpu.make_async_copy(source, late_refs[i], late_refs[count].at[i]))
        return copies

    def run_late(self, kernel, scratch=()):
        count = len(self.lates)
        steps = self.grid[0]

        def wrapped(*refs):
            refs, late_refs = refs[: -count - 1], refs[-count - 1 :]
            copies = self.late_copies(refs, late_refs)

            @pl.when(pl.program_id(0) == 0)
            def _():
                for copy in copies:
                    copy.start()

            def fetch():
                for copy in copies:
                    copy.wait()

            refs = list(refs)
            for i, (place, _, _, _) in enumerate(self.lates):
                refs[place] = late_refs[i]
            kernel(fetch, *refs)

        buffers = [pltpu.VMEM(block, dtype) for _, block, _, dtype in self.lates]
        return self.run(
            wrapped, list(scratch) + buffers + [pltpu.SemaphoreType.DMA((count,))]
        )

    def weight(self, weight):
        array, block, index = weight
        self.ins.append(array)
        self.in_specs.append(pl.BlockSpec(block, lambda *g: index, pipeline_mode=pl.Buffered(1)))
        self.bytes += array.shape[-1] ** 2 * 2

    def out(self, shape, dtype, block=None, index=None):
        zeros = (0,) * len(shape)
        self.out_shapes.append(jax.ShapeDtypeStruct(shape, dtype))
        self.out_specs.append(pl.BlockSpec(block or shape, index or (lambda *g: zeros)))
        size = 1
        for n in shape:
            size *= n
        self.bytes += size * jnp.dtype(dtype).itemsize

    def run(self, kernel, scratch=()):
        return pl.pallas_call(
            kernel,
            grid=self.grid,
            in_specs=self.in_specs,
            out_specs=self.out_specs,
            out_shape=self.out_shapes,
            scratch_shapes=list(scratch),
            compiler_params=pltpu.CompilerParams(vmem_limit_bytes=VMEM_LIMIT),
            cost_estimate=pl.CostEstimate(
                flops=int(self.flops), bytes_accessed=int(self.bytes), transcendentals=int(self.exps)
            ),
            name=self.name,
        )(*self.ins)


class Halves:
    def __init__(self, call, count, owners, owned_rows, width, heads=None, index=None):
        self.owned_rows = owned_rows
        self.even = owned_rows % 8 == 0
        if self.even:
            shape, outs = (owners // 2, count, owned_rows, width), 2
            block = (heads or owners // 2, 1 if index else count, owned_rows, width)
        else:
            shape, outs = (count, owners * owned_rows, width), 1
            block = (1 if index else count, 2 * (heads or owners // 2) * owned_rows, width)
        for _ in range(outs):
            if index is None:
                call.out(shape, jnp.bfloat16)
            elif self.even:
                call.out(shape, jnp.bfloat16, block, lambda *g: index(*g) + (0, 0))
            else:
                call.out(shape, jnp.bfloat16, block, lambda *g: index(*g)[::-1] + (0,))
        self.outs = outs

    def store(self, refs, at, value, mine):
        if not self.even:
            refs[0][at] = low(value)
            return
        parts = value.reshape(-1, 2, self.owned_rows, value.shape[-1])
        first, second = low(parts[:, 0]), low(parts[:, 1])
        refs[0][:, at] = jnp.where(mine == 0, first, second)
        refs[1][:, at] = jnp.where(mine == 0, second, first)

    def pair(self, results, mine):
        if self.even:
            return tuple(results)
        whole = results[0]
        parts = whole.reshape(whole.shape[0], -1, 2, self.owned_rows, whole.shape[-1])
        return tuple(
            lax.dynamic_index_in_dim(parts, which, 2, keepdims=False).transpose(1, 0, 2, 3)
            for which in (mine, 1 - mine)
        )


def load(ref):
    value = ref[...]
    return value.reshape(-1, value.shape[-1])


def row(vecs_ref, index):
    return vecs_ref[index : index + 1, :]


def fill_bias(bias_ref, chunk, rows, ids_ref):
    half, block = rows // 2, rows // 4
    key = lax.broadcasted_iota(jnp.int32, (rows, rows), 0)
    query = lax.broadcasted_iota(jnp.int32, (rows, rows), 1)
    key_block = jnp.where(
        lax.rem(key, half) < block, ids_ref[2 * chunk], ids_ref[2 * chunk + 1]
    )
    query_block = jnp.where(lax.rem(query, half) < block, ids_ref[0], ids_ref[1])
    key_place = key_block * block + lax.rem(key, block)
    query_place = query_block * block + lax.rem(query, block)
    causal = key_place <= query_place
    prompt_key = key < half
    prompt_query = query < half
    allowed = (prompt_key & prompt_query & causal) | (
        jnp.logical_not(prompt_query)
        & ((prompt_key & (key_place < ids_ref[4])) | (jnp.logical_not(prompt_key) & causal))
    )
    bias_ref[chunk] = jnp.where(allowed, 0.0, NEG)


def lane_masks(values):
    lane = lax.broadcasted_iota(jnp.int32, values.shape, 1)
    zero = jnp.zeros_like(values)
    first = lane < values.shape[1] // 2
    return jnp.where(first, values, zero), jnp.where(first, zero, values)


def key_parts(key_rows, masked):
    if not masked:
        return [(0, key_rows, 0)]
    half = key_rows // 2
    return [(0, half, 0), (half, key_rows, half)]


def widened(values, first, rows, fill):
    if first == 0:
        return values
    blank = jnp.full(values.shape[:-1] + (first,), fill, values.dtype)
    return jnp.concatenate([blank, values], axis=-1)


def attend_pair(queries, keys, values, bias_ref, log_ref):
    rows = queries.shape[0]
    queries = lane_masks(queries)
    parts = [
        (chunk,) + part
        for part in key_parts(keys[0].shape[0], bias_ref is not None)
        for chunk in range(len(keys))
    ]
    outs = []
    for head in range(2):
        scores = []
        for chunk, low_key, high_key, first in parts:
            part = times_transpose(keys[chunk][low_key:high_key], queries[head][first:])
            if bias_ref is not None:
                part = part + bias_ref[chunk, low_key:high_key, first:]
            scores.append(part)
        top = None
        for part, (_, _, _, first) in zip(scores, parts):
            most = widened(part.max(axis=0, keepdims=True), first, rows, NEG)
            top = most if top is None else jnp.maximum(top, most)
        total, mixed = 0.0, 0.0
        for part, (chunk, low_key, high_key, first) in zip(scores, parts):
            weights = jnp.exp(part - top[:, first:])
            total = total + widened(weights.sum(axis=0, keepdims=True), first, rows, 0.0)
            out = contract_rows(values[chunk][low_key:high_key], low(weights))
            mixed = mixed + widened(out, first, rows, 0.0)
        outs.append(mixed * (1.0 / total))
        log_ref[0, head : head + 1, :] = top + jnp.log(total)
    lane = lax.broadcasted_iota(jnp.int32, outs[0].shape, 0)
    return low(jnp.where(lane < outs[0].shape[0] // 2, outs[0], outs[1]).T)


def attend_pair_backward(queries, keys, values, bias_ref, log_ref, mixed, upstream):
    rows = queries.shape[0]
    queries = lane_masks(queries)
    ups = lane_masks(upstream)
    product = widen(mixed) * widen(upstream)
    high = low(product)
    rest = low(product - widen(high))
    pair = product.shape[1]
    lane = lax.broadcasted_iota(jnp.int32, (8, pair), 1)
    line = lax.broadcasted_iota(jnp.int32, (8, pair), 0)
    pick = jnp.where(
        ((lane < pair // 2) & (line == 0)) | ((lane >= pair // 2) & (line == 1)), 1.0, 0.0
    ).astype(jnp.bfloat16)
    delta = times_transpose(pick, high) + times_transpose(pick, rest)
    dq = 0.0
    parts = key_parts(keys[0].shape[0], bias_ref is not None)
    dk = [[0.0] * len(parts) for _ in keys]
    dv = [[0.0] * len(parts) for _ in keys]
    for head in range(2):
        for chunk in range(len(keys)):
            masked_keys = lane_masks(keys[chunk])[head]
            for i, (low_key, high_key, first) in enumerate(parts):
                part = times_transpose(keys[chunk][low_key:high_key], queries[head][first:])
                if bias_ref is not None:
                    part = part + bias_ref[chunk, low_key:high_key, first:]
                probs = jnp.exp(part - log_ref[0, head : head + 1, first:])
                up = ups[head][first:]
                prob_grad = times_transpose(values[chunk][low_key:high_key], up)
                score_grad = low(probs * (prob_grad - delta[head : head + 1, first:]))
                dv[chunk][i] = dv[chunk][i] + matmul(low(probs), up)
                dk[chunk][i] = dk[chunk][i] + matmul(score_grad, queries[head][first:])
                out = contract_rows(masked_keys[low_key:high_key], score_grad)
                dq = dq + widened(out, first, rows, 0.0)
    join = [
        [v[0] if len(v) == 1 else jnp.concatenate(v, axis=0) for v in side] for side in (dk, dv)
    ]
    return low(dq.T), join[0], join[1]


def project_kernel(scaled, x_ref, *refs):
    vecs_ref = refs[-3] if scaled else refs[-2]
    values = x_ref[...]
    if scaled:
        wq_ref, wk_ref, wv_ref = refs[:3]
        q_ref, kv_ref = refs[-2:]
        q_ref[...] = low((matmul(values, load(wq_ref)) + row(vecs_ref, SELF_Q)) * 0.125)
        bias = row(vecs_ref, SELF_V)
    else:
        wk_ref, wv_ref = refs[:2]
        kv_ref = refs[-1]
        bias = row(vecs_ref, CROSS_V)
    kv_ref[0] = low(matmul(values, load(wk_ref)))
    kv_ref[1] = low(matmul(values, load(wv_ref)) + bias)


def project(tokens, weights, vecs):
    rows, width = tokens.shape
    scaled = len(weights) == 3
    call = Call("project", (1,))
    call.whole(tokens)
    for weight in weights:
        call.weight(weight)
    call.whole(vecs)
    if scaled:
        call.out((rows, width), jnp.bfloat16)
    call.out((2, rows, width), jnp.bfloat16)
    call.flops = 2 * len(weights) * rows * width * width

    def kernel(*refs):
        project_kernel(scaled, *refs)

    return call.run(kernel)


def lanes_of(width):
    lanes = 2 * (width // HEADS)

    def at(h):
        return pl.ds(pl.multiple_of(h * lanes, lanes), lanes)

    return lanes, at


def self_attend(ids, queries, own, other):
    rows, width = queries.shape
    pairs = HEADS // 2
    lanes, _ = lanes_of(width)
    call = Call("self_attend", (pairs,))
    call.scalars(ids)
    call.blocked(queries, (rows, lanes), lambda h: (0, h))
    for array in (own, other):
        call.blocked(array, (2, rows, lanes), lambda h: (0, 0, h))
    call.out((rows, width), jnp.bfloat16, (rows, lanes), lambda h: (0, h))
    call.out((pairs, 2, rows), jnp.float32, (1, 2, rows), lambda h: (h, 0, 0))
    call.flops = 16 * rows * rows * width
    call.exps = 2 * rows * rows * HEADS

    def kernel(ids_ref, q_ref, own_ref, other_ref, mixed_ref, log_ref, bias_ref):
        @pl.when(pl.program_id(0) == 0)
        def _():
            for chunk in range(2):
                fill_bias(bias_ref, chunk, rows, ids_ref)

        keys, values = (own_ref[0], other_ref[0]), (own_ref[1], other_ref[1])
        mixed_ref[...] = attend_pair(q_ref[...], keys, values, bias_ref, log_ref)

    return call.run(kernel, [pltpu.VMEM((2, rows, rows), jnp.float32)])


def self_finish(tokens, mixed, out_weight, query_weight, vecs):
    rows, width = tokens.shape
    call = Call("self_finish", (1,))
    call.whole(tokens)
    call.whole(mixed)
    call.weight(out_weight)
    call.weight(query_weight)
    call.whole(vecs)
    call.out((rows, width), jnp.float32)
    call.out((rows, width), jnp.bfloat16)
    call.out((rows, width), jnp.bfloat16)
    call.flops = 4 * rows * width * width

    def kernel(x_ref, mixed_ref, wo_ref, wq_ref, vecs_ref, pre_ref, low_ref, next_ref):
        pre = widen(x_ref[...]) + matmul(mixed_ref[...], load(wo_ref)) + row(vecs_ref, SELF_O)
        pre_ref[...] = pre
        first = low(normalize(pre, row(vecs_ref, GAIN_ONE), row(vecs_ref, SHIFT_ONE)))
        low_ref[...] = first
        next_ref[...] = low((matmul(first, load(wq_ref)) + row(vecs_ref, CROSS_Q)) * 0.125)

    return call.run(kernel)


def cross_attend(queries, keys, first_pre, out_weight, vecs):
    rows, width = queries.shape
    key_rows = keys.shape[1]
    pairs = HEADS // 2
    lanes, at = lanes_of(width)
    call = Call("cross_attend", (pairs,))
    call.blocked(queries, (rows, lanes), lambda h: (0, h))
    call.blocked(keys, (2, key_rows, lanes), lambda h: (0, 0, h))
    call.late(first_pre)
    call.late_weight(out_weight)
    call.whole(vecs)
    call.out((rows, width), jnp.bfloat16)
    call.out((pairs, 2, rows), jnp.float32, (1, 2, rows), lambda h: (h, 0, 0))
    call.out((rows, width), jnp.float32)
    call.out((rows, width), jnp.bfloat16)
    call.flops = 8 * rows * key_rows * width + 2 * rows * width * width
    call.exps = 2 * rows * key_rows * HEADS

    def kernel(
        fetch, q_ref, keys_ref, first_ref, wo_ref, vecs_ref, mixed_ref, log_ref, pre_ref, low_ref
    ):
        step = pl.program_id(0)
        mixed_ref[:, at(step)] = attend_pair(
            q_ref[...], (keys_ref[0],), (keys_ref[1],), None, log_ref
        )

        @pl.when(step == pairs - 1)
        def _():
            fetch()
            first = normalize(first_ref[...], row(vecs_ref, GAIN_ONE), row(vecs_ref, SHIFT_ONE))
            pre = first + matmul(mixed_ref[...], load(wo_ref)) + row(vecs_ref, CROSS_O)
            pre_ref[...] = pre
            low_ref[...] = low(normalize(pre, row(vecs_ref, GAIN_TWO), row(vecs_ref, SHIFT_TWO)))

    return call.run_late(kernel)


def feed_blocks(call, feed, width, chunks, owned_rows):
    owners = feed.shape[0]

    def at(i):
        return jnp.minimum(i, chunks - 1)

    hidden_rows = chunks * owned_rows
    if owned_rows % 8 == 0:
        call.blocked(feed, (owners, owned_rows, width), lambda i: (0, chunks + at(i), 0))
        call.blocked(feed, (owners // chunks, hidden_rows, width), lambda i: (at(i), 0, 0))
    else:
        parts = [
            feed[:, hidden_rows + i * owned_rows : hidden_rows + (i + 1) * owned_rows]
            for i in range(chunks)
        ]
        parts = [p.reshape(-1, width) for p in parts]
        call.blocked(jnp.concatenate(parts, axis=1), (width, width), lambda i: (0, at(i)))
        call.blocked(feed[:, :hidden_rows].reshape(-1, width), (width, width), lambda i: (at(i), 0))


def feed_forward(ids, second_pre, second_low, upstream, feed, vecs, chunks, owned_rows):
    rows, width = second_low.shape
    hidden = chunks * width
    owners = width // owned_rows
    call = Call("feed_forward", (2 * chunks,))
    call.scalars(ids)
    call.whole(second_pre)
    call.whole(second_low)
    call.late(upstream)
    feed_blocks(call, feed, width, chunks, owned_rows)
    call.whole(vecs)
    call.out(
        (rows, hidden), jnp.bfloat16, (rows, width), lambda i: (0, jnp.minimum(i, chunks - 1))
    )
    call.out((rows, width), jnp.bfloat16)
    call.out((rows, width), jnp.float32)
    call.out((rows, width), jnp.bfloat16)
    call.out((24, width), jnp.float32)
    half = Halves(
        call,
        1,
        owners,
        chunks * owned_rows,
        width,
        owners // 2 // chunks,
        lambda i: (jnp.maximum(i - chunks, 0), 0),
    )
    call.flops = 6 * rows * hidden * width
    call.exps = 2 * rows * hidden

    def kernel(
        fetch, ids_ref, pre_ref, low_ref, up_ref, inner_ref, outer_ref, vecs_ref, slope_ref, out_ref,
        grad_ref, third_low_ref, sums_ref, *rest,
    ):
        grads, (active_ref, third_ref) = rest[:-2], rest[-2:]
        step = pl.program_id(0)

        @pl.when(step == 0)
        def _():
            second = normalize(pre_ref[...], row(vecs_ref, GAIN_TWO), row(vecs_ref, SHIFT_TWO))
            third_ref[...] = second + row(vecs_ref, OUTER_B)

        @pl.when(step < chunks)
        def _():
            inner = matmul(low_ref[...], load(inner_ref)) + vecs_ref[pl.ds(INNER_B + step, 1), :]
            bell = 0.5 * (1.0 + lax.erf(inner * 0.7071067811865476))
            active = low(inner * bell)
            active_ref[step] = active
            density = jnp.exp(-0.5 * inner * inner) * 0.3989422804014327
            slope_ref[...] = low(bell + inner * density)
            third_ref[...] += matmul(active, load(outer_ref))

        @pl.when(step == chunks - 1)
        def _():
            fetch()
            third = third_ref[...]
            gain = row(vecs_ref, GAIN_THREE)
            out_ref[...] = low(normalize(third, gain, row(vecs_ref, SHIFT_THREE)))
            grad, gain_sum, shift_sum = norm_backward(third, gain, widen(up_ref[...]))
            grad_ref[...] = grad
            third_low_ref[...] = low(grad)
            sums_ref[...] = jnp.zeros_like(sums_ref)
            sums_ref[GAIN_THREE : GAIN_THREE + 1, :] = gain_sum
            sums_ref[SHIFT_THREE : SHIFT_THREE + 1, :] = shift_sum
            sums_ref[OUTER_B : OUTER_B + 1, :] = jnp.sum(widen(low(grad)), axis=0, keepdims=True)

        @pl.when(step >= chunks)
        def _():
            active = active_ref[jnp.maximum(step - chunks, 0)]
            half.store(grads, 0, contract_rows(active, third_low_ref[...]), ids_ref[5])

    results = call.run_late(
        kernel,
        [pltpu.VMEM((chunks, rows, width), jnp.bfloat16), pltpu.VMEM((rows, width), jnp.float32)],
    )
    return tuple(results[:5]) + (half.pair(results[5:], ids[5]),)


def inner_backward(
    ids, third_grad, third_low, sums, second_pre, second_low, slope, cross_mixed, feed, out_weight, vecs,
    chunks, owned_rows,
):
    rows, width = second_low.shape
    owners = width // owned_rows
    call = Call("inner_backward", (chunks,))
    call.scalars(ids)
    for array in (third_grad, third_low, sums):
        call.whole(array)
    call.late(second_pre)
    call.whole(second_low)
    call.blocked(slope, (rows, width), lambda i: (0, i))
    call.late(cross_mixed)
    feed_blocks(call, feed, width, chunks, owned_rows)
    call.late_weight(out_weight)
    call.whole(vecs)
    call.out((rows, width), jnp.float32)
    call.out((rows, width), jnp.bfloat16)
    call.out((24, width), jnp.float32)
    inner_half = Halves(call, chunks, owners, owned_rows, width, owners // 2, lambda i: (0, i))
    out_half = Halves(call, 1, owners, owned_rows, width)
    call.flops = 6 * rows * chunks * width * width + 4 * rows * width * width
    outs = inner_half.outs

    def kernel(
        fetch, ids_ref, third_ref, third_low_ref, sums_in_ref, second_ref, low_ref, slope_ref, mixed_ref, inner_ref, outer_ref,
        wo_ref, vecs_ref, second_grad_ref, mix_ref, sums_ref, *rest,
    ):
        inner_grads, out_grads, total_ref = rest[:outs], rest[outs:-1], rest[-1]
        step = pl.program_id(0)
        mine = ids_ref[5]

        @pl.when(step == 0)
        def _():
            total_ref[...] = third_ref[...]
            sums_ref[...] = sums_in_ref[...]

        inner_low = low(times_transpose(third_low_ref[...], load(outer_ref)) * widen(slope_ref[...]))
        total_ref[...] += times_transpose(inner_low, load(inner_ref))
        inner_half.store(inner_grads, 0, contract_rows(low_ref[...], inner_low), mine)
        sums_ref[pl.ds(INNER_B + step, 1), :] = jnp.sum(widen(inner_low), axis=0, keepdims=True)

        @pl.when(step == chunks - 1)
        def _():
            fetch()
            grad, gain_sum, shift_sum = norm_backward(
                second_ref[...], row(vecs_ref, GAIN_TWO), total_ref[...]
            )
            second_grad_ref[...] = grad
            cross_low = low(grad)
            sums_ref[GAIN_TWO : GAIN_TWO + 1, :] = gain_sum
            sums_ref[SHIFT_TWO : SHIFT_TWO + 1, :] = shift_sum
            sums_ref[CROSS_O : CROSS_O + 1, :] = jnp.sum(widen(cross_low), axis=0, keepdims=True)
            mix_ref[...] = low(times_transpose(cross_low, load(wo_ref)))
            out_half.store(out_grads, 0, contract_rows(mixed_ref[...], cross_low), mine)

    results = call.run_late(kernel, [pltpu.VMEM((rows, width), jnp.float32)])
    core = ids[5]
    return tuple(results[:3]) + (
        inner_half.pair(results[3 : 3 + outs], core),
        out_half.pair(results[3 + outs :], core),
    )


def cross_backward(
    ids, queries, keys, mixed, upstream, logsum, first_low, first_pre, second_grad, self_mixed, sums,
    encoder, query_weight, out_weight, key_weight, value_weight, vecs, owned_rows,
):
    rows, width = queries.shape
    key_rows = keys.shape[1]
    pairs = HEADS // 2
    lanes, at = lanes_of(width)
    call = Call("cross_backward", (pairs,))
    call.scalars(ids)
    for array in (queries, mixed, upstream):
        call.blocked(array, (rows, lanes), lambda h: (0, h))
    call.blocked(logsum, (1, 2, rows), lambda h: (h, 0, 0))
    call.blocked(keys, (2, key_rows, lanes), lambda h: (0, 0, h))
    for array in (first_low, first_pre, second_grad, self_mixed):
        call.late(array)
    call.whole(sums)
    call.late_weight(query_weight)
    call.late_weight(out_weight)
    call.late(encoder)
    call.late_weight(key_weight)
    call.late_weight(value_weight)
    call.whole(vecs)
    call.out((key_rows, width), jnp.bfloat16)
    call.out((rows, width), jnp.float32)
    call.out((rows, width), jnp.bfloat16)
    call.out((24, width), jnp.float32)
    halves = [Halves(call, 2, width // owned_rows, owned_rows, width) for _ in range(2)]
    outs = halves[0].outs
    call.flops = 20 * rows * key_rows * width + 8 * (rows + key_rows) * width * width
    call.exps = 2 * rows * key_rows * HEADS

    def kernel(
        fetch, ids_ref, q_ref, mixed_ref, up_ref, log_ref, keys_ref, low_ref, pre_ref, grad_ref,
        self_mixed_ref, sums_in_ref, wq_ref, wo_ref, enc_ref, wk_ref, wv_ref, vecs_ref, enc_back_ref, first_ref, mix_ref,
        sums_ref, *rest,
    ):
        step = pl.program_id(0)
        weights_refs, (dq_ref, dkv_ref) = rest[:-2], rest[-2:]

        @pl.when(step == 0)
        def _():
            sums_ref[...] = sums_in_ref[...]

        dq, dk, dv = attend_pair_backward(
            q_ref[...], (keys_ref[0],), (keys_ref[1],), None, log_ref, mixed_ref[...], up_ref[...]
        )
        dq_ref[:, at(step)] = dq
        dkv_ref[0, :, at(step)] = low(dk[0])
        dkv_ref[1, :, at(step)] = low(dv[0])
        sums_ref[CROSS_V : CROSS_V + 1, at(step)] = sum(jnp.sum(v, axis=0, keepdims=True) for v in dv)

        @pl.when(step == pairs - 1)
        def _():
            fetch()
            query_low = dq_ref[...]
            halves[0].store(weights_refs[:outs], 0, contract_rows(low_ref[...], query_low) * 0.125, ids_ref[5])
            for i in range(2):
                value = contract_rows(enc_ref[...], dkv_ref[i])
                halves[1].store(weights_refs[outs:], i, value, ids_ref[5])
            enc_back_ref[...] = low(
                times_transpose(dkv_ref[0], load(wk_ref)) + times_transpose(dkv_ref[1], load(wv_ref))
            )
            total = grad_ref[...] + times_transpose(query_low, load(wq_ref)) * 0.125
            grad, gain_sum, shift_sum = norm_backward(pre_ref[...], row(vecs_ref, GAIN_ONE), total)
            first_ref[...] = grad
            self_low = low(grad)
            mix_ref[...] = low(times_transpose(self_low, load(wo_ref)))
            halves[0].store(weights_refs[:outs], 1, contract_rows(self_mixed_ref[...], self_low), ids_ref[5])
            sums_ref[GAIN_ONE : GAIN_ONE + 1, :] = gain_sum
            sums_ref[SHIFT_ONE : SHIFT_ONE + 1, :] = shift_sum
            sums_ref[SELF_O : SELF_O + 1, :] = jnp.sum(widen(self_low), axis=0, keepdims=True)
            sums_ref[CROSS_Q : CROSS_Q + 1, :] = jnp.sum(widen(query_low), axis=0, keepdims=True) * 0.125

    results = call.run_late(
        kernel,
        [pltpu.VMEM((rows, width), jnp.bfloat16), pltpu.VMEM((2, key_rows, width), jnp.bfloat16)],
    )
    return tuple(results[:4]) + (
        halves[0].pair(results[4 : 4 + outs], ids[5]),
        halves[1].pair(results[4 + outs :], ids[5]),
    )


def self_backward(ids, queries, own, other, mixed, upstream, logsum, first, last):
    rows, width = queries.shape
    lanes, _ = lanes_of(width)
    count = last - first
    call = Call("self_backward", (count,))
    call.scalars(ids)
    for array in (queries, mixed, upstream):
        call.blocked(array, (rows, lanes), lambda h: (0, first + h))
    call.blocked(logsum, (1, 2, rows), lambda h: (first + h, 0, 0))
    for array in (own, other):
        call.blocked(array, (2, rows, lanes), lambda h: (0, 0, first + h))
    call.out((rows, count * lanes), jnp.bfloat16, (rows, lanes), lambda h: (0, h))
    for _ in range(2):
        call.out(
            (2, rows, count * lanes), jnp.bfloat16, (2, rows, lanes), lambda h: (0, 0, h)
        )
    call.out((8, count * lanes), jnp.float32, (8, lanes), lambda h: (0, h))
    call.flops = 40 * rows * rows * count * lanes
    call.exps = 4 * rows * rows * count

    def kernel(
        ids_ref, q_ref, mixed_ref, up_ref, log_ref, own_ref, other_ref, dq_ref, own_out_ref,
        other_out_ref, sums_ref, bias_ref,
    ):
        @pl.when(pl.program_id(0) == 0)
        def _():
            for chunk in range(2):
                fill_bias(bias_ref, chunk, rows, ids_ref)

        keys, values = (own_ref[0], other_ref[0]), (own_ref[1], other_ref[1])
        dq, dk, dv = attend_pair_backward(
            q_ref[...], keys, values, bias_ref, log_ref, mixed_ref[...], up_ref[...]
        )
        dq_ref[...] = dq
        for chunk, out in enumerate((own_out_ref, other_out_ref)):
            out[0] = low(dk[chunk])
            out[1] = low(dv[chunk])
        sums_ref[0:1, :] = sum(jnp.sum(v, axis=0, keepdims=True) for v in dv)
        sums_ref[1:2, :] = jnp.sum(widen(dq), axis=0, keepdims=True) * 0.125

    return call.run(kernel, [pltpu.VMEM((2, rows, rows), jnp.float32)])


def query_backward(ids, tokens, query_low, half_sums, sums, first_grad, query_weight, owned_rows):
    rows, width = tokens.shape
    call = Call("query_backward", (1,))
    call.scalars(ids)
    for array in (tokens, first_grad, sums) + tuple(query_low) + tuple(half_sums):
        call.whole(array)
    call.weight(query_weight)
    call.out((rows, width), jnp.float32)
    call.out((24, width), jnp.float32)
    half = Halves(call, 1, width // owned_rows, owned_rows, width)
    call.flops = 4 * rows * width * width

    def kernel(
        ids_ref, x_ref, grad_ref, sums_in_ref, first_ref, second_ref, first_sums_ref, second_sums_ref,
        wq_ref, part_ref, sums_ref, *weights_refs,
    ):
        sums_ref[...] = sums_in_ref[...]
        cut = first_ref.shape[1]
        for lanes, ref in ((slice(0, cut), first_sums_ref), (slice(cut, width), second_sums_ref)):
            sums_ref[SELF_V : SELF_V + 1, lanes] = ref[0:1, :]
            sums_ref[SELF_Q : SELF_Q + 1, lanes] = ref[1:2, :]
        query = jnp.concatenate([first_ref[...], second_ref[...]], axis=1)
        half.store(weights_refs, 0, contract_rows(x_ref[...], query) * 0.125, ids_ref[5])
        part_ref[...] = grad_ref[...] + times_transpose(query, load(wq_ref)) * 0.125

    results = call.run(kernel)
    return results[0], results[1], half.pair(results[2:], ids[5])


def key_weights(ids, tokens, mine, got, owned_rows):
    rows, width = tokens.shape
    call = Call("key_weights", (1,))
    call.scalars(ids)
    for array in (tokens,) + tuple(mine) + tuple(got):
        call.whole(array)
    call.out((2, rows, width), jnp.bfloat16)
    halves = [Halves(call, 1, width // owned_rows, owned_rows, width) for _ in range(2)]
    outs = halves[0].outs
    call.flops = 4 * rows * width * width

    def kernel(ids_ref, x_ref, mine_a, mine_b, got_a, got_b, total_ref, *weights_refs):
        values = x_ref[...]
        for i in range(2):
            total = low(
                jnp.concatenate(
                    [widen(m[i]) + widen(g[i]) for m, g in ((mine_a, got_a), (mine_b, got_b))], axis=1
                )
            )
            total_ref[i] = total
            refs = weights_refs[i * outs : (i + 1) * outs]
            halves[i].store(refs, 0, contract_rows(values, total), ids_ref[5])

    results = call.run(kernel)
    return (results[0],) + tuple(
        halves[i].pair(results[1 + i * outs : 1 + (i + 1) * outs], ids[5]) for i in range(2)
    )


def token_backward(total, part, key_weight, value_weight):
    rows, width = part.shape
    call = Call("token_backward", (1,))
    call.whole(total)
    call.whole(part)
    call.weight(key_weight)
    call.weight(value_weight)
    call.out((rows, width), jnp.bfloat16)
    call.flops = 4 * rows * width * width

    def kernel(total_ref, part_ref, wk_ref, wv_ref, out_ref):
        out_ref[...] = low(
            part_ref[...]
            + times_transpose(total_ref[0], load(wk_ref))
            + times_transpose(total_ref[1], load(wv_ref))
        )

    return call.run(kernel)[0]


def flip(size, bit):
    return [(i, i ^ bit) for i in range(size)]


def swap_seq(values, bits):
    return lax.ppermute(values, "seq", flip(lax.axis_size("seq"), bits))


def tie(*values):
    return lax.optimization_barrier(values)


def bit_order(dp_size, seq_size):
    return [("dp", b) for b in range(dp_size.bit_length() - 1)][::-1] + [
        ("seq", b) for b in range(seq_size.bit_length() - 1)
    ][::-1]


class Moves:
    def __init__(self):
        self.spots = {name: lax.axis_index(name) for name in ("dp", "seq")}
        self.sizes = {name: lax.axis_size(name) for name in ("dp", "seq")}
        self.canonical = bit_order(self.sizes["dp"], self.sizes["seq"])

    def mine(self, step):
        return (self.spots[step[0]] >> step[1]) & 1

    def send(self, values, step):
        name, bit = step
        flat = values.reshape(-1, values.shape[-1])
        return lax.ppermute(flat, name, flip(self.sizes[name], 1 << bit)).reshape(values.shape)


def split_sum(keep, got, at, mine):
    def side(which):
        first, second = [
            lax.dynamic_index_in_dim(v, which, at, keepdims=False) for v in (keep, got)
        ]
        return low(widen(first) + widen(second))

    return side(mine), side(1 - mine)


class Scatter:
    def __init__(self, moves, pairs, order):
        self.moves = moves
        self.dims = [step for step in moves.canonical if step != order[0]]
        self.order = list(order)
        pieces = (2,) * len(self.dims)

        def join(arrays):
            arrays = [a.reshape(pieces + (-1, a.shape[-1])) for a in arrays]
            return arrays[0] if len(arrays) == 1 else jnp.concatenate(arrays, axis=-2)

        self.keep = join([k for k, _ in pairs])
        self.away = join([a for _, a in pairs])
        self.got = None

    def ship(self):
        self.got = self.moves.send(self.away, self.order.pop(0))
        self.away = None

    def take(self):
        got, self.got = self.got, None
        if self.order:
            step = self.order[0]
            at = self.dims.index(step)
            self.keep, self.away = split_sum(self.keep, got, at, self.moves.mine(step))
            self.dims.pop(at)
        else:
            self.held = widen(self.keep) + widen(got)

    def total(self):
        return low(widen(self.keep) + widen(self.got))


def joined(chains):
    first = chains[0]
    chain = object.__new__(Scatter)
    chain.moves, chain.dims, chain.order, chain.got = first.moves, first.dims, first.order, None
    chain.keep = jnp.concatenate([c.keep for c in chains], axis=-2)
    chain.away = jnp.concatenate([c.away for c in chains], axis=-2)
    return chain


def receive(chains, *values):
    tied = tie(*[c.got for c in chains], *values)
    for chain, got in zip(chains, tied):
        chain.got = got
        chain.take()
    values = tied[len(chains) :]
    return values[0] if len(values) == 1 else values


def depart(chains, *values):
    tied = tie(*[c.away for c in chains], *values)
    for chain, away in zip(chains, tied):
        chain.away = away
        chain.ship()
    values = tied[len(chains) :]
    return values[0] if len(values) == 1 else values


def advance(chains, *values):
    values = receive(chains, *values)
    return depart(chains, *(values if isinstance(values, (list, tuple)) else (values,)))


def line_sends(moves, totals, first):
    count = totals.shape[0]
    spot = moves.spots["dp"] >> first
    keep = lax.dynamic_index_in_dim(totals, spot, 0, keepdims=False)
    away = [
        lax.dynamic_index_in_dim(totals, spot ^ i, 0, keepdims=False) for i in range(1, count)
    ]
    away = tie(*away)
    size = moves.sizes["dp"]
    return keep, [lax.ppermute(v, "dp", flip(size, i << first)) for i, v in enumerate(away, 1)]


class Gather:
    def __init__(self, moves, held, order, dims=()):
        self.moves, self.held, self.order, self.dims = moves, held, list(order), list(dims)

    def ship(self):
        self.got = self.moves.send(self.held, self.order[0])

    def take(self):
        step = self.order.pop(0)
        mine = self.moves.mine(step)
        first = jnp.where(mine == 0, self.held, self.got)
        second = jnp.where(mine == 0, self.got, self.held)
        self.held = jnp.stack([first, second], axis=0)
        self.dims.insert(0, step)

    def part(self, first, last, order):
        return Gather(self.moves, self.held[..., first:last, :], order, self.dims)

    def result(self):
        order = [self.dims.index(step) for step in self.moves.canonical]
        count = len(order)
        held = self.held.transpose(order + [count, count + 1])
        return held.reshape((-1,) + held.shape[-2:])


def pump(taking, shipping, *values):
    tied = tie(*[g.got for g in taking], *values)
    for gather, got in zip(taking, tied):
        gather.got = got
        gather.take()
    tied = tie(*[g.held for g in shipping], *tied[len(taking) :])
    for gather, held in zip(shipping, tied):
        gather.held = held
        gather.ship()
    values = tied[len(shipping) :]
    return values[0] if len(values) == 1 else values


def body(
    prompt_in,
    cont_in,
    enc_out,
    prefix,
    prompt_cot,
    cont_cot,
    self_query,
    self_qbias,
    self_key,
    self_value,
    self_vbias,
    self_out,
    self_obias,
    gain_one,
    shift_one,
    cross_query,
    cross_qbias,
    cross_key,
    cross_value,
    cross_vbias,
    cross_out,
    cross_obias,
    gain_two,
    shift_two,
    inner_mat,
    inner_bias,
    outer_mat,
    outer_bias,
    gain_three,
    shift_three,
):
    seq = lax.axis_index("seq")
    parts, blocks = lax.axis_size("seq"), lax.axis_size("dp")
    rows = prompt_in.shape[1]
    width = prompt_in.shape[2]
    owned_rows = self_query.shape[0]
    group = seq // 2
    ids = jnp.stack([seq, 3 - seq, seq ^ 1, 3 - (seq ^ 1), prefix[group], seq & 1]).astype(jnp.int32)

    def pick(array, index):
        return lax.dynamic_index_in_dim(array, index, 0, keepdims=False)

    vectors = [
        self_qbias,
        self_vbias,
        self_obias,
        gain_one,
        shift_one,
        cross_qbias,
        cross_vbias,
        cross_obias,
        gain_two,
        shift_two,
        outer_bias,
        gain_three,
        shift_three,
    ]
    hidden_rows = outer_mat.shape[0]
    chunks = hidden_rows // owned_rows
    first_part, second_part, feed = pack(
        [self_query, self_key, self_value],
        vectors + [inner_bias],
        [self_out, cross_query],
        outer_mat,
        inner_mat,
        [cross_key, cross_value, cross_out],
    )
    moves = Moves()
    bits = moves.canonical
    dp_bits, hi, lo = bits[:-2], bits[-2], bits[-1]
    line, near = dp_bits[:-1], dp_bits[-1]
    cut = 2 * owned_rows
    one = Gather(moves, first_part, line)
    one.ship()
    prompt_got = swap_seq(pick(prompt_in, 1 - group), 3)
    sent = jnp.concatenate([pick(v, 1 - group) for v in (cont_in, enc_out)], axis=0)
    feed = lax.all_gather(feed, ("dp", "seq"), axis=0, tiled=False)
    prompt_got, sent, second_part = pump([one], [one], prompt_got, sent, second_part)
    two = Gather(moves, second_part, line)
    got = swap_seq(sent, 3)
    while len(one.order) > 1:
        pump([one], [one])
    got = pump([one], [], got)
    one_parts = [
        one.part(0, cut, [near, hi, lo]),
        one.part(cut, first_part.shape[0], [hi, near, lo]),
    ]
    got = pump([], one_parts + [two], got)
    got = pump(one_parts + [two], one_parts + [two], got)
    while len(two.order) > 1:
        got = pump([two], [two], got)
    got = pump(one_parts + [two], one_parts, got)
    two_parts = [
        two.part(0, owned_rows, [near, hi, lo]),
        two.part(owned_rows, second_part.shape[0], [hi, near, lo]),
    ]
    got = pump(one_parts, two_parts, got)

    tokens = jnp.concatenate(
        [pick(prompt_in, group), prompt_got, pick(cont_in, group), got[:rows]], axis=0
    )
    encoder = jnp.concatenate([pick(enc_out, group), got[rows:]], axis=0)
    enc_other = swap_seq(encoder, 1)

    def square(array, index):
        if owned_rows % 8 == 0:
            return array, (array.shape[0], owned_rows, width), (0, index, 0)
        part = array[:, index * owned_rows : (index + 1) * owned_rows].reshape(-1, width)
        return part, part.shape, (0, 0)

    front, back = [g.result() for g in one_parts]
    self_query, self_key, self_value = square(front, 0), square(front, 1), square(back, 0)
    tail = back[:, owned_rows:]
    owners = parts * blocks
    counts = 13 * owned_rows
    slots = tail.reshape(owners, 8, -1, 128)[:, :, :2, :owned_rows]
    vecs = slots.transpose(2, 1, 0, 3).reshape(16, width)[:13]
    biases = tail[:, 5, 128 : 128 + hidden_rows].reshape(chunks, width)
    vecs = widen(jnp.concatenate([vecs, biases], axis=0))

    queries, own = project(tokens, [self_query, self_key, self_value], vecs)
    own = pump(two_parts, two_parts, own)
    other = swap_seq(own, 1)
    mixed, logsum = self_attend(ids, queries, own, other)
    mixed = pump(two_parts, two_parts, mixed)
    mixed = pump(two_parts, [], mixed)
    front, back = [g.result() for g in two_parts]
    self_out, cross_query = square(front, 0), square(back, 0)
    cot_sent = jnp.concatenate([pick(v, 1 - group) for v in (prompt_cot, cont_cot)], axis=0)
    cot_sent, mixed = tie(cot_sent, mixed)
    cot_got = swap_seq(cot_sent, 3)
    first_pre, first_low, cross_queries = self_finish(tokens, mixed, self_out, cross_query, vecs)
    cross_queries, cot_got, feed = tie(cross_queries, cot_got, feed)
    cross_key, cross_value, cross_out = [square(feed, 2 * chunks + i) for i in range(3)]
    both = jnp.concatenate([encoder, enc_other], axis=0)
    (cross_keys,) = project(both, [cross_key, cross_value], vecs)
    cross_mixed, cross_logsum, second_pre, second_low = cross_attend(
        cross_queries, cross_keys, first_pre, cross_out, vecs
    )
    upstream = jnp.concatenate(
        [pick(prompt_cot, group), cot_got[:rows], pick(cont_cot, group), cot_got[rows:]], axis=0
    )
    slope, result, third_grad, third_low, sums, outer_pair = feed_forward(
        ids, second_pre, second_low, upstream, feed, vecs, chunks, owned_rows
    )

    def send_back(own, *values):
        away = jnp.concatenate([own[rows : 2 * rows], own[3 * rows :]], axis=0)
        tied = tie(away, *values)
        return (own, swap_seq(tied[0], 3)) + tuple(tied[1:])

    def place(own, back):
        kept = (own[:rows], own[2 * rows : 3 * rows])
        back = (back[:rows], back[rows:])
        return [
            jnp.where(group == 0, jnp.stack([a, b]), jnp.stack([b, a])) for a, b in zip(kept, back)
        ]

    bits = dp_bits[::-1]
    x_first = [lo, hi] + bits
    y_first = [lo, bits[0], hi] + bits[1:]
    outer_chain = Scatter(moves, [outer_pair], x_first)
    third_low = depart([outer_chain], third_low)
    result, result_back, third_low = send_back(result, third_low)
    second_grad, cross_mix, sums, inner_pair, cross_out_pair = inner_backward(
        ids, third_grad, third_low, sums, second_pre, second_low, slope, cross_mixed, feed, cross_out,
        vecs, chunks, owned_rows,
    )
    cross_mix, result_back = tie(cross_mix, result_back)
    prompt_out, cont_out = place(result, result_back)
    inner_chain = Scatter(moves, [inner_pair], y_first)
    feed_chains = [outer_chain, inner_chain]
    cross_mix = receive([outer_chain], cross_mix)
    cross_mix = depart([inner_chain], cross_mix)
    cross_mix = depart([outer_chain], cross_mix)
    cross_mix = advance([inner_chain], cross_mix)
    enc_part, first_grad, mix, sums, query_pair, key_pair = cross_backward(
        ids, cross_queries, cross_keys, cross_mixed, cross_mix, cross_logsum, first_low, first_pre,
        second_grad, mixed, sums, both, cross_query, self_out, cross_key, cross_value, vecs, owned_rows,
    )
    mix, enc_part = receive(feed_chains, mix, enc_part)
    cross_chains = [
        Scatter(moves, [query_pair], x_first),
        Scatter(moves, [key_pair, cross_out_pair], y_first),
    ]
    enc_half = encoder.shape[0]
    enc_there = swap_seq(enc_part[enc_half:], 1)
    enc_rows = enc_out.shape[1]
    mix = depart(cross_chains + feed_chains, mix)
    halfway = HEADS // 4
    one = self_backward(ids, queries, own, other, mixed, mix, logsum, 0, halfway)
    tied = receive(cross_chains, enc_there, outer_chain.got, inner_chain.got, mix, *one)
    enc_there, outer_chain.got, inner_chain.got, mix = tied[:4]
    one = tied[4:]
    enc_back = low(widen(enc_part[:enc_half]) + widen(enc_there))
    enc_sent, mix = tie(enc_back[enc_rows:], mix)
    enc_got = swap_seq(enc_sent, 3)
    rest = jnp.concatenate([c.total() for c in feed_chains], axis=-2)
    rest, mix = tie(rest, mix)
    rest = rest.reshape((-1,) + rest.shape[-2:])
    lines = [[i for i in range(blocks) if i % 2 == side] for side in range(2)]
    rest = lax.psum_scatter(
        rest, "dp", scatter_dimension=0, axis_index_groups=lines, tiled=True
    )[0]
    mix = depart(cross_chains, mix)
    two = self_backward(ids, queries, own, other, mixed, mix, logsum, halfway, HEADS // 2)
    tied = receive(cross_chains, enc_got, *two)
    enc_got, two = tied[0], tied[1:]
    sent = [tie(h[2], *[c.away for c in cross_chains])[0] for h in (one, two)]
    got_one, got_two = [swap_seq(v, 1) for v in sent]
    part, sums, self_query_pair = query_backward(
        ids, tokens, (one[0], two[0]), (one[3], two[3]), sums, first_grad, self_query, owned_rows
    )
    got_one, got_two, part = tie(got_one, got_two, part)
    bias_sums = sums[INNER_B : INNER_B + chunks].reshape(owners, hidden_rows)
    sums = sums[:13].reshape(13, owners, owned_rows).transpose(1, 0, 2).reshape(owners, counts)
    sums = low(jnp.concatenate([sums, bias_sums], axis=1))
    sums = jnp.pad(sums[:, None, :], ((0, 0), (0, 7), (0, width - counts - hidden_rows)))
    sums = sums.reshape(-1, 2, 8, width)
    sums_pair = (
        lax.dynamic_index_in_dim(sums, seq & 1, 1, keepdims=False),
        lax.dynamic_index_in_dim(sums, 1 - (seq & 1), 1, keepdims=False),
    )
    query_chain = Scatter(moves, [self_query_pair, sums_pair], x_first)
    got_one = depart(cross_chains + [query_chain], got_one)
    total, key_pair, value_pair = key_weights(
        ids, tokens, (one[1], two[1]), (got_one, got_two), owned_rows
    )
    key_chains = [Scatter(moves, [key_pair], x_first), Scatter(moves, [value_pair], y_first)]
    total = receive(cross_chains + [query_chain], total)
    cross_last = joined(cross_chains)
    total = depart(key_chains + [query_chain, cross_last], total)
    token_grad = token_backward(total, part, self_key, self_value)
    token_grad = receive(key_chains + [query_chain, cross_last], token_grad)
    token_grad, token_back, key_chains[0].away = send_back(token_grad, key_chains[0].away)
    depart(key_chains + [query_chain, cross_last])
    token_back = receive(key_chains, token_back)
    depart(key_chains)
    totals = [query_chain.total()]
    key_chains[0].got, key_chains[1].got, totals[0] = tie(
        key_chains[0].got, key_chains[1].got, totals[0]
    )
    totals = jnp.concatenate([c.total() for c in key_chains] + totals, axis=-2)
    totals = totals.reshape((-1,) + totals.shape[-2:])
    if totals.shape[0] <= 4:
        keep, gots = line_sends(moves, totals, 1)
        tied = tie(*gots, cross_last.got)
        gots, cross_last.got = tied[:-1], tied[-1]
        tail_held = widen(keep) + sum(widen(g) for g in gots)
    else:
        tail_held = widen(
            lax.psum_scatter(totals, "dp", scatter_dimension=0, axis_index_groups=lines, tiled=True)[0]
        )
    while cross_last.got is not None:
        receive([cross_last])
        if cross_last.order:
            cross_last.ship()

    def cut_rows(held, sizes):
        ends = [sum(sizes[: i + 1]) for i in range(len(sizes))]
        return [held[e - n : e] for e, n in zip(ends, sizes)]

    self_key_grad, self_value_grad, self_query_grad, vec = cut_rows(
        tail_held, [owned_rows, owned_rows, owned_rows, 8]
    )
    cross_held = cross_last.held.reshape(-1, owned_rows, width)
    vec = vec[0]
    prompt_grad, cont_grad = place(token_grad, token_back)
    enc_grad = jnp.where(
        group == 0,
        jnp.stack([enc_back[:enc_rows], enc_got]),
        jnp.stack([enc_got, enc_back[:enc_rows]]),
    )

    rest = widen(rest)
    outer_mat_grad = rest[:hidden_rows]
    inner_mat_grad = jnp.concatenate(
        [rest[hidden_rows + i * owned_rows : hidden_rows + (i + 1) * owned_rows] for i in range(chunks)],
        axis=1,
    )
    vec_out = [vec[i * owned_rows : (i + 1) * owned_rows] for i in range(13)]
    inner_bias_out = vec[counts : counts + hidden_rows]
    return (
        prompt_out,
        cont_out,
        prompt_grad,
        cont_grad,
        enc_grad,
        self_query_grad,
        vec_out[0],
        self_key_grad,
        self_value_grad,
        vec_out[1],
        cross_held[1],
        vec_out[2],
        vec_out[3],
        vec_out[4],
        cross_held[0],
        vec_out[5],
        cross_held[2],
        cross_held[3],
        vec_out[6],
        cross_held[4],
        vec_out[7],
        vec_out[8],
        vec_out[9],
        inner_mat_grad,
        inner_bias_out,
        outer_mat_grad,
        vec_out[10],
        vec_out[11],
        vec_out[12],
    )


def solution(mesh):
    rows_spec = P("dp", "seq", None)
    mat, vec = P(("dp", "seq"), None), P(("dp", "seq"))
    weights = (
        mat,
        vec,
        mat,
        mat,
        vec,
        mat,
        vec,
        vec,
        vec,
        mat,
        vec,
        mat,
        mat,
        vec,
        mat,
        vec,
        vec,
        vec,
        mat,
        vec,
        mat,
        vec,
        vec,
        vec,
    )
    in_specs = (rows_spec, rows_spec, rows_spec, P("dp"), rows_spec, rows_spec) + weights
    out_specs = (rows_spec,) * 5 + weights
    return jax.shard_map(body, mesh=mesh, in_specs=in_specs, out_specs=out_specs, check_vma=False)
```

```python
import jax
import jax.numpy as jnp
from jax import lax
from jax.experimental import pallas as pl
from jax.experimental.pallas import tpu as pltpu
from jax.sharding import PartitionSpec as P

HEADS = 12
VMEM_LIMIT = 60 * 1024 * 1024
NEG = -1e30
FOLD = 6
SELF_FOLD = 3
SELF_BACK_FOLD = 1


def matmul(left, right):
    return jnp.dot(left, right, preferred_element_type=jnp.float32)


def contract_rows(left, right):
    return lax.dot_general(
        left, right, (((0,), (0,)), ((), ())), preferred_element_type=jnp.float32
    )


def times_transpose(left, right):
    return lax.dot_general(
        left, right, (((1,), (1,)), ((), ())), preferred_element_type=jnp.float32
    )


def widen(values):
    return values.astype(jnp.float32)


def low(values):
    return values.astype(jnp.bfloat16)


def normalize(values, gain, shift):
    centred = values - jnp.mean(values, axis=-1, keepdims=True)
    scale = lax.rsqrt(jnp.mean(centred * centred, axis=-1, keepdims=True) + 1e-05)
    return centred * scale * gain + shift


def norm_backward(values, gain, upstream):
    centred = values - jnp.mean(values, axis=-1, keepdims=True)
    scale = lax.rsqrt(jnp.mean(centred * centred, axis=-1, keepdims=True) + 1e-05)
    normed = centred * scale
    scaled = upstream * gain
    result = scale * (
        scaled
        - jnp.mean(scaled, axis=-1, keepdims=True)
        - normed * jnp.mean(scaled * normed, axis=-1, keepdims=True)
    )
    return (
        result,
        jnp.sum(upstream * normed, axis=0, keepdims=True),
        jnp.sum(upstream, axis=0, keepdims=True),
    )


(
    SELF_Q,
    SELF_V,
    SELF_O,
    GAIN_ONE,
    SHIFT_ONE,
    CROSS_Q,
    CROSS_V,
    CROSS_O,
    GAIN_TWO,
    SHIFT_TWO,
    OUTER_B,
    GAIN_THREE,
    SHIFT_THREE,
    INNER_B,
) = range(14)


def pack_vectors(vectors, out_ref, base):
    out_ref[base : base + 8, :] = jnp.zeros((8, out_ref.shape[1]), out_ref.dtype)
    for i, ref in enumerate(vectors):
        at = 128 * (i // 8)
        out_ref[base + i % 8 : base + i % 8 + 1, at : at + ref.shape[1]] = ref[...]


def pack(first, vectors, second, outer, inner, rest):
    rows, width = first[0].shape
    chunks = inner.shape[1] // width
    counts = (len(first), len(vectors), len(second), 1, 1, len(rest))

    def kernel(*refs):
        groups, at = [], 0
        for count in counts:
            groups.append(refs[at : at + count])
            at += count
        outs = refs[at:]
        if rows % 8 == 0:
            for i, ref in enumerate(groups[0]):
                outs[0][i * rows : (i + 1) * rows, :] = ref[...]
            for i, ref in enumerate(groups[2]):
                outs[1][i * rows : (i + 1) * rows, :] = ref[...]
            outs[2][: chunks * rows, :] = groups[3][0][...]
            for i in range(chunks):
                at = (chunks + i) * rows
                outs[2][at : at + rows, :] = groups[4][0][:, i * width : (i + 1) * width]
            for i, ref in enumerate(groups[5]):
                at = (2 * chunks + i) * rows
                outs[2][at : at + rows, :] = ref[...]
        pack_vectors(groups[1], outs[0], len(first) * rows if rows % 8 == 0 else 0)

    shapes = [len(first) * rows + 8, len(second) * rows, (2 * chunks + len(rest)) * rows]
    if rows % 8:
        shapes = [8, 8, 8]
    outs = pl.pallas_call(
        kernel,
        out_shape=[jax.ShapeDtypeStruct((n, width), outer.dtype) for n in shapes],
        name="pack",
    )(*first, *[v[None, :] for v in vectors], *second, outer, inner, *rest)
    if rows % 8 == 0:
        return outs
    inner = [inner[:, i * width : (i + 1) * width] for i in range(chunks)]
    return [
        jnp.concatenate(list(first) + [outs[0]], axis=0),
        jnp.concatenate(second, axis=0),
        jnp.concatenate([outer] + inner + list(rest), axis=0),
    ]


class Call:
    def __init__(self, name, grid):
        self.name, self.grid = name, grid
        self.ins, self.in_specs, self.out_shapes, self.out_specs = [], [], [], []
        self.flops, self.bytes, self.exps = 0, 0, 0
        self.lates = []

    def whole(self, array):
        zeros = (0,) * array.ndim
        self.blocked(array, array.shape, lambda *g: zeros, buffers=1)

    def blocked(self, array, block, index, buffers=2):
        mode = {} if buffers == 2 else {"pipeline_mode": pl.Buffered(buffers)}
        self.ins.append(array)
        self.in_specs.append(pl.BlockSpec(block, index, **mode))
        self.bytes += array.size * array.dtype.itemsize

    def scalars(self, array):
        self.ins.append(array)
        self.in_specs.append(pl.BlockSpec(memory_space=pltpu.SMEM))

    def late(self, array, block=None, index=None):
        self.ins.append(array)
        self.in_specs.append(pl.BlockSpec(memory_space=pl.ANY))
        block = block or array.shape
        self.bytes += array.dtype.itemsize * array.size
        self.lates.append((len(self.ins) - 1, block, index, array.dtype))

    def late_weight(self, weight):
        array, block, index = weight
        self.late(array, block, tuple(i * n for i, n in zip(index, block)))

    def late_copies(self, refs, late_refs):
        count = len(self.lates)
        copies = []
        for i, (place, block, start, _) in enumerate(self.lates):
            source = refs[place]
            if start is not None:
                source = source.at[tuple(pl.ds(a, n) for a, n in zip(start, block))]
            copies.append(pltpu.make_async_copy(source, late_refs[i], late_refs[count].at[i]))
        return copies

    def run_late(self, kernel, scratch=()):
        count = len(self.lates)
        steps = self.grid[0]

        def wrapped(*refs):
            refs, late_refs = refs[: -count - 1], refs[-count - 1 :]
            copies = self.late_copies(refs, late_refs)

            @pl.when(pl.program_id(0) == 0)
            def _():
                for copy in copies:
                    copy.start()

            def fetch():
                for copy in copies:
                    copy.wait()

            refs = list(refs)
            for i, (place, _, _, _) in enumerate(self.lates):
                refs[place] = late_refs[i]
            kernel(fetch, *refs)

        buffers = [pltpu.VMEM(block, dtype) for _, block, _, dtype in self.lates]
        return self.run(
            wrapped, list(scratch) + buffers + [pltpu.SemaphoreType.DMA((count,))]
        )

    def weight(self, weight):
        array, block, index = weight
        self.ins.append(array)
        self.in_specs.append(pl.BlockSpec(block, lambda *g: index, pipeline_mode=pl.Buffered(1)))
        self.bytes += array.shape[-1] ** 2 * 2

    def out(self, shape, dtype, block=None, index=None):
        zeros = (0,) * len(shape)
        self.out_shapes.append(jax.ShapeDtypeStruct(shape, dtype))
        self.out_specs.append(pl.BlockSpec(block or shape, index or (lambda *g: zeros)))
        size = 1
        for n in shape:
            size *= n
        self.bytes += size * jnp.dtype(dtype).itemsize

    def run(self, kernel, scratch=()):
        return pl.pallas_call(
            kernel,
            grid=self.grid,
            in_specs=self.in_specs,
            out_specs=self.out_specs,
            out_shape=self.out_shapes,
            scratch_shapes=list(scratch),
            compiler_params=pltpu.CompilerParams(vmem_limit_bytes=VMEM_LIMIT),
            cost_estimate=pl.CostEstimate(
                flops=int(self.flops), bytes_accessed=int(self.bytes), transcendentals=int(self.exps)
            ),
            name=self.name,
        )(*self.ins)


class Halves:
    def __init__(self, call, count, owners, owned_rows, width, heads=None, index=None):
        self.owned_rows = owned_rows
        self.even = owned_rows % 8 == 0
        if self.even:
            shape, outs = (owners // 2, count, owned_rows, width), 2
            block = (heads or owners // 2, 1 if index else count, owned_rows, width)
        else:
            shape, outs = (count, owners * owned_rows, width), 1
            block = (1 if index else count, 2 * (heads or owners // 2) * owned_rows, width)
        for _ in range(outs):
            if index is None:
                call.out(shape, jnp.bfloat16)
            elif self.even:
                call.out(shape, jnp.bfloat16, block, lambda *g: index(*g) + (0, 0))
            else:
                call.out(shape, jnp.bfloat16, block, lambda *g: index(*g)[::-1] + (0,))
        self.outs = outs

    def store(self, refs, at, value, mine):
        if not self.even:
            refs[0][at] = low(value)
            return
        parts = value.reshape(-1, 2, self.owned_rows, value.shape[-1])
        first, second = low(parts[:, 0]), low(parts[:, 1])
        refs[0][:, at] = jnp.where(mine == 0, first, second)
        refs[1][:, at] = jnp.where(mine == 0, second, first)

    def pair(self, results, mine):
        if self.even:
            return tuple(results)
        whole = results[0]
        parts = whole.reshape(whole.shape[0], -1, 2, self.owned_rows, whole.shape[-1])
        return tuple(
            lax.dynamic_index_in_dim(parts, which, 2, keepdims=False).transpose(1, 0, 2, 3)
            for which in (mine, 1 - mine)
        )


def load(ref):
    value = ref[...]
    return value.reshape(-1, value.shape[-1])


def row(vecs_ref, index):
    return vecs_ref[index : index + 1, :]


def fill_bias(bias_ref, chunk, rows, ids_ref):
    half, block = rows // 2, rows // 4
    key = lax.broadcasted_iota(jnp.int32, (rows, rows), 0)
    query = lax.broadcasted_iota(jnp.int32, (rows, rows), 1)
    key_block = jnp.where(
        lax.rem(key, half) < block, ids_ref[2 * chunk], ids_ref[2 * chunk + 1]
    )
    query_block = jnp.where(lax.rem(query, half) < block, ids_ref[0], ids_ref[1])
    key_place = key_block * block + lax.rem(key, block)
    query_place = query_block * block + lax.rem(query, block)
    causal = key_place <= query_place
    prompt_key = key < half
    prompt_query = query < half
    allowed = (prompt_key & prompt_query & causal) | (
        jnp.logical_not(prompt_query)
        & ((prompt_key & (key_place < ids_ref[4])) | (jnp.logical_not(prompt_key) & causal))
    )
    bias_ref[chunk] = jnp.where(allowed, 0.0, NEG)


def lane_masks(values):
    lane = lax.broadcasted_iota(jnp.int32, values.shape, 1)
    zero = jnp.zeros_like(values)
    first = lane < values.shape[1] // 2
    return jnp.where(first, values, zero), jnp.where(first, zero, values)


def key_parts(key_rows, masked):
    if not masked:
        return [(0, key_rows, 0)]
    half = key_rows // 2
    return [(0, half, 0), (half, key_rows, half)]


def widened(values, first, rows, fill):
    if first == 0:
        return values
    blank = jnp.full(values.shape[:-1] + (first,), fill, values.dtype)
    return jnp.concatenate([blank, values], axis=-1)


def attend_pair(queries, keys, values, bias_ref, log_ref):
    rows = queries.shape[0]
    queries = lane_masks(queries)
    parts = [
        (chunk,) + part
        for part in key_parts(keys[0].shape[0], bias_ref is not None)
        for chunk in range(len(keys))
    ]
    outs = []
    for head in range(2):
        scores = []
        for chunk, low_key, high_key, first in parts:
            part = times_transpose(keys[chunk][low_key:high_key], queries[head][first:])
            if bias_ref is not None:
                part = part + bias_ref[chunk, low_key:high_key, first:]
            scores.append(part)
        top = None
        for part, (_, _, _, first) in zip(scores, parts):
            most = widened(part.max(axis=0, keepdims=True), first, rows, NEG)
            top = most if top is None else jnp.maximum(top, most)
        total, mixed = 0.0, 0.0
        for part, (chunk, low_key, high_key, first) in zip(scores, parts):
            weights = jnp.exp(part - top[:, first:])
            total = total + widened(weights.sum(axis=0, keepdims=True), first, rows, 0.0)
            out = contract_rows(values[chunk][low_key:high_key], low(weights))
            mixed = mixed + widened(out, first, rows, 0.0)
        outs.append(mixed * (1.0 / total))
        log_ref[0, head : head + 1, :] = top + jnp.log(total)
    lane = lax.broadcasted_iota(jnp.int32, outs[0].shape, 0)
    return low(jnp.where(lane < outs[0].shape[0] // 2, outs[0], outs[1]).T)


def attend_pair_backward(queries, keys, values, bias_ref, log_ref, mixed, upstream):
    rows = queries.shape[0]
    queries = lane_masks(queries)
    ups = lane_masks(upstream)
    product = widen(mixed) * widen(upstream)
    high = low(product)
    rest = low(product - widen(high))
    pair = product.shape[1]
    lane = lax.broadcasted_iota(jnp.int32, (8, pair), 1)
    line = lax.broadcasted_iota(jnp.int32, (8, pair), 0)
    pick = jnp.where(
        ((lane < pair // 2) & (line == 0)) | ((lane >= pair // 2) & (line == 1)), 1.0, 0.0
    ).astype(jnp.bfloat16)
    delta = times_transpose(pick, high) + times_transpose(pick, rest)
    dq = 0.0
    parts = key_parts(keys[0].shape[0], bias_ref is not None)
    dk = [[0.0] * len(parts) for _ in keys]
    dv = [[0.0] * len(parts) for _ in keys]
    for head in range(2):
        for chunk in range(len(keys)):
            masked_keys = lane_masks(keys[chunk])[head]
            for i, (low_key, high_key, first) in enumerate(parts):
                part = times_transpose(keys[chunk][low_key:high_key], queries[head][first:])
                if bias_ref is not None:
                    part = part + bias_ref[chunk, low_key:high_key, first:]
                probs = jnp.exp(part - log_ref[0, head : head + 1, first:])
                up = ups[head][first:]
                prob_grad = times_transpose(values[chunk][low_key:high_key], up)
                score_grad = low(probs * (prob_grad - delta[head : head + 1, first:]))
                dv[chunk][i] = dv[chunk][i] + matmul(low(probs), up)
                dk[chunk][i] = dk[chunk][i] + matmul(score_grad, queries[head][first:])
                out = contract_rows(masked_keys[low_key:high_key], score_grad)
                dq = dq + widened(out, first, rows, 0.0)
    join = [
        [v[0] if len(v) == 1 else jnp.concatenate(v, axis=0) for v in side] for side in (dk, dv)
    ]
    return low(dq.T), join[0], join[1]


def project_kernel(scaled, x_ref, *refs):
    vecs_ref = refs[-3] if scaled else refs[-2]
    values = x_ref[...]
    if scaled:
        wq_ref, wk_ref, wv_ref = refs[:3]
        q_ref, kv_ref = refs[-2:]
        q_ref[...] = low((matmul(values, load(wq_ref)) + row(vecs_ref, SELF_Q)) * 0.125)
        bias = row(vecs_ref, SELF_V)
    else:
        wk_ref, wv_ref = refs[:2]
        kv_ref = refs[-1]
        bias = row(vecs_ref, CROSS_V)
    kv_ref[0] = low(matmul(values, load(wk_ref)))
    kv_ref[1] = low(matmul(values, load(wv_ref)) + bias)


def project(tokens, weights, vecs):
    rows, width = tokens.shape
    scaled = len(weights) == 3
    call = Call("project", (1,))
    call.whole(tokens)
    for weight in weights:
        call.weight(weight)
    call.whole(vecs)
    if scaled:
        call.out((rows, width), jnp.bfloat16)
    call.out((2, rows, width), jnp.bfloat16)
    call.flops = 2 * len(weights) * rows * width * width

    def kernel(*refs):
        project_kernel(scaled, *refs)

    return call.run(kernel)


def lanes_of(width):
    lanes = 2 * (width // HEADS)

    def at(h):
        return pl.ds(pl.multiple_of(h * lanes, lanes), lanes)

    return lanes, at


def self_attend(ids, queries, own, other):
    rows, width = queries.shape
    pairs, fold = HEADS // 2, SELF_FOLD
    lanes, _ = lanes_of(width)
    call = Call("self_attend", (pairs // fold,))
    call.scalars(ids)
    call.blocked(queries, (rows, fold * lanes), lambda h: (0, h))
    for array in (own, other):
        call.blocked(array, (2, rows, fold * lanes), lambda h: (0, 0, h))
    call.out((rows, width), jnp.bfloat16, (rows, fold * lanes), lambda h: (0, h))
    call.out((pairs, 2, rows), jnp.float32, (fold, 2, rows), lambda h: (h, 0, 0))
    call.flops = 16 * rows * rows * width
    call.exps = 2 * rows * rows * HEADS

    def kernel(ids_ref, q_ref, own_ref, other_ref, mixed_ref, log_ref, bias_ref):
        @pl.when(pl.program_id(0) == 0)
        def _():
            for chunk in range(2):
                fill_bias(bias_ref, chunk, rows, ids_ref)

        for i in range(fold):
            part = slice(i * lanes, (i + 1) * lanes)
            keys, values = [(own_ref[n, :, part], other_ref[n, :, part]) for n in range(2)]
            mixed_ref[:, part] = attend_pair(
                q_ref[:, part], keys, values, bias_ref, log_ref.at[pl.ds(i, 1)]
            )

    return call.run(kernel, [pltpu.VMEM((2, rows, rows), jnp.float32)])


def self_finish(tokens, mixed, out_weight, query_weight, vecs):
    rows, width = tokens.shape
    call = Call("self_finish", (1,))
    call.whole(tokens)
    call.whole(mixed)
    call.weight(out_weight)
    call.weight(query_weight)
    call.whole(vecs)
    call.out((rows, width), jnp.float32)
    call.out((rows, width), jnp.bfloat16)
    call.out((rows, width), jnp.bfloat16)
    call.flops = 4 * rows * width * width

    def kernel(x_ref, mixed_ref, wo_ref, wq_ref, vecs_ref, pre_ref, low_ref, next_ref):
        pre = widen(x_ref[...]) + matmul(mixed_ref[...], load(wo_ref)) + row(vecs_ref, SELF_O)
        pre_ref[...] = pre
        first = low(normalize(pre, row(vecs_ref, GAIN_ONE), row(vecs_ref, SHIFT_ONE)))
        low_ref[...] = first
        next_ref[...] = low((matmul(first, load(wq_ref)) + row(vecs_ref, CROSS_Q)) * 0.125)

    return call.run(kernel)


def cross_attend(queries, keys, first_pre, out_weight, vecs):
    rows, width = queries.shape
    key_rows = keys.shape[1]
    pairs, fold = HEADS // 2, FOLD
    lanes, at = lanes_of(width)
    call = Call("cross_attend", (pairs // fold,))
    call.blocked(queries, (rows, fold * lanes), lambda h: (0, h))
    call.blocked(keys, (2, key_rows, fold * lanes), lambda h: (0, 0, h))
    call.late(first_pre)
    call.late_weight(out_weight)
    call.whole(vecs)
    call.out((rows, width), jnp.bfloat16)
    call.out((pairs, 2, rows), jnp.float32, (fold, 2, rows), lambda h: (h, 0, 0))
    call.out((rows, width), jnp.float32)
    call.out((rows, width), jnp.bfloat16)
    call.flops = 8 * rows * key_rows * width + 2 * rows * width * width
    call.exps = 2 * rows * key_rows * HEADS

    def kernel(
        fetch, q_ref, keys_ref, first_ref, wo_ref, vecs_ref, mixed_ref, log_ref, pre_ref, low_ref
    ):
        step = pl.program_id(0)
        for i in range(fold):
            part = slice(i * lanes, (i + 1) * lanes)
            mixed_ref[:, at(step * fold + i)] = attend_pair(
                q_ref[:, part],
                (keys_ref[0, :, part],),
                (keys_ref[1, :, part],),
                None,
                log_ref.at[pl.ds(i, 1)],
            )

        @pl.when(step == pairs // fold - 1)
        def _():
            fetch()
            first = normalize(first_ref[...], row(vecs_ref, GAIN_ONE), row(vecs_ref, SHIFT_ONE))
            pre = first + matmul(mixed_ref[...], load(wo_ref)) + row(vecs_ref, CROSS_O)
            pre_ref[...] = pre
            low_ref[...] = low(normalize(pre, row(vecs_ref, GAIN_TWO), row(vecs_ref, SHIFT_TWO)))

    return call.run_late(kernel)


def feed_blocks(call, feed, width, chunks, owned_rows):
    owners = feed.shape[0]

    def at(i):
        return jnp.minimum(i, chunks - 1)

    hidden_rows = chunks * owned_rows
    if owned_rows % 8 == 0:
        call.blocked(feed, (owners, owned_rows, width), lambda i: (0, chunks + at(i), 0))
        call.blocked(feed, (owners // chunks, hidden_rows, width), lambda i: (at(i), 0, 0))
    else:
        parts = [
            feed[:, hidden_rows + i * owned_rows : hidden_rows + (i + 1) * owned_rows]
            for i in range(chunks)
        ]
        parts = [p.reshape(-1, width) for p in parts]
        call.blocked(jnp.concatenate(parts, axis=1), (width, width), lambda i: (0, at(i)))
        call.blocked(feed[:, :hidden_rows].reshape(-1, width), (width, width), lambda i: (at(i), 0))


def feed_forward(ids, second_pre, second_low, upstream, feed, vecs, chunks, owned_rows):
    rows, width = second_low.shape
    hidden = chunks * width
    owners = width // owned_rows
    call = Call("feed_forward", (2 * chunks,))
    call.scalars(ids)
    call.whole(second_pre)
    call.whole(second_low)
    call.late(upstream)
    feed_blocks(call, feed, width, chunks, owned_rows)
    call.whole(vecs)
    call.out(
        (rows, hidden), jnp.bfloat16, (rows, width), lambda i: (0, jnp.minimum(i, chunks - 1))
    )
    call.out((rows, width), jnp.bfloat16)
    call.out((rows, width), jnp.float32)
    call.out((rows, width), jnp.bfloat16)
    call.out((24, width), jnp.float32)
    half = Halves(
        call,
        1,
        owners,
        chunks * owned_rows,
        width,
        owners // 2 // chunks,
        lambda i: (jnp.maximum(i - chunks, 0), 0),
    )
    call.flops = 6 * rows * hidden * width
    call.exps = 2 * rows * hidden

    def kernel(
        fetch, ids_ref, pre_ref, low_ref, up_ref, inner_ref, outer_ref, vecs_ref, slope_ref, out_ref,
        grad_ref, third_low_ref, sums_ref, *rest,
    ):
        grads, (active_ref, third_ref) = rest[:-2], rest[-2:]
        step = pl.program_id(0)

        @pl.when(step == 0)
        def _():
            second = normalize(pre_ref[...], row(vecs_ref, GAIN_TWO), row(vecs_ref, SHIFT_TWO))
            third_ref[...] = second + row(vecs_ref, OUTER_B)

        @pl.when(step < chunks)
        def _():
            inner = matmul(low_ref[...], load(inner_ref)) + vecs_ref[pl.ds(INNER_B + step, 1), :]
            bell = 0.5 * (1.0 + lax.erf(inner * 0.7071067811865476))
            active = low(inner * bell)
            active_ref[step] = active
            density = jnp.exp(-0.5 * inner * inner) * 0.3989422804014327
            slope_ref[...] = low(bell + inner * density)
            third_ref[...] += matmul(active, load(outer_ref))

        @pl.when(step == chunks - 1)
        def _():
            fetch()
            third = third_ref[...]
            gain = row(vecs_ref, GAIN_THREE)
            out_ref[...] = low(normalize(third, gain, row(vecs_ref, SHIFT_THREE)))
            grad, gain_sum, shift_sum = norm_backward(third, gain, widen(up_ref[...]))
            grad_ref[...] = grad
            third_low_ref[...] = low(grad)
            sums_ref[...] = jnp.zeros_like(sums_ref)
            sums_ref[GAIN_THREE : GAIN_THREE + 1, :] = gain_sum
            sums_ref[SHIFT_THREE : SHIFT_THREE + 1, :] = shift_sum
            sums_ref[OUTER_B : OUTER_B + 1, :] = jnp.sum(widen(low(grad)), axis=0, keepdims=True)

        @pl.when(step >= chunks)
        def _():
            active = active_ref[jnp.maximum(step - chunks, 0)]
            half.store(grads, 0, contract_rows(active, third_low_ref[...]), ids_ref[5])

    results = call.run_late(
        kernel,
        [pltpu.VMEM((chunks, rows, width), jnp.bfloat16), pltpu.VMEM((rows, width), jnp.float32)],
    )
    return tuple(results[:5]) + (half.pair(results[5:], ids[5]),)


def inner_backward(
    ids, third_grad, third_low, sums, second_pre, second_low, slope, feed, out_weight, vecs,
    chunks, owned_rows,
):
    rows, width = second_low.shape
    owners = width // owned_rows
    call = Call("inner_backward", (chunks,))
    call.scalars(ids)
    for array in (third_grad, third_low, sums):
        call.whole(array)
    call.late(second_pre)
    call.whole(second_low)
    call.blocked(slope, (rows, width), lambda i: (0, i))
    feed_blocks(call, feed, width, chunks, owned_rows)
    call.late_weight(out_weight)
    call.whole(vecs)
    call.out((rows, width), jnp.float32)
    call.out((rows, width), jnp.bfloat16)
    call.out((24, width), jnp.float32)
    inner_half = Halves(call, chunks, owners, owned_rows, width, owners // 2, lambda i: (0, i))
    call.flops = 6 * rows * chunks * width * width + 4 * rows * width * width

    def kernel(
        fetch, ids_ref, third_ref, third_low_ref, sums_in_ref, second_ref, low_ref, slope_ref, inner_ref, outer_ref,
        wo_ref, vecs_ref, second_grad_ref, mix_ref, sums_ref, *rest,
    ):
        inner_grads, total_ref = rest[:-1], rest[-1]
        step = pl.program_id(0)
        mine = ids_ref[5]

        @pl.when(step == 0)
        def _():
            total_ref[...] = third_ref[...]
            sums_ref[...] = sums_in_ref[...]

        inner_low = low(times_transpose(third_low_ref[...], load(outer_ref)) * widen(slope_ref[...]))
        total_ref[...] += times_transpose(inner_low, load(inner_ref))
        inner_half.store(inner_grads, 0, contract_rows(low_ref[...], inner_low), mine)
        sums_ref[pl.ds(INNER_B + step, 1), :] = jnp.sum(widen(inner_low), axis=0, keepdims=True)

        @pl.when(step == chunks - 1)
        def _():
            fetch()
            grad, gain_sum, shift_sum = norm_backward(
                second_ref[...], row(vecs_ref, GAIN_TWO), total_ref[...]
            )
            second_grad_ref[...] = grad
            cross_low = low(grad)
            sums_ref[GAIN_TWO : GAIN_TWO + 1, :] = gain_sum
            sums_ref[SHIFT_TWO : SHIFT_TWO + 1, :] = shift_sum
            sums_ref[CROSS_O : CROSS_O + 1, :] = jnp.sum(widen(cross_low), axis=0, keepdims=True)
            mix_ref[...] = low(times_transpose(cross_low, load(wo_ref)))

    results = call.run_late(kernel, [pltpu.VMEM((rows, width), jnp.float32)])
    return tuple(results[:3]) + (inner_half.pair(results[3:], ids[5]),)


def cross_backward(
    ids, queries, keys, mixed, upstream, logsum, first_low, first_pre, second_grad, self_mixed, sums,
    encoder, query_weight, out_weight, key_weight, value_weight, vecs, owned_rows,
):
    rows, width = queries.shape
    key_rows = keys.shape[1]
    pairs, fold = HEADS // 2, FOLD
    lanes, at = lanes_of(width)
    call = Call("cross_backward", (pairs // fold,))
    call.scalars(ids)
    for array in (queries, mixed, upstream):
        call.blocked(array, (rows, fold * lanes), lambda h: (0, h))
    call.blocked(logsum, (fold, 2, rows), lambda h: (h, 0, 0))
    call.blocked(keys, (2, key_rows, fold * lanes), lambda h: (0, 0, h))
    for array in (first_low, first_pre, second_grad, self_mixed, mixed):
        call.late(array)
    call.whole(sums)
    call.late_weight(query_weight)
    call.late_weight(out_weight)
    call.late(encoder)
    call.late_weight(key_weight)
    call.late_weight(value_weight)
    call.whole(vecs)
    call.out((key_rows, width), jnp.bfloat16)
    call.out((rows, width), jnp.float32)
    call.out((rows, width), jnp.bfloat16)
    call.out((24, width), jnp.float32)
    halves = [Halves(call, n, width // owned_rows, owned_rows, width) for n in (2, 3)]
    outs = halves[0].outs
    call.flops = 20 * rows * key_rows * width + 8 * (rows + key_rows) * width * width
    call.exps = 2 * rows * key_rows * HEADS

    def kernel(
        fetch, ids_ref, q_ref, mixed_ref, up_ref, log_ref, keys_ref, low_ref, pre_ref, grad_ref,
        self_mixed_ref, all_mixed_ref, sums_in_ref, wq_ref, wo_ref, enc_ref, wk_ref, wv_ref, vecs_ref, enc_back_ref, first_ref, mix_ref,
        sums_ref, *rest,
    ):
        step = pl.program_id(0)
        weights_refs, (dq_ref, dkv_ref) = rest[:-2], rest[-2:]

        @pl.when(step == 0)
        def _():
            sums_ref[...] = sums_in_ref[...]

        for i in range(fold):
            part = slice(i * lanes, (i + 1) * lanes)
            dq, dk, dv = attend_pair_backward(
                q_ref[:, part],
                (keys_ref[0, :, part],),
                (keys_ref[1, :, part],),
                None,
                log_ref.at[pl.ds(i, 1)],
                mixed_ref[:, part],
                up_ref[:, part],
            )
            place = at(step * fold + i)
            dq_ref[:, place] = dq
            dkv_ref[0, :, place] = low(dk[0])
            dkv_ref[1, :, place] = low(dv[0])
            sums_ref[CROSS_V : CROSS_V + 1, place] = jnp.sum(dv[0], axis=0, keepdims=True)

        @pl.when(step == pairs // fold - 1)
        def _():
            fetch()
            query_low = dq_ref[...]
            halves[0].store(weights_refs[:outs], 0, contract_rows(low_ref[...], query_low) * 0.125, ids_ref[5])
            for i in range(2):
                value = contract_rows(enc_ref[...], dkv_ref[i])
                halves[1].store(weights_refs[outs:], i, value, ids_ref[5])
            cross_low = low(grad_ref[...])
            value = contract_rows(all_mixed_ref[...], cross_low)
            halves[1].store(weights_refs[outs:], 2, value, ids_ref[5])
            enc_back_ref[...] = low(
                times_transpose(dkv_ref[0], load(wk_ref)) + times_transpose(dkv_ref[1], load(wv_ref))
            )
            total = grad_ref[...] + times_transpose(query_low, load(wq_ref)) * 0.125
            grad, gain_sum, shift_sum = norm_backward(pre_ref[...], row(vecs_ref, GAIN_ONE), total)
            first_ref[...] = grad
            self_low = low(grad)
            mix_ref[...] = low(times_transpose(self_low, load(wo_ref)))
            halves[0].store(weights_refs[:outs], 1, contract_rows(self_mixed_ref[...], self_low), ids_ref[5])
            sums_ref[GAIN_ONE : GAIN_ONE + 1, :] = gain_sum
            sums_ref[SHIFT_ONE : SHIFT_ONE + 1, :] = shift_sum
            sums_ref[SELF_O : SELF_O + 1, :] = jnp.sum(widen(self_low), axis=0, keepdims=True)
            sums_ref[CROSS_Q : CROSS_Q + 1, :] = jnp.sum(widen(query_low), axis=0, keepdims=True) * 0.125

    results = call.run_late(
        kernel,
        [pltpu.VMEM((rows, width), jnp.bfloat16), pltpu.VMEM((2, key_rows, width), jnp.bfloat16)],
    )
    return tuple(results[:4]) + (
        halves[0].pair(results[4 : 4 + outs], ids[5]),
        halves[1].pair(results[4 + outs :], ids[5]),
    )


def self_backward(ids, queries, own, other, mixed, upstream, logsum, first, last):
    rows, width = queries.shape
    lanes, _ = lanes_of(width)
    count, fold = last - first, SELF_BACK_FOLD
    start = first // fold
    call = Call("self_backward", (count // fold,))
    call.scalars(ids)
    for array in (queries, mixed, upstream):
        call.blocked(array, (rows, fold * lanes), lambda h: (0, start + h))
    call.blocked(logsum, (fold, 2, rows), lambda h: (start + h, 0, 0))
    for array in (own, other):
        call.blocked(array, (2, rows, fold * lanes), lambda h: (0, 0, start + h))
    call.out((rows, count * lanes), jnp.bfloat16, (rows, fold * lanes), lambda h: (0, h))
    for _ in range(2):
        call.out(
            (2, rows, count * lanes), jnp.bfloat16, (2, rows, fold * lanes), lambda h: (0, 0, h)
        )
    call.out((8, count * lanes), jnp.float32, (8, fold * lanes), lambda h: (0, h))
    call.flops = 40 * rows * rows * count * lanes
    call.exps = 4 * rows * rows * count

    def kernel(
        ids_ref, q_ref, mixed_ref, up_ref, log_ref, own_ref, other_ref, dq_ref, own_out_ref,
        other_out_ref, sums_ref, bias_ref,
    ):
        @pl.when(pl.program_id(0) == 0)
        def _():
            for chunk in range(2):
                fill_bias(bias_ref, chunk, rows, ids_ref)

        for i in range(fold):
            part = slice(i * lanes, (i + 1) * lanes)
            keys, values = [(own_ref[n, :, part], other_ref[n, :, part]) for n in range(2)]
            dq, dk, dv = attend_pair_backward(
                q_ref[:, part],
                keys,
                values,
                bias_ref,
                log_ref.at[pl.ds(i, 1)],
                mixed_ref[:, part],
                up_ref[:, part],
            )
            dq_ref[:, part] = dq
            for chunk, out in enumerate((own_out_ref, other_out_ref)):
                out[0, :, part] = low(dk[chunk])
                out[1, :, part] = low(dv[chunk])
            sums_ref[0:1, part] = sum(jnp.sum(v, axis=0, keepdims=True) for v in dv)
            sums_ref[1:2, part] = jnp.sum(widen(dq), axis=0, keepdims=True) * 0.125

    return call.run(kernel, [pltpu.VMEM((2, rows, rows), jnp.float32)])


def query_backward(ids, tokens, query_low, half_sums, sums, first_grad, query_weight, owned_rows):
    rows, width = tokens.shape
    call = Call("query_backward", (1,))
    call.scalars(ids)
    for array in (tokens, first_grad, sums) + tuple(query_low) + tuple(half_sums):
        call.whole(array)
    call.weight(query_weight)
    call.out((rows, width), jnp.float32)
    call.out((24, width), jnp.float32)
    half = Halves(call, 1, width // owned_rows, owned_rows, width)
    call.flops = 4 * rows * width * width

    def kernel(
        ids_ref, x_ref, grad_ref, sums_in_ref, first_ref, second_ref, first_sums_ref, second_sums_ref,
        wq_ref, part_ref, sums_ref, *weights_refs,
    ):
        sums_ref[...] = sums_in_ref[...]
        cut = first_ref.shape[1]
        for lanes, ref in ((slice(0, cut), first_sums_ref), (slice(cut, width), second_sums_ref)):
            sums_ref[SELF_V : SELF_V + 1, lanes] = ref[0:1, :]
            sums_ref[SELF_Q : SELF_Q + 1, lanes] = ref[1:2, :]
        query = jnp.concatenate([first_ref[...], second_ref[...]], axis=1)
        half.store(weights_refs, 0, contract_rows(x_ref[...], query) * 0.125, ids_ref[5])
        part_ref[...] = grad_ref[...] + times_transpose(query, load(wq_ref)) * 0.125

    results = call.run(kernel)
    return results[0], results[1], half.pair(results[2:], ids[5])


def key_weights(ids, tokens, mine, got, owned_rows):
    rows, width = tokens.shape
    call = Call("key_weights", (1,))
    call.scalars(ids)
    for array in (tokens,) + tuple(mine) + tuple(got):
        call.whole(array)
    call.out((2, rows, width), jnp.bfloat16)
    halves = [Halves(call, 1, width // owned_rows, owned_rows, width) for _ in range(2)]
    outs = halves[0].outs
    call.flops = 4 * rows * width * width

    def kernel(ids_ref, x_ref, mine_a, mine_b, got_a, got_b, total_ref, *weights_refs):
        values = x_ref[...]
        for i in range(2):
            total = low(
                jnp.concatenate(
                    [widen(m[i]) + widen(g[i]) for m, g in ((mine_a, got_a), (mine_b, got_b))], axis=1
                )
            )
            total_ref[i] = total
            refs = weights_refs[i * outs : (i + 1) * outs]
            halves[i].store(refs, 0, contract_rows(values, total), ids_ref[5])

    results = call.run(kernel)
    return (results[0],) + tuple(
        halves[i].pair(results[1 + i * outs : 1 + (i + 1) * outs], ids[5]) for i in range(2)
    )


def token_backward(total, part, key_weight, value_weight):
    rows, width = part.shape
    call = Call("token_backward", (1,))
    call.whole(total)
    call.whole(part)
    call.weight(key_weight)
    call.weight(value_weight)
    call.out((rows, width), jnp.bfloat16)
    call.flops = 4 * rows * width * width

    def kernel(total_ref, part_ref, wk_ref, wv_ref, out_ref):
        out_ref[...] = low(
            part_ref[...]
            + times_transpose(total_ref[0], load(wk_ref))
            + times_transpose(total_ref[1], load(wv_ref))
        )

    return call.run(kernel)[0]


def flip(size, bit):
    return [(i, i ^ bit) for i in range(size)]


def swap_seq(values, bits):
    return lax.ppermute(values, "seq", flip(lax.axis_size("seq"), bits))


def tie(*values):
    return lax.optimization_barrier(values)


def bit_order(dp_size, seq_size):
    return [("dp", b) for b in range(dp_size.bit_length() - 1)][::-1] + [
        ("seq", b) for b in range(seq_size.bit_length() - 1)
    ][::-1]


class Moves:
    def __init__(self):
        self.spots = {name: lax.axis_index(name) for name in ("dp", "seq")}
        self.sizes = {name: lax.axis_size(name) for name in ("dp", "seq")}
        self.canonical = bit_order(self.sizes["dp"], self.sizes["seq"])

    def mine(self, step):
        return (self.spots[step[0]] >> step[1]) & 1

    def send(self, values, step):
        name, bit = step
        flat = values.reshape(-1, values.shape[-1])
        return lax.ppermute(flat, name, flip(self.sizes[name], 1 << bit)).reshape(values.shape)


def split_sum(keep, got, at, mine):
    def side(which):
        first, second = [
            lax.dynamic_index_in_dim(v, which, at, keepdims=False) for v in (keep, got)
        ]
        return low(widen(first) + widen(second))

    return side(mine), side(1 - mine)


class Scatter:
    def __init__(self, moves, pairs, order):
        self.moves = moves
        self.dims = [step for step in moves.canonical if step != order[0]]
        self.order = list(order)
        pieces = (2,) * len(self.dims)

        def join(arrays):
            arrays = [a.reshape(pieces + (-1, a.shape[-1])) for a in arrays]
            return arrays[0] if len(arrays) == 1 else jnp.concatenate(arrays, axis=-2)

        self.keep = join([k for k, _ in pairs])
        self.away = join([a for _, a in pairs])
        self.got = None

    def ship(self):
        self.got = self.moves.send(self.away, self.order.pop(0))
        self.away = None

    def take(self):
        got, self.got = self.got, None
        if self.order:
            step = self.order[0]
            at = self.dims.index(step)
            self.keep, self.away = split_sum(self.keep, got, at, self.moves.mine(step))
            self.dims.pop(at)
        else:
            self.held = widen(self.keep) + widen(got)

    def total(self):
        return low(widen(self.keep) + widen(self.got))


def joined(chains):
    first = chains[0]
    chain = object.__new__(Scatter)
    chain.moves, chain.dims, chain.order, chain.got = first.moves, first.dims, first.order, None
    chain.keep = jnp.concatenate([c.keep for c in chains], axis=-2)
    chain.away = jnp.concatenate([c.away for c in chains], axis=-2)
    return chain


def receive(chains, *values):
    tied = tie(*[c.got for c in chains], *values)
    for chain, got in zip(chains, tied):
        chain.got = got
        chain.take()
    values = tied[len(chains) :]
    return values[0] if len(values) == 1 else values


def depart(chains, *values):
    tied = tie(*[c.away for c in chains], *values)
    for chain, away in zip(chains, tied):
        chain.away = away
        chain.ship()
    values = tied[len(chains) :]
    return values[0] if len(values) == 1 else values


def advance(chains, *values):
    values = receive(chains, *values)
    return depart(chains, *(values if isinstance(values, (list, tuple)) else (values,)))


def line_sends(moves, totals, first):
    count = totals.shape[0]
    spot = moves.spots["dp"] >> first
    keep = lax.dynamic_index_in_dim(totals, spot, 0, keepdims=False)
    away = [
        lax.dynamic_index_in_dim(totals, spot ^ i, 0, keepdims=False) for i in range(1, count)
    ]
    away = tie(*away)
    size = moves.sizes["dp"]
    return keep, [lax.ppermute(v, "dp", flip(size, i << first)) for i, v in enumerate(away, 1)]


class Gather:
    def __init__(self, moves, held, order, dims=()):
        self.moves, self.held, self.order, self.dims = moves, held, list(order), list(dims)

    def ship(self):
        self.got = self.moves.send(self.held, self.order[0])

    def take(self):
        step = self.order.pop(0)
        mine = self.moves.mine(step)
        first = jnp.where(mine == 0, self.held, self.got)
        second = jnp.where(mine == 0, self.got, self.held)
        self.held = jnp.stack([first, second], axis=0)
        self.dims.insert(0, step)

    def part(self, first, last, order):
        return Gather(self.moves, self.held[..., first:last, :], order, self.dims)

    def result(self):
        order = [self.dims.index(step) for step in self.moves.canonical]
        count = len(order)
        held = self.held.transpose(order + [count, count + 1])
        return held.reshape((-1,) + held.shape[-2:])


def pump(taking, shipping, *values):
    tied = tie(*[g.got for g in taking], *values)
    for gather, got in zip(taking, tied):
        gather.got = got
        gather.take()
    tied = tie(*[g.held for g in shipping], *tied[len(taking) :])
    for gather, held in zip(shipping, tied):
        gather.held = held
        gather.ship()
    values = tied[len(shipping) :]
    return values[0] if len(values) == 1 else values


def body(
    prompt_in,
    cont_in,
    enc_out,
    prefix,
    prompt_cot,
    cont_cot,
    self_query,
    self_qbias,
    self_key,
    self_value,
    self_vbias,
    self_out,
    self_obias,
    gain_one,
    shift_one,
    cross_query,
    cross_qbias,
    cross_key,
    cross_value,
    cross_vbias,
    cross_out,
    cross_obias,
    gain_two,
    shift_two,
    inner_mat,
    inner_bias,
    outer_mat,
    outer_bias,
    gain_three,
    shift_three,
):
    seq = lax.axis_index("seq")
    parts, blocks = lax.axis_size("seq"), lax.axis_size("dp")
    rows = prompt_in.shape[1]
    width = prompt_in.shape[2]
    owned_rows = self_query.shape[0]
    group = seq // 2
    ids = jnp.stack([seq, 3 - seq, seq ^ 1, 3 - (seq ^ 1), prefix[group], seq & 1]).astype(jnp.int32)

    def pick(array, index):
        return lax.dynamic_index_in_dim(array, index, 0, keepdims=False)

    vectors = [
        self_qbias,
        self_vbias,
        self_obias,
        gain_one,
        shift_one,
        cross_qbias,
        cross_vbias,
        cross_obias,
        gain_two,
        shift_two,
        outer_bias,
        gain_three,
        shift_three,
    ]
    hidden_rows = outer_mat.shape[0]
    chunks = hidden_rows // owned_rows
    first_part, second_part, feed = pack(
        [self_query, self_key, self_value],
        vectors + [inner_bias],
        [self_out, cross_query],
        outer_mat,
        inner_mat,
        [cross_key, cross_value, cross_out],
    )
    moves = Moves()
    bits = moves.canonical
    dp_bits, hi, lo = bits[:-2], bits[-2], bits[-1]
    line, near = dp_bits[:-1], dp_bits[-1]
    cut = 2 * owned_rows
    one = Gather(moves, first_part, line)
    one.ship()
    prompt_got = swap_seq(pick(prompt_in, 1 - group), 3)
    sent = jnp.concatenate([pick(v, 1 - group) for v in (cont_in, enc_out)], axis=0)
    feed = lax.all_gather(feed, ("dp", "seq"), axis=0, tiled=False)
    prompt_got, sent, second_part = pump([one], [one], prompt_got, sent, second_part)
    two = Gather(moves, second_part, line)
    got = swap_seq(sent, 3)
    while len(one.order) > 1:
        pump([one], [one])
    got = pump([one], [], got)
    one_parts = [
        one.part(0, cut, [near, hi, lo]),
        one.part(cut, first_part.shape[0], [hi, near, lo]),
    ]
    got = pump([], one_parts + [two], got)
    got = pump(one_parts + [two], one_parts + [two], got)
    while len(two.order) > 1:
        got = pump([two], [two], got)
    got = pump(one_parts + [two], one_parts, got)
    two_parts = [
        two.part(0, owned_rows, [near, hi, lo]),
        two.part(owned_rows, second_part.shape[0], [hi, near, lo]),
    ]
    got = pump(one_parts, two_parts, got)

    tokens = jnp.concatenate(
        [pick(prompt_in, group), prompt_got, pick(cont_in, group), got[:rows]], axis=0
    )
    encoder = jnp.concatenate([pick(enc_out, group), got[rows:]], axis=0)
    enc_other = swap_seq(encoder, 1)

    def square(array, index):
        if owned_rows % 8 == 0:
            return array, (array.shape[0], owned_rows, width), (0, index, 0)
        part = array[:, index * owned_rows : (index + 1) * owned_rows].reshape(-1, width)
        return part, part.shape, (0, 0)

    front, back = [g.result() for g in one_parts]
    self_query, self_key, self_value = square(front, 0), square(front, 1), square(back, 0)
    tail = back[:, owned_rows:]
    owners = parts * blocks
    counts = 13 * owned_rows
    slots = tail.reshape(owners, 8, -1, 128)[:, :, :2, :owned_rows]
    vecs = slots.transpose(2, 1, 0, 3).reshape(16, width)[:13]
    biases = tail[:, 5, 128 : 128 + hidden_rows].reshape(chunks, width)
    vecs = widen(jnp.concatenate([vecs, biases], axis=0))

    queries, own = project(tokens, [self_query, self_key, self_value], vecs)
    own = pump(two_parts, two_parts, own)
    other = swap_seq(own, 1)
    mixed, logsum = self_attend(ids, queries, own, other)
    mixed = pump(two_parts, two_parts, mixed)
    mixed = pump(two_parts, [], mixed)
    front, back = [g.result() for g in two_parts]
    self_out, cross_query = square(front, 0), square(back, 0)
    cot_sent = jnp.concatenate([pick(v, 1 - group) for v in (prompt_cot, cont_cot)], axis=0)
    cot_sent, mixed = tie(cot_sent, mixed)
    cot_got = swap_seq(cot_sent, 3)
    first_pre, first_low, cross_queries = self_finish(tokens, mixed, self_out, cross_query, vecs)
    cross_queries, cot_got, feed = tie(cross_queries, cot_got, feed)
    cross_key, cross_value, cross_out = [square(feed, 2 * chunks + i) for i in range(3)]
    both = jnp.concatenate([encoder, enc_other], axis=0)
    (cross_keys,) = project(both, [cross_key, cross_value], vecs)
    cross_mixed, cross_logsum, second_pre, second_low = cross_attend(
        cross_queries, cross_keys, first_pre, cross_out, vecs
    )
    upstream = jnp.concatenate(
        [pick(prompt_cot, group), cot_got[:rows], pick(cont_cot, group), cot_got[rows:]], axis=0
    )
    slope, result, third_grad, third_low, sums, outer_pair = feed_forward(
        ids, second_pre, second_low, upstream, feed, vecs, chunks, owned_rows
    )

    def send_back(own, *values):
        away = jnp.concatenate([own[rows : 2 * rows], own[3 * rows :]], axis=0)
        tied = tie(away, *values)
        return (own, swap_seq(tied[0], 3)) + tuple(tied[1:])

    def place(own, back):
        kept = (own[:rows], own[2 * rows : 3 * rows])
        back = (back[:rows], back[rows:])
        return [
            jnp.where(group == 0, jnp.stack([a, b]), jnp.stack([b, a])) for a, b in zip(kept, back)
        ]

    bits = dp_bits[::-1]
    x_first = [lo, hi] + bits
    y_first = [lo, bits[0], hi] + bits[1:]
    outer_chain = Scatter(moves, [outer_pair], x_first)
    third_low = depart([outer_chain], third_low)
    result, result_back, third_low = send_back(result, third_low)
    second_grad, cross_mix, sums, inner_pair = inner_backward(
        ids, third_grad, third_low, sums, second_pre, second_low, slope, feed, cross_out, vecs, chunks,
        owned_rows,
    )
    cross_mix, result_back = tie(cross_mix, result_back)
    prompt_out, cont_out = place(result, result_back)
    inner_chain = Scatter(moves, [inner_pair], y_first)
    feed_chains = [outer_chain, inner_chain]
    cross_mix = receive([outer_chain], cross_mix)
    cross_mix = depart([inner_chain], cross_mix)
    cross_mix = depart([outer_chain], cross_mix)
    cross_mix = advance([inner_chain], cross_mix)
    enc_part, first_grad, mix, sums, query_pair, key_pair = cross_backward(
        ids, cross_queries, cross_keys, cross_mixed, cross_mix, cross_logsum, first_low, first_pre,
        second_grad, mixed, sums, both, cross_query, self_out, cross_key, cross_value, vecs, owned_rows,
    )
    mix, enc_part = receive(feed_chains, mix, enc_part)
    cross_chains = [
        Scatter(moves, [query_pair], x_first),
        Scatter(moves, [key_pair], y_first),
    ]
    enc_half = encoder.shape[0]
    enc_there = swap_seq(enc_part[enc_half:], 1)
    enc_rows = enc_out.shape[1]
    mix = depart(cross_chains + feed_chains, mix)
    halfway = HEADS // 4
    one = self_backward(ids, queries, own, other, mixed, mix, logsum, 0, halfway)
    tied = receive(cross_chains, enc_there, outer_chain.got, inner_chain.got, mix, *one)
    enc_there, outer_chain.got, inner_chain.got, mix = tied[:4]
    one = tied[4:]
    enc_back = low(widen(enc_part[:enc_half]) + widen(enc_there))
    enc_sent, mix = tie(enc_back[enc_rows:], mix)
    enc_got = swap_seq(enc_sent, 3)
    rest = jnp.concatenate([c.total() for c in feed_chains], axis=-2)
    rest = rest.reshape((-1,) + rest.shape[-2:])
    lines = [[i for i in range(blocks) if i % 2 == side] for side in range(2)]
    rest = lax.psum_scatter(
        rest, "dp", scatter_dimension=0, axis_index_groups=lines, tiled=True
    )[0]
    mix = depart(cross_chains, mix)
    two = self_backward(ids, queries, own, other, mixed, mix, logsum, halfway, HEADS // 2)
    tied = receive(cross_chains, enc_got, *two)
    enc_got, two = tied[0], tied[1:]
    sent = [tie(h[2], *[c.away for c in cross_chains])[0] for h in (one, two)]
    got_one, got_two = [swap_seq(v, 1) for v in sent]
    part, sums, self_query_pair = query_backward(
        ids, tokens, (one[0], two[0]), (one[3], two[3]), sums, first_grad, self_query, owned_rows
    )
    got_one, got_two, part = tie(got_one, got_two, part)
    bias_sums = sums[INNER_B : INNER_B + chunks].reshape(owners, hidden_rows)
    sums = sums[:13].reshape(13, owners, owned_rows).transpose(1, 0, 2).reshape(owners, counts)
    sums = low(jnp.concatenate([sums, bias_sums], axis=1))
    sums = jnp.pad(sums[:, None, :], ((0, 0), (0, 7), (0, width - counts - hidden_rows)))
    sums = sums.reshape(-1, 2, 8, width)
    sums_pair = (
        lax.dynamic_index_in_dim(sums, seq & 1, 1, keepdims=False),
        lax.dynamic_index_in_dim(sums, 1 - (seq & 1), 1, keepdims=False),
    )
    query_chain = Scatter(moves, [self_query_pair, sums_pair], x_first)
    got_one = depart(cross_chains + [query_chain], got_one)
    total, key_pair, value_pair = key_weights(
        ids, tokens, (one[1], two[1]), (got_one, got_two), owned_rows
    )
    key_chains = [Scatter(moves, [key_pair], x_first), Scatter(moves, [value_pair], y_first)]
    total = receive(cross_chains + [query_chain], total)
    cross_last = joined(cross_chains)
    total = depart(key_chains + [query_chain, cross_last], total)
    token_grad = token_backward(total, part, self_key, self_value)
    token_grad = receive(key_chains + [query_chain, cross_last], token_grad)
    token_grad, token_back, key_chains[0].away = send_back(token_grad, key_chains[0].away)
    depart(key_chains + [query_chain, cross_last])
    token_back = receive(key_chains, token_back)
    depart(key_chains)
    totals = [query_chain.total()]
    key_chains[0].got, key_chains[1].got, totals[0] = tie(
        key_chains[0].got, key_chains[1].got, totals[0]
    )
    totals = jnp.concatenate([c.total() for c in key_chains] + totals, axis=-2)
    totals = totals.reshape((-1,) + totals.shape[-2:])
    if totals.shape[0] <= 4:
        keep, gots = line_sends(moves, totals, 1)
        tied = tie(*gots, cross_last.got)
        gots, cross_last.got = tied[:-1], tied[-1]
        tail_held = widen(keep) + sum(widen(g) for g in gots)
    else:
        tail_held = widen(
            lax.psum_scatter(totals, "dp", scatter_dimension=0, axis_index_groups=lines, tiled=True)[0]
        )
    while cross_last.got is not None:
        receive([cross_last])
        if cross_last.order:
            cross_last.ship()

    def cut_rows(held, sizes):
        ends = [sum(sizes[: i + 1]) for i in range(len(sizes))]
        return [held[e - n : e] for e, n in zip(ends, sizes)]

    self_key_grad, self_value_grad, self_query_grad, vec = cut_rows(
        tail_held, [owned_rows, owned_rows, owned_rows, 8]
    )
    cross_held = cross_last.held.reshape(-1, owned_rows, width)
    vec = vec[0]
    prompt_grad, cont_grad = place(token_grad, token_back)
    enc_grad = jnp.where(
        group == 0,
        jnp.stack([enc_back[:enc_rows], enc_got]),
        jnp.stack([enc_got, enc_back[:enc_rows]]),
    )

    rest = widen(rest)
    outer_mat_grad = rest[:hidden_rows]
    inner_mat_grad = jnp.concatenate(
        [rest[hidden_rows + i * owned_rows : hidden_rows + (i + 1) * owned_rows] for i in range(chunks)],
        axis=1,
    )
    vec_out = [vec[i * owned_rows : (i + 1) * owned_rows] for i in range(13)]
    inner_bias_out = vec[counts : counts + hidden_rows]
    return (
        prompt_out,
        cont_out,
        prompt_grad,
        cont_grad,
        enc_grad,
        self_query_grad,
        vec_out[0],
        self_key_grad,
        self_value_grad,
        vec_out[1],
        cross_held[1],
        vec_out[2],
        vec_out[3],
        vec_out[4],
        cross_held[0],
        vec_out[5],
        cross_held[2],
        cross_held[3],
        vec_out[6],
        cross_held[4],
        vec_out[7],
        vec_out[8],
        vec_out[9],
        inner_mat_grad,
        inner_bias_out,
        outer_mat_grad,
        vec_out[10],
        vec_out[11],
        vec_out[12],
    )


def solution(mesh):
    rows_spec = P("dp", "seq", None)
    mat, vec = P(("dp", "seq"), None), P(("dp", "seq"))
    weights = (
        mat,
        vec,
        mat,
        mat,
        vec,
        mat,
        vec,
        vec,
        vec,
        mat,
        vec,
        mat,
        mat,
        vec,
        mat,
        vec,
        vec,
        vec,
        mat,
        vec,
        mat,
        vec,
        vec,
        vec,
    )
    in_specs = (rows_spec, rows_spec, rows_spec, P("dp"), rows_spec, rows_spec) + weights
    out_specs = (rows_spec,) * 5 + weights
    return jax.shard_map(body, mesh=mesh, in_specs=in_specs, out_specs=out_specs, check_vma=False)
```

```python
import jax
import jax.numpy as jnp
from jax import lax
from jax.experimental import pallas as pl
from jax.experimental.pallas import tpu as pltpu
from jax.sharding import PartitionSpec as P

HEADS = 12
VMEM_LIMIT = 60 * 1024 * 1024
NEG = -1e30
FOLD = 6
SELF_FOLD = 3
SELF_BACK_FOLD = 1


def matmul(left, right):
    return jnp.dot(left, right, preferred_element_type=jnp.float32)


def contract_rows(left, right):
    return lax.dot_general(
        left, right, (((0,), (0,)), ((), ())), preferred_element_type=jnp.float32
    )


def times_transpose(left, right):
    return lax.dot_general(
        left, right, (((1,), (1,)), ((), ())), preferred_element_type=jnp.float32
    )


def widen(values):
    return values.astype(jnp.float32)


def low(values):
    return values.astype(jnp.bfloat16)


def normalize(values, gain, shift):
    centred = values - jnp.mean(values, axis=-1, keepdims=True)
    scale = lax.rsqrt(jnp.mean(centred * centred, axis=-1, keepdims=True) + 1e-05)
    return centred * scale * gain + shift


def norm_backward(values, gain, upstream):
    centred = values - jnp.mean(values, axis=-1, keepdims=True)
    scale = lax.rsqrt(jnp.mean(centred * centred, axis=-1, keepdims=True) + 1e-05)
    normed = centred * scale
    scaled = upstream * gain
    result = scale * (
        scaled
        - jnp.mean(scaled, axis=-1, keepdims=True)
        - normed * jnp.mean(scaled * normed, axis=-1, keepdims=True)
    )
    return (
        result,
        jnp.sum(upstream * normed, axis=0, keepdims=True),
        jnp.sum(upstream, axis=0, keepdims=True),
    )


(
    SELF_Q,
    SELF_V,
    SELF_O,
    GAIN_ONE,
    SHIFT_ONE,
    CROSS_Q,
    CROSS_V,
    CROSS_O,
    GAIN_TWO,
    SHIFT_TWO,
    OUTER_B,
    GAIN_THREE,
    SHIFT_THREE,
    INNER_B,
) = range(14)


def pack_vectors(vectors, out_ref, base):
    out_ref[base : base + 8, :] = jnp.zeros((8, out_ref.shape[1]), out_ref.dtype)
    for i, ref in enumerate(vectors):
        at = 128 * (i // 8)
        out_ref[base + i % 8 : base + i % 8 + 1, at : at + ref.shape[1]] = ref[...]


def pack(first, vectors, second, outer, inner, rest):
    rows, width = first[0].shape
    chunks = inner.shape[1] // width
    counts = (len(first), len(vectors), len(second), 1, 1, len(rest))

    def kernel(*refs):
        groups, at = [], 0
        for count in counts:
            groups.append(refs[at : at + count])
            at += count
        outs = refs[at:]
        if rows % 8 == 0:
            for i, ref in enumerate(groups[0]):
                outs[0][i * rows : (i + 1) * rows, :] = ref[...]
            for i, ref in enumerate(groups[2]):
                outs[1][i * rows : (i + 1) * rows, :] = ref[...]
            outs[2][: chunks * rows, :] = groups[3][0][...]
            for i in range(chunks):
                at = (chunks + i) * rows
                outs[2][at : at + rows, :] = groups[4][0][:, i * width : (i + 1) * width]
            for i, ref in enumerate(groups[5]):
                at = (2 * chunks + i) * rows
                outs[2][at : at + rows, :] = ref[...]
        pack_vectors(groups[1], outs[0], len(first) * rows if rows % 8 == 0 else 0)

    shapes = [len(first) * rows + 8, len(second) * rows, (2 * chunks + len(rest)) * rows]
    if rows % 8:
        shapes = [8, 8, 8]
    outs = pl.pallas_call(
        kernel,
        out_shape=[jax.ShapeDtypeStruct((n, width), outer.dtype) for n in shapes],
        name="pack",
    )(*first, *[v[None, :] for v in vectors], *second, outer, inner, *rest)
    if rows % 8 == 0:
        return outs
    inner = [inner[:, i * width : (i + 1) * width] for i in range(chunks)]
    return [
        jnp.concatenate(list(first) + [outs[0]], axis=0),
        jnp.concatenate(second, axis=0),
        jnp.concatenate([outer] + inner + list(rest), axis=0),
    ]


class Call:
    def __init__(self, name, grid):
        self.name, self.grid = name, grid
        self.ins, self.in_specs, self.out_shapes, self.out_specs = [], [], [], []
        self.flops, self.bytes, self.exps = 0, 0, 0
        self.lates = []

    def whole(self, array):
        zeros = (0,) * array.ndim
        self.blocked(array, array.shape, lambda *g: zeros, buffers=1)

    def blocked(self, array, block, index, buffers=2):
        mode = {} if buffers == 2 else {"pipeline_mode": pl.Buffered(buffers)}
        self.ins.append(array)
        self.in_specs.append(pl.BlockSpec(block, index, **mode))
        self.bytes += array.size * array.dtype.itemsize

    def scalars(self, array):
        self.ins.append(array)
        self.in_specs.append(pl.BlockSpec(memory_space=pltpu.SMEM))

    def late(self, array, block=None, index=None):
        self.ins.append(array)
        self.in_specs.append(pl.BlockSpec(memory_space=pl.ANY))
        block = block or array.shape
        self.bytes += array.dtype.itemsize * array.size
        self.lates.append((len(self.ins) - 1, block, index, array.dtype))

    def late_weight(self, weight):
        array, block, index = weight
        self.late(array, block, tuple(i * n for i, n in zip(index, block)))

    def late_copies(self, refs, late_refs):
        count = len(self.lates)
        copies = []
        for i, (place, block, start, _) in enumerate(self.lates):
            source = refs[place]
            if start is not None:
                source = source.at[tuple(pl.ds(a, n) for a, n in zip(start, block))]
            copies.append(pltpu.make_async_copy(source, late_refs[i], late_refs[count].at[i]))
        return copies

    def run_late(self, kernel, scratch=()):
        count = len(self.lates)
        steps = self.grid[0]

        def wrapped(*refs):
            refs, late_refs = refs[: -count - 1], refs[-count - 1 :]
            copies = self.late_copies(refs, late_refs)

            @pl.when(pl.program_id(0) == 0)
            def _():
                for copy in copies:
                    copy.start()

            def fetch():
                for copy in copies:
                    copy.wait()

            refs = list(refs)
            for i, (place, _, _, _) in enumerate(self.lates):
                refs[place] = late_refs[i]
            kernel(fetch, *refs)

        buffers = [pltpu.VMEM(block, dtype) for _, block, _, dtype in self.lates]
        return self.run(
            wrapped, list(scratch) + buffers + [pltpu.SemaphoreType.DMA((count,))]
        )

    def weight(self, weight):
        array, block, index = weight
        self.ins.append(array)
        self.in_specs.append(pl.BlockSpec(block, lambda *g: index, pipeline_mode=pl.Buffered(1)))
        self.bytes += array.shape[-1] ** 2 * 2

    def out(self, shape, dtype, block=None, index=None):
        zeros = (0,) * len(shape)
        self.out_shapes.append(jax.ShapeDtypeStruct(shape, dtype))
        self.out_specs.append(pl.BlockSpec(block or shape, index or (lambda *g: zeros)))
        size = 1
        for n in shape:
            size *= n
        self.bytes += size * jnp.dtype(dtype).itemsize

    def run(self, kernel, scratch=()):
        return pl.pallas_call(
            kernel,
            grid=self.grid,
            in_specs=self.in_specs,
            out_specs=self.out_specs,
            out_shape=self.out_shapes,
            scratch_shapes=list(scratch),
            compiler_params=pltpu.CompilerParams(vmem_limit_bytes=VMEM_LIMIT),
            cost_estimate=pl.CostEstimate(
                flops=int(self.flops), bytes_accessed=int(self.bytes), transcendentals=int(self.exps)
            ),
            name=self.name,
        )(*self.ins)


class Halves:
    def __init__(self, call, count, owners, owned_rows, width, heads=None, index=None):
        self.owned_rows = owned_rows
        self.even = owned_rows % 8 == 0
        if self.even:
            shape, outs = (owners // 2, count, owned_rows, width), 2
            block = (heads or owners // 2, 1 if index else count, owned_rows, width)
        else:
            shape, outs = (count, owners * owned_rows, width), 1
            block = (1 if index else count, 2 * (heads or owners // 2) * owned_rows, width)
        for _ in range(outs):
            if index is None:
                call.out(shape, jnp.bfloat16)
            elif self.even:
                call.out(shape, jnp.bfloat16, block, lambda *g: index(*g) + (0, 0))
            else:
                call.out(shape, jnp.bfloat16, block, lambda *g: index(*g)[::-1] + (0,))
        self.outs = outs

    def store(self, refs, at, value, mine):
        if not self.even:
            refs[0][at] = low(value)
            return
        parts = value.reshape(-1, 2, self.owned_rows, value.shape[-1])
        first, second = low(parts[:, 0]), low(parts[:, 1])
        refs[0][:, at] = jnp.where(mine == 0, first, second)
        refs[1][:, at] = jnp.where(mine == 0, second, first)

    def pair(self, results, mine):
        if self.even:
            return tuple(results)
        whole = results[0]
        parts = whole.reshape(whole.shape[0], -1, 2, self.owned_rows, whole.shape[-1])
        return tuple(
            lax.dynamic_index_in_dim(parts, which, 2, keepdims=False).transpose(1, 0, 2, 3)
            for which in (mine, 1 - mine)
        )


def load(ref):
    value = ref[...]
    return value.reshape(-1, value.shape[-1])


def row(vecs_ref, index):
    return vecs_ref[index : index + 1, :]


def fill_bias(bias_ref, chunk, rows, ids_ref):
    half, block = rows // 2, rows // 4
    key = lax.broadcasted_iota(jnp.int32, (rows, rows), 0)
    query = lax.broadcasted_iota(jnp.int32, (rows, rows), 1)
    key_block = jnp.where(
        lax.rem(key, half) < block, ids_ref[2 * chunk], ids_ref[2 * chunk + 1]
    )
    query_block = jnp.where(lax.rem(query, half) < block, ids_ref[0], ids_ref[1])
    key_place = key_block * block + lax.rem(key, block)
    query_place = query_block * block + lax.rem(query, block)
    causal = key_place <= query_place
    prompt_key = key < half
    prompt_query = query < half
    allowed = (prompt_key & prompt_query & causal) | (
        jnp.logical_not(prompt_query)
        & ((prompt_key & (key_place < ids_ref[4])) | (jnp.logical_not(prompt_key) & causal))
    )
    bias_ref[chunk] = jnp.where(allowed, 0.0, NEG)


def lane_masks(values):
    lane = lax.broadcasted_iota(jnp.int32, values.shape, 1)
    zero = jnp.zeros_like(values)
    first = lane < values.shape[1] // 2
    return jnp.where(first, values, zero), jnp.where(first, zero, values)


def key_parts(key_rows, masked):
    if not masked:
        return [(0, key_rows, 0)]
    half = key_rows // 2
    return [(0, half, 0), (half, key_rows, half)]


def widened(values, first, rows, fill):
    if first == 0:
        return values
    blank = jnp.full(values.shape[:-1] + (first,), fill, values.dtype)
    return jnp.concatenate([blank, values], axis=-1)


def attend_pair(queries, keys, values, bias_ref, log_ref):
    rows = queries.shape[0]
    queries = lane_masks(queries)
    parts = [
        (chunk,) + part
        for part in key_parts(keys[0].shape[0], bias_ref is not None)
        for chunk in range(len(keys))
    ]
    outs = []
    for head in range(2):
        scores = []
        for chunk, low_key, high_key, first in parts:
            part = times_transpose(keys[chunk][low_key:high_key], queries[head][first:])
            if bias_ref is not None:
                part = part + bias_ref[chunk, low_key:high_key, first:]
            scores.append(part)
        top = None
        for part, (_, _, _, first) in zip(scores, parts):
            most = widened(part.max(axis=0, keepdims=True), first, rows, NEG)
            top = most if top is None else jnp.maximum(top, most)
        total, mixed = 0.0, 0.0
        for part, (chunk, low_key, high_key, first) in zip(scores, parts):
            weights = jnp.exp(part - top[:, first:])
            total = total + widened(weights.sum(axis=0, keepdims=True), first, rows, 0.0)
            out = contract_rows(values[chunk][low_key:high_key], low(weights))
            mixed = mixed + widened(out, first, rows, 0.0)
        outs.append(mixed * (1.0 / total))
        log_ref[0, head : head + 1, :] = top + jnp.log(total)
    lane = lax.broadcasted_iota(jnp.int32, outs[0].shape, 0)
    return low(jnp.where(lane < outs[0].shape[0] // 2, outs[0], outs[1]).T)


def attend_pair_backward(queries, keys, values, bias_ref, log_ref, mixed, upstream):
    rows = queries.shape[0]
    queries = lane_masks(queries)
    ups = lane_masks(upstream)
    product = widen(mixed) * widen(upstream)
    high = low(product)
    rest = low(product - widen(high))
    pair = product.shape[1]
    lane = lax.broadcasted_iota(jnp.int32, (8, pair), 1)
    line = lax.broadcasted_iota(jnp.int32, (8, pair), 0)
    pick = jnp.where(
        ((lane < pair // 2) & (line == 0)) | ((lane >= pair // 2) & (line == 1)), 1.0, 0.0
    ).astype(jnp.bfloat16)
    delta = times_transpose(pick, high) + times_transpose(pick, rest)
    dq = 0.0
    parts = key_parts(keys[0].shape[0], bias_ref is not None)
    dk = [[0.0] * len(parts) for _ in keys]
    dv = [[0.0] * len(parts) for _ in keys]
    for head in range(2):
        for chunk in range(len(keys)):
            masked_keys = lane_masks(keys[chunk])[head]
            for i, (low_key, high_key, first) in enumerate(parts):
                part = times_transpose(keys[chunk][low_key:high_key], queries[head][first:])
                if bias_ref is not None:
                    part = part + bias_ref[chunk, low_key:high_key, first:]
                probs = jnp.exp(part - log_ref[0, head : head + 1, first:])
                up = ups[head][first:]
                prob_grad = times_transpose(values[chunk][low_key:high_key], up)
                score_grad = low(probs * (prob_grad - delta[head : head + 1, first:]))
                dv[chunk][i] = dv[chunk][i] + matmul(low(probs), up)
                dk[chunk][i] = dk[chunk][i] + matmul(score_grad, queries[head][first:])
                out = contract_rows(masked_keys[low_key:high_key], score_grad)
                dq = dq + widened(out, first, rows, 0.0)
    join = [
        [v[0] if len(v) == 1 else jnp.concatenate(v, axis=0) for v in side] for side in (dk, dv)
    ]
    return low(dq.T), join[0], join[1]


def project_kernel(scaled, x_ref, *refs):
    vecs_ref = refs[-3] if scaled else refs[-2]
    values = x_ref[...]
    if scaled:
        wq_ref, wk_ref, wv_ref = refs[:3]
        q_ref, kv_ref = refs[-2:]
        q_ref[...] = low((matmul(values, load(wq_ref)) + row(vecs_ref, SELF_Q)) * 0.125)
        bias = row(vecs_ref, SELF_V)
    else:
        wk_ref, wv_ref = refs[:2]
        kv_ref = refs[-1]
        bias = row(vecs_ref, CROSS_V)
    kv_ref[0] = low(matmul(values, load(wk_ref)))
    kv_ref[1] = low(matmul(values, load(wv_ref)) + bias)


def project(tokens, weights, vecs):
    rows, width = tokens.shape
    scaled = len(weights) == 3
    call = Call("project", (1,))
    call.whole(tokens)
    for weight in weights:
        call.weight(weight)
    call.whole(vecs)
    if scaled:
        call.out((rows, width), jnp.bfloat16)
    call.out((2, rows, width), jnp.bfloat16)
    call.flops = 2 * len(weights) * rows * width * width

    def kernel(*refs):
        project_kernel(scaled, *refs)

    return call.run(kernel)


def lanes_of(width):
    lanes = 2 * (width // HEADS)

    def at(h):
        return pl.ds(pl.multiple_of(h * lanes, lanes), lanes)

    return lanes, at


def self_attend(ids, queries, own, other):
    rows, width = queries.shape
    pairs, fold = HEADS // 2, SELF_FOLD
    lanes, _ = lanes_of(width)
    call = Call("self_attend", (pairs // fold,))
    call.scalars(ids)
    call.blocked(queries, (rows, fold * lanes), lambda h: (0, h))
    for array in (own, other):
        call.blocked(array, (2, rows, fold * lanes), lambda h: (0, 0, h))
    call.out((rows, width), jnp.bfloat16, (rows, fold * lanes), lambda h: (0, h))
    call.out((pairs, 2, rows), jnp.float32, (fold, 2, rows), lambda h: (h, 0, 0))
    call.flops = 16 * rows * rows * width
    call.exps = 2 * rows * rows * HEADS

    def kernel(ids_ref, q_ref, own_ref, other_ref, mixed_ref, log_ref, bias_ref):
        @pl.when(pl.program_id(0) == 0)
        def _():
            for chunk in range(2):
                fill_bias(bias_ref, chunk, rows, ids_ref)

        for i in range(fold):
            part = slice(i * lanes, (i + 1) * lanes)
            keys, values = [(own_ref[n, :, part], other_ref[n, :, part]) for n in range(2)]
            mixed_ref[:, part] = attend_pair(
                q_ref[:, part], keys, values, bias_ref, log_ref.at[pl.ds(i, 1)]
            )

    return call.run(kernel, [pltpu.VMEM((2, rows, rows), jnp.float32)])


def self_finish(tokens, mixed, out_weight, query_weight, vecs):
    rows, width = tokens.shape
    call = Call("self_finish", (1,))
    call.whole(tokens)
    call.whole(mixed)
    call.weight(out_weight)
    call.weight(query_weight)
    call.whole(vecs)
    call.out((rows, width), jnp.float32)
    call.out((rows, width), jnp.bfloat16)
    call.out((rows, width), jnp.bfloat16)
    call.flops = 4 * rows * width * width

    def kernel(x_ref, mixed_ref, wo_ref, wq_ref, vecs_ref, pre_ref, low_ref, next_ref):
        pre = widen(x_ref[...]) + matmul(mixed_ref[...], load(wo_ref)) + row(vecs_ref, SELF_O)
        pre_ref[...] = pre
        first = low(normalize(pre, row(vecs_ref, GAIN_ONE), row(vecs_ref, SHIFT_ONE)))
        low_ref[...] = first
        next_ref[...] = low((matmul(first, load(wq_ref)) + row(vecs_ref, CROSS_Q)) * 0.125)

    return call.run(kernel)


def cross_attend(queries, keys, first_pre, out_weight, vecs):
    rows, width = queries.shape
    key_rows = keys.shape[1]
    pairs, fold = HEADS // 2, FOLD
    lanes, at = lanes_of(width)
    call = Call("cross_attend", (pairs // fold,))
    call.blocked(queries, (rows, fold * lanes), lambda h: (0, h))
    call.blocked(keys, (2, key_rows, fold * lanes), lambda h: (0, 0, h))
    call.late(first_pre)
    call.late_weight(out_weight)
    call.whole(vecs)
    call.out((rows, width), jnp.bfloat16)
    call.out((pairs, 2, rows), jnp.float32, (fold, 2, rows), lambda h: (h, 0, 0))
    call.out((rows, width), jnp.float32)
    call.out((rows, width), jnp.bfloat16)
    call.flops = 8 * rows * key_rows * width + 2 * rows * width * width
    call.exps = 2 * rows * key_rows * HEADS

    def kernel(
        fetch, q_ref, keys_ref, first_ref, wo_ref, vecs_ref, mixed_ref, log_ref, pre_ref, low_ref
    ):
        step = pl.program_id(0)
        for i in range(fold):
            part = slice(i * lanes, (i + 1) * lanes)
            mixed_ref[:, at(step * fold + i)] = attend_pair(
                q_ref[:, part],
                (keys_ref[0, :, part],),
                (keys_ref[1, :, part],),
                None,
                log_ref.at[pl.ds(i, 1)],
            )

        @pl.when(step == pairs // fold - 1)
        def _():
            fetch()
            first = normalize(first_ref[...], row(vecs_ref, GAIN_ONE), row(vecs_ref, SHIFT_ONE))
            pre = first + matmul(mixed_ref[...], load(wo_ref)) + row(vecs_ref, CROSS_O)
            pre_ref[...] = pre
            low_ref[...] = low(normalize(pre, row(vecs_ref, GAIN_TWO), row(vecs_ref, SHIFT_TWO)))

    return call.run_late(kernel)


def feed_blocks(call, feed, width, chunks, owned_rows):
    owners = feed.shape[0]

    def at(i):
        return jnp.minimum(i, chunks - 1)

    hidden_rows = chunks * owned_rows
    if owned_rows % 8 == 0:
        call.blocked(feed, (owners, owned_rows, width), lambda i: (0, chunks + at(i), 0))
        call.blocked(feed, (owners // chunks, hidden_rows, width), lambda i: (at(i), 0, 0))
    else:
        parts = [
            feed[:, hidden_rows + i * owned_rows : hidden_rows + (i + 1) * owned_rows]
            for i in range(chunks)
        ]
        parts = [p.reshape(-1, width) for p in parts]
        call.blocked(jnp.concatenate(parts, axis=1), (width, width), lambda i: (0, at(i)))
        call.blocked(feed[:, :hidden_rows].reshape(-1, width), (width, width), lambda i: (at(i), 0))


def feed_forward(ids, second_pre, second_low, upstream, feed, vecs, chunks, owned_rows):
    rows, width = second_low.shape
    hidden = chunks * width
    owners = width // owned_rows
    call = Call("feed_forward", (2 * chunks,))
    call.scalars(ids)
    call.whole(second_pre)
    call.whole(second_low)
    call.late(upstream)
    feed_blocks(call, feed, width, chunks, owned_rows)
    call.whole(vecs)
    call.out(
        (rows, hidden), jnp.bfloat16, (rows, width), lambda i: (0, jnp.minimum(i, chunks - 1))
    )
    call.out((rows, width), jnp.bfloat16)
    call.out((rows, width), jnp.float32)
    call.out((rows, width), jnp.bfloat16)
    call.out((24, width), jnp.float32)
    half = Halves(
        call,
        1,
        owners,
        chunks * owned_rows,
        width,
        owners // 2 // chunks,
        lambda i: (jnp.maximum(i - chunks, 0), 0),
    )
    call.flops = 6 * rows * hidden * width
    call.exps = 2 * rows * hidden

    def kernel(
        fetch, ids_ref, pre_ref, low_ref, up_ref, inner_ref, outer_ref, vecs_ref, slope_ref, out_ref,
        grad_ref, third_low_ref, sums_ref, *rest,
    ):
        grads, (active_ref, third_ref) = rest[:-2], rest[-2:]
        step = pl.program_id(0)

        @pl.when(step == 0)
        def _():
            second = normalize(pre_ref[...], row(vecs_ref, GAIN_TWO), row(vecs_ref, SHIFT_TWO))
            third_ref[...] = second + row(vecs_ref, OUTER_B)

        @pl.when(step < chunks)
        def _():
            inner = matmul(low_ref[...], load(inner_ref)) + vecs_ref[pl.ds(INNER_B + step, 1), :]
            bell = 0.5 * (1.0 + lax.erf(inner * 0.7071067811865476))
            active = low(inner * bell)
            active_ref[step] = active
            density = jnp.exp(-0.5 * inner * inner) * 0.3989422804014327
            slope_ref[...] = low(bell + inner * density)
            third_ref[...] += matmul(active, load(outer_ref))

        @pl.when(step == chunks - 1)
        def _():
            fetch()
            third = third_ref[...]
            gain = row(vecs_ref, GAIN_THREE)
            out_ref[...] = low(normalize(third, gain, row(vecs_ref, SHIFT_THREE)))
            grad, gain_sum, shift_sum = norm_backward(third, gain, widen(up_ref[...]))
            grad_ref[...] = grad
            third_low_ref[...] = low(grad)
            sums_ref[...] = jnp.zeros_like(sums_ref)
            sums_ref[GAIN_THREE : GAIN_THREE + 1, :] = gain_sum
            sums_ref[SHIFT_THREE : SHIFT_THREE + 1, :] = shift_sum
            sums_ref[OUTER_B : OUTER_B + 1, :] = jnp.sum(widen(low(grad)), axis=0, keepdims=True)

        @pl.when(step >= chunks)
        def _():
            active = active_ref[jnp.maximum(step - chunks, 0)]
            half.store(grads, 0, contract_rows(active, third_low_ref[...]), ids_ref[5])

    results = call.run_late(
        kernel,
        [pltpu.VMEM((chunks, rows, width), jnp.bfloat16), pltpu.VMEM((rows, width), jnp.float32)],
    )
    return tuple(results[:5]) + (half.pair(results[5:], ids[5]),)


def inner_backward(
    ids, third_grad, third_low, sums, second_pre, second_low, slope, feed, out_weight, vecs,
    chunks, owned_rows,
):
    rows, width = second_low.shape
    owners = width // owned_rows
    call = Call("inner_backward", (chunks,))
    call.scalars(ids)
    for array in (third_grad, third_low, sums):
        call.whole(array)
    call.late(second_pre)
    call.whole(second_low)
    call.blocked(slope, (rows, width), lambda i: (0, i))
    feed_blocks(call, feed, width, chunks, owned_rows)
    call.late_weight(out_weight)
    call.whole(vecs)
    call.out((rows, width), jnp.float32)
    call.out((rows, width), jnp.bfloat16)
    call.out((24, width), jnp.float32)
    inner_half = Halves(call, chunks, owners, owned_rows, width, owners // 2, lambda i: (0, i))
    call.flops = 6 * rows * chunks * width * width + 4 * rows * width * width

    def kernel(
        fetch, ids_ref, third_ref, third_low_ref, sums_in_ref, second_ref, low_ref, slope_ref, inner_ref, outer_ref,
        wo_ref, vecs_ref, second_grad_ref, mix_ref, sums_ref, *rest,
    ):
        inner_grads, total_ref = rest[:-1], rest[-1]
        step = pl.program_id(0)
        mine = ids_ref[5]

        @pl.when(step == 0)
        def _():
            total_ref[...] = third_ref[...]
            sums_ref[...] = sums_in_ref[...]

        inner_low = low(times_transpose(third_low_ref[...], load(outer_ref)) * widen(slope_ref[...]))
        total_ref[...] += times_transpose(inner_low, load(inner_ref))
        inner_half.store(inner_grads, 0, contract_rows(low_ref[...], inner_low), mine)
        sums_ref[pl.ds(INNER_B + step, 1), :] = jnp.sum(widen(inner_low), axis=0, keepdims=True)

        @pl.when(step == chunks - 1)
        def _():
            fetch()
            grad, gain_sum, shift_sum = norm_backward(
                second_ref[...], row(vecs_ref, GAIN_TWO), total_ref[...]
            )
            second_grad_ref[...] = grad
            cross_low = low(grad)
            sums_ref[GAIN_TWO : GAIN_TWO + 1, :] = gain_sum
            sums_ref[SHIFT_TWO : SHIFT_TWO + 1, :] = shift_sum
            sums_ref[CROSS_O : CROSS_O + 1, :] = jnp.sum(widen(cross_low), axis=0, keepdims=True)
            mix_ref[...] = low(times_transpose(cross_low, load(wo_ref)))

    results = call.run_late(kernel, [pltpu.VMEM((rows, width), jnp.float32)])
    return tuple(results[:3]) + (inner_half.pair(results[3:], ids[5]),)


def cross_backward(
    ids, queries, keys, mixed, upstream, logsum, first_low, first_pre, second_grad, self_mixed, sums,
    encoder, query_weight, out_weight, key_weight, value_weight, vecs, owned_rows,
):
    rows, width = queries.shape
    key_rows = keys.shape[1]
    pairs, fold = HEADS // 2, FOLD
    lanes, at = lanes_of(width)
    call = Call("cross_backward", (pairs // fold,))
    call.scalars(ids)
    for array in (queries, mixed, upstream):
        call.blocked(array, (rows, fold * lanes), lambda h: (0, h))
    call.blocked(logsum, (fold, 2, rows), lambda h: (h, 0, 0))
    call.blocked(keys, (2, key_rows, fold * lanes), lambda h: (0, 0, h))
    for array in (first_low, first_pre, second_grad, self_mixed, mixed):
        call.late(array)
    call.whole(sums)
    call.late_weight(query_weight)
    call.late_weight(out_weight)
    call.late(encoder)
    call.late_weight(key_weight)
    call.late_weight(value_weight)
    call.whole(vecs)
    call.out((key_rows, width), jnp.bfloat16)
    call.out((rows, width), jnp.float32)
    call.out((rows, width), jnp.bfloat16)
    call.out((24, width), jnp.float32)
    halves = [Halves(call, n, width // owned_rows, owned_rows, width) for n in (2, 3)]
    outs = halves[0].outs
    call.flops = 20 * rows * key_rows * width + 8 * (rows + key_rows) * width * width
    call.exps = 2 * rows * key_rows * HEADS

    def kernel(
        fetch, ids_ref, q_ref, mixed_ref, up_ref, log_ref, keys_ref, low_ref, pre_ref, grad_ref,
        self_mixed_ref, all_mixed_ref, sums_in_ref, wq_ref, wo_ref, enc_ref, wk_ref, wv_ref, vecs_ref, enc_back_ref, first_ref, mix_ref,
        sums_ref, *rest,
    ):
        step = pl.program_id(0)
        weights_refs, (dq_ref, dkv_ref) = rest[:-2], rest[-2:]

        @pl.when(step == 0)
        def _():
            sums_ref[...] = sums_in_ref[...]

        for i in range(fold):
            part = slice(i * lanes, (i + 1) * lanes)
            dq, dk, dv = attend_pair_backward(
                q_ref[:, part],
                (keys_ref[0, :, part],),
                (keys_ref[1, :, part],),
                None,
                log_ref.at[pl.ds(i, 1)],
                mixed_ref[:, part],
                up_ref[:, part],
            )
            place = at(step * fold + i)
            dq_ref[:, place] = dq
            dkv_ref[0, :, place] = low(dk[0])
            dkv_ref[1, :, place] = low(dv[0])
            sums_ref[CROSS_V : CROSS_V + 1, place] = jnp.sum(dv[0], axis=0, keepdims=True)

        @pl.when(step == pairs // fold - 1)
        def _():
            fetch()
            query_low = dq_ref[...]
            halves[0].store(weights_refs[:outs], 0, contract_rows(low_ref[...], query_low) * 0.125, ids_ref[5])
            for i in range(2):
                value = contract_rows(enc_ref[...], dkv_ref[i])
                halves[1].store(weights_refs[outs:], i, value, ids_ref[5])
            cross_low = low(grad_ref[...])
            value = contract_rows(all_mixed_ref[...], cross_low)
            halves[1].store(weights_refs[outs:], 2, value, ids_ref[5])
            enc_back_ref[...] = low(
                times_transpose(dkv_ref[0], load(wk_ref)) + times_transpose(dkv_ref[1], load(wv_ref))
            )
            total = grad_ref[...] + times_transpose(query_low, load(wq_ref)) * 0.125
            grad, gain_sum, shift_sum = norm_backward(pre_ref[...], row(vecs_ref, GAIN_ONE), total)
            first_ref[...] = grad
            self_low = low(grad)
            mix_ref[...] = low(times_transpose(self_low, load(wo_ref)))
            halves[0].store(weights_refs[:outs], 1, contract_rows(self_mixed_ref[...], self_low), ids_ref[5])
            sums_ref[GAIN_ONE : GAIN_ONE + 1, :] = gain_sum
            sums_ref[SHIFT_ONE : SHIFT_ONE + 1, :] = shift_sum
            sums_ref[SELF_O : SELF_O + 1, :] = jnp.sum(widen(self_low), axis=0, keepdims=True)
            sums_ref[CROSS_Q : CROSS_Q + 1, :] = jnp.sum(widen(query_low), axis=0, keepdims=True) * 0.125

    results = call.run_late(
        kernel,
        [pltpu.VMEM((rows, width), jnp.bfloat16), pltpu.VMEM((2, key_rows, width), jnp.bfloat16)],
    )
    return tuple(results[:4]) + (
        halves[0].pair(results[4 : 4 + outs], ids[5]),
        halves[1].pair(results[4 + outs :], ids[5]),
    )


def self_backward(ids, queries, own, other, mixed, upstream, logsum, first, last):
    rows, width = queries.shape
    lanes, _ = lanes_of(width)
    count, fold = last - first, SELF_BACK_FOLD
    start = first // fold
    call = Call("self_backward", (count // fold,))
    call.scalars(ids)
    for array in (queries, mixed, upstream):
        call.blocked(array, (rows, fold * lanes), lambda h: (0, start + h))
    call.blocked(logsum, (fold, 2, rows), lambda h: (start + h, 0, 0))
    for array in (own, other):
        call.blocked(array, (2, rows, fold * lanes), lambda h: (0, 0, start + h))
    call.out((rows, count * lanes), jnp.bfloat16, (rows, fold * lanes), lambda h: (0, h))
    for _ in range(2):
        call.out(
            (2, rows, count * lanes), jnp.bfloat16, (2, rows, fold * lanes), lambda h: (0, 0, h)
        )
    call.out((8, count * lanes), jnp.float32, (8, fold * lanes), lambda h: (0, h))
    call.flops = 40 * rows * rows * count * lanes
    call.exps = 4 * rows * rows * count

    def kernel(
        ids_ref, q_ref, mixed_ref, up_ref, log_ref, own_ref, other_ref, dq_ref, own_out_ref,
        other_out_ref, sums_ref, bias_ref,
    ):
        @pl.when(pl.program_id(0) == 0)
        def _():
            for chunk in range(2):
                fill_bias(bias_ref, chunk, rows, ids_ref)

        for i in range(fold):
            part = slice(i * lanes, (i + 1) * lanes)
            keys, values = [(own_ref[n, :, part], other_ref[n, :, part]) for n in range(2)]
            dq, dk, dv = attend_pair_backward(
                q_ref[:, part],
                keys,
                values,
                bias_ref,
                log_ref.at[pl.ds(i, 1)],
                mixed_ref[:, part],
                up_ref[:, part],
            )
            dq_ref[:, part] = dq
            for chunk, out in enumerate((own_out_ref, other_out_ref)):
                out[0, :, part] = low(dk[chunk])
                out[1, :, part] = low(dv[chunk])
            sums_ref[0:1, part] = sum(jnp.sum(v, axis=0, keepdims=True) for v in dv)
            sums_ref[1:2, part] = jnp.sum(widen(dq), axis=0, keepdims=True) * 0.125

    return call.run(kernel, [pltpu.VMEM((2, rows, rows), jnp.float32)])


def query_backward(ids, tokens, query_low, half_sums, sums, first_grad, query_weight, owned_rows):
    rows, width = tokens.shape
    call = Call("query_backward", (1,))
    call.scalars(ids)
    for array in (tokens, first_grad, sums) + tuple(query_low) + tuple(half_sums):
        call.whole(array)
    call.weight(query_weight)
    call.out((rows, width), jnp.float32)
    call.out((24, width), jnp.float32)
    half = Halves(call, 1, width // owned_rows, owned_rows, width)
    call.flops = 4 * rows * width * width

    def kernel(
        ids_ref, x_ref, grad_ref, sums_in_ref, first_ref, second_ref, first_sums_ref, second_sums_ref,
        wq_ref, part_ref, sums_ref, *weights_refs,
    ):
        sums_ref[...] = sums_in_ref[...]
        cut = first_ref.shape[1]
        for lanes, ref in ((slice(0, cut), first_sums_ref), (slice(cut, width), second_sums_ref)):
            sums_ref[SELF_V : SELF_V + 1, lanes] = ref[0:1, :]
            sums_ref[SELF_Q : SELF_Q + 1, lanes] = ref[1:2, :]
        query = jnp.concatenate([first_ref[...], second_ref[...]], axis=1)
        half.store(weights_refs, 0, contract_rows(x_ref[...], query) * 0.125, ids_ref[5])
        part_ref[...] = grad_ref[...] + times_transpose(query, load(wq_ref)) * 0.125

    results = call.run(kernel)
    return results[0], results[1], half.pair(results[2:], ids[5])


def key_weights(ids, tokens, mine, got, owned_rows):
    rows, width = tokens.shape
    call = Call("key_weights", (1,))
    call.scalars(ids)
    for array in (tokens,) + tuple(mine) + tuple(got):
        call.whole(array)
    call.out((2, rows, width), jnp.bfloat16)
    halves = [Halves(call, 1, width // owned_rows, owned_rows, width) for _ in range(2)]
    outs = halves[0].outs
    call.flops = 4 * rows * width * width

    def kernel(ids_ref, x_ref, mine_a, mine_b, got_a, got_b, total_ref, *weights_refs):
        values = x_ref[...]
        for i in range(2):
            total = low(
                jnp.concatenate(
                    [widen(m[i]) + widen(g[i]) for m, g in ((mine_a, got_a), (mine_b, got_b))], axis=1
                )
            )
            total_ref[i] = total
            refs = weights_refs[i * outs : (i + 1) * outs]
            halves[i].store(refs, 0, contract_rows(values, total), ids_ref[5])

    results = call.run(kernel)
    return (results[0],) + tuple(
        halves[i].pair(results[1 + i * outs : 1 + (i + 1) * outs], ids[5]) for i in range(2)
    )


def token_backward(total, part, key_weight, value_weight):
    rows, width = part.shape
    call = Call("token_backward", (1,))
    call.whole(total)
    call.whole(part)
    call.weight(key_weight)
    call.weight(value_weight)
    call.out((rows, width), jnp.bfloat16)
    call.flops = 4 * rows * width * width

    def kernel(total_ref, part_ref, wk_ref, wv_ref, out_ref):
        out_ref[...] = low(
            part_ref[...]
            + times_transpose(total_ref[0], load(wk_ref))
            + times_transpose(total_ref[1], load(wv_ref))
        )

    return call.run(kernel)[0]


def flip(size, bit):
    return [(i, i ^ bit) for i in range(size)]


def swap_seq(values, bits):
    return lax.ppermute(values, "seq", flip(lax.axis_size("seq"), bits))


def tie(*values):
    return lax.optimization_barrier(values)


def bit_order(dp_size, seq_size):
    return [("dp", b) for b in range(dp_size.bit_length() - 1)][::-1] + [
        ("seq", b) for b in range(seq_size.bit_length() - 1)
    ][::-1]


class Moves:
    def __init__(self):
        self.spots = {name: lax.axis_index(name) for name in ("dp", "seq")}
        self.sizes = {name: lax.axis_size(name) for name in ("dp", "seq")}
        self.canonical = bit_order(self.sizes["dp"], self.sizes["seq"])

    def mine(self, step):
        return (self.spots[step[0]] >> step[1]) & 1

    def send(self, values, step):
        name, bit = step
        flat = values.reshape(-1, values.shape[-1])
        return lax.ppermute(flat, name, flip(self.sizes[name], 1 << bit)).reshape(values.shape)


def split_sum(keep, got, at, mine):
    def side(which):
        first, second = [
            lax.dynamic_index_in_dim(v, which, at, keepdims=False) for v in (keep, got)
        ]
        return low(widen(first) + widen(second))

    return side(mine), side(1 - mine)


class Scatter:
    def __init__(self, moves, pairs, order):
        self.moves = moves
        self.dims = [step for step in moves.canonical if step != order[0]]
        self.order = list(order)
        pieces = (2,) * len(self.dims)

        def join(arrays):
            arrays = [a.reshape(pieces + (-1, a.shape[-1])) for a in arrays]
            return arrays[0] if len(arrays) == 1 else jnp.concatenate(arrays, axis=-2)

        self.keep = join([k for k, _ in pairs])
        self.away = join([a for _, a in pairs])
        self.got = None

    def ship(self):
        self.got = self.moves.send(self.away, self.order.pop(0))
        self.away = None

    def take(self):
        got, self.got = self.got, None
        if self.order:
            step = self.order[0]
            at = self.dims.index(step)
            self.keep, self.away = split_sum(self.keep, got, at, self.moves.mine(step))
            self.dims.pop(at)
        else:
            self.held = widen(self.keep) + widen(got)

    def total(self):
        return low(widen(self.keep) + widen(self.got))


def joined(chains):
    first = chains[0]
    chain = object.__new__(Scatter)
    chain.moves, chain.dims, chain.order, chain.got = first.moves, first.dims, first.order, None
    chain.keep = jnp.concatenate([c.keep for c in chains], axis=-2)
    chain.away = jnp.concatenate([c.away for c in chains], axis=-2)
    return chain


def receive(chains, *values):
    tied = tie(*[c.got for c in chains], *values)
    for chain, got in zip(chains, tied):
        chain.got = got
        chain.take()
    values = tied[len(chains) :]
    return values[0] if len(values) == 1 else values


def depart(chains, *values):
    tied = tie(*[c.away for c in chains], *values)
    for chain, away in zip(chains, tied):
        chain.away = away
        chain.ship()
    values = tied[len(chains) :]
    return values[0] if len(values) == 1 else values


def advance(chains, *values):
    values = receive(chains, *values)
    return depart(chains, *(values if isinstance(values, (list, tuple)) else (values,)))


def line_sends(moves, totals, first):
    count = totals.shape[0]
    spot = moves.spots["dp"] >> first
    keep = lax.dynamic_index_in_dim(totals, spot, 0, keepdims=False)
    away = [
        lax.dynamic_index_in_dim(totals, spot ^ i, 0, keepdims=False) for i in range(1, count)
    ]
    away = tie(*away)
    size = moves.sizes["dp"]
    return keep, [lax.ppermute(v, "dp", flip(size, i << first)) for i, v in enumerate(away, 1)]


class Gather:
    def __init__(self, moves, held, order, dims=()):
        self.moves, self.held, self.order, self.dims = moves, held, list(order), list(dims)

    def ship(self):
        self.got = self.moves.send(self.held, self.order[0])

    def take(self):
        step = self.order.pop(0)
        mine = self.moves.mine(step)
        first = jnp.where(mine == 0, self.held, self.got)
        second = jnp.where(mine == 0, self.got, self.held)
        self.held = jnp.stack([first, second], axis=0)
        self.dims.insert(0, step)

    def part(self, first, last, order):
        return Gather(self.moves, self.held[..., first:last, :], order, self.dims)

    def result(self):
        order = [self.dims.index(step) for step in self.moves.canonical]
        count = len(order)
        held = self.held.transpose(order + [count, count + 1])
        return held.reshape((-1,) + held.shape[-2:])


def pump(taking, shipping, *values):
    tied = tie(*[g.got for g in taking], *values)
    for gather, got in zip(taking, tied):
        gather.got = got
        gather.take()
    tied = tie(*[g.held for g in shipping], *tied[len(taking) :])
    for gather, held in zip(shipping, tied):
        gather.held = held
        gather.ship()
    values = tied[len(shipping) :]
    return values[0] if len(values) == 1 else values


def body(
    prompt_in,
    cont_in,
    enc_out,
    prefix,
    prompt_cot,
    cont_cot,
    self_query,
    self_qbias,
    self_key,
    self_value,
    self_vbias,
    self_out,
    self_obias,
    gain_one,
    shift_one,
    cross_query,
    cross_qbias,
    cross_key,
    cross_value,
    cross_vbias,
    cross_out,
    cross_obias,
    gain_two,
    shift_two,
    inner_mat,
    inner_bias,
    outer_mat,
    outer_bias,
    gain_three,
    shift_three,
):
    seq = lax.axis_index("seq")
    parts, blocks = lax.axis_size("seq"), lax.axis_size("dp")
    rows = prompt_in.shape[1]
    width = prompt_in.shape[2]
    owned_rows = self_query.shape[0]
    group = seq // 2
    ids = jnp.stack([seq, 3 - seq, seq ^ 1, 3 - (seq ^ 1), prefix[group], seq & 1]).astype(jnp.int32)

    def pick(array, index):
        return lax.dynamic_index_in_dim(array, index, 0, keepdims=False)

    vectors = [
        self_qbias,
        self_vbias,
        self_obias,
        gain_one,
        shift_one,
        cross_qbias,
        cross_vbias,
        cross_obias,
        gain_two,
        shift_two,
        outer_bias,
        gain_three,
        shift_three,
    ]
    hidden_rows = outer_mat.shape[0]
    chunks = hidden_rows // owned_rows
    first_part, second_part, feed = pack(
        [self_query, self_key, self_value],
        vectors + [inner_bias],
        [self_out, cross_query],
        outer_mat,
        inner_mat,
        [cross_key, cross_value, cross_out],
    )
    moves = Moves()
    bits = moves.canonical
    dp_bits, hi, lo = bits[:-2], bits[-2], bits[-1]
    line, near = dp_bits[:-1], dp_bits[-1]
    cut = 2 * owned_rows
    one = Gather(moves, first_part, line)
    one.ship()
    prompt_got = swap_seq(pick(prompt_in, 1 - group), 3)
    sent = jnp.concatenate([pick(v, 1 - group) for v in (cont_in, enc_out)], axis=0)
    feed = lax.all_gather(feed, ("dp", "seq"), axis=0, tiled=False)
    prompt_got, sent, second_part = pump([one], [one], prompt_got, sent, second_part)
    two = Gather(moves, second_part, line)
    got = swap_seq(sent, 3)
    while len(one.order) > 1:
        pump([one], [one])
    got = pump([one], [], got)
    one_parts = [
        one.part(0, cut, [near, hi, lo]),
        one.part(cut, first_part.shape[0], [hi, near, lo]),
    ]
    got = pump([], one_parts + [two], got)
    got = pump(one_parts + [two], one_parts + [two], got)
    while len(two.order) > 1:
        got = pump([two], [two], got)
    got = pump(one_parts + [two], one_parts, got)
    two_parts = [
        two.part(0, owned_rows, [near, hi, lo]),
        two.part(owned_rows, second_part.shape[0], [hi, near, lo]),
    ]
    got = pump(one_parts, two_parts, got)

    tokens = jnp.concatenate(
        [pick(prompt_in, group), prompt_got, pick(cont_in, group), got[:rows]], axis=0
    )
    encoder = jnp.concatenate([pick(enc_out, group), got[rows:]], axis=0)
    enc_other = swap_seq(encoder, 1)

    def square(array, index):
        if owned_rows % 8 == 0:
            return array, (array.shape[0], owned_rows, width), (0, index, 0)
        part = array[:, index * owned_rows : (index + 1) * owned_rows].reshape(-1, width)
        return part, part.shape, (0, 0)

    front, back = [g.result() for g in one_parts]
    self_query, self_key, self_value = square(front, 0), square(front, 1), square(back, 0)
    tail = back[:, owned_rows:]
    owners = parts * blocks
    counts = 13 * owned_rows
    slots = tail.reshape(owners, 8, -1, 128)[:, :, :2, :owned_rows]
    vecs = slots.transpose(2, 1, 0, 3).reshape(16, width)[:13]
    biases = tail[:, 5, 128 : 128 + hidden_rows].reshape(chunks, width)
    vecs = widen(jnp.concatenate([vecs, biases], axis=0))

    queries, own = project(tokens, [self_query, self_key, self_value], vecs)
    own = pump(two_parts, two_parts, own)
    other = swap_seq(own, 1)
    mixed, logsum = self_attend(ids, queries, own, other)
    mixed = pump(two_parts, two_parts, mixed)
    mixed = pump(two_parts, [], mixed)
    front, back = [g.result() for g in two_parts]
    self_out, cross_query = square(front, 0), square(back, 0)
    cot_sent = jnp.concatenate([pick(v, 1 - group) for v in (prompt_cot, cont_cot)], axis=0)
    cot_sent, mixed = tie(cot_sent, mixed)
    cot_got = swap_seq(cot_sent, 3)
    first_pre, first_low, cross_queries = self_finish(tokens, mixed, self_out, cross_query, vecs)
    cross_queries, cot_got, feed = tie(cross_queries, cot_got, feed)
    cross_key, cross_value, cross_out = [square(feed, 2 * chunks + i) for i in range(3)]
    both = jnp.concatenate([encoder, enc_other], axis=0)
    (cross_keys,) = project(both, [cross_key, cross_value], vecs)
    cross_mixed, cross_logsum, second_pre, second_low = cross_attend(
        cross_queries, cross_keys, first_pre, cross_out, vecs
    )
    upstream = jnp.concatenate(
        [pick(prompt_cot, group), cot_got[:rows], pick(cont_cot, group), cot_got[rows:]], axis=0
    )
    slope, result, third_grad, third_low, sums, outer_pair = feed_forward(
        ids, second_pre, second_low, upstream, feed, vecs, chunks, owned_rows
    )

    def send_back(own, *values):
        away = jnp.concatenate([own[rows : 2 * rows], own[3 * rows :]], axis=0)
        tied = tie(away, *values)
        return (own, swap_seq(tied[0], 3)) + tuple(tied[1:])

    def place(own, back):
        kept = (own[:rows], own[2 * rows : 3 * rows])
        back = (back[:rows], back[rows:])
        return [
            jnp.where(group == 0, jnp.stack([a, b]), jnp.stack([b, a])) for a, b in zip(kept, back)
        ]

    bits = dp_bits[::-1]
    x_first = [lo, hi] + bits
    y_first = [lo, bits[0], hi] + bits[1:]
    outer_chain = Scatter(moves, [outer_pair], x_first)
    third_low = depart([outer_chain], third_low)
    result, result_back, third_low = send_back(result, third_low)
    second_grad, cross_mix, sums, inner_pair = inner_backward(
        ids, third_grad, third_low, sums, second_pre, second_low, slope, feed, cross_out, vecs, chunks,
        owned_rows,
    )
    cross_mix, result_back = tie(cross_mix, result_back)
    prompt_out, cont_out = place(result, result_back)
    inner_chain = Scatter(moves, [inner_pair], y_first)
    feed_chains = [outer_chain, inner_chain]
    cross_mix = receive([outer_chain], cross_mix)
    cross_mix = depart([inner_chain], cross_mix)
    cross_mix = depart([outer_chain], cross_mix)
    cross_mix = advance([inner_chain], cross_mix)
    enc_part, first_grad, mix, sums, query_pair, key_pair = cross_backward(
        ids, cross_queries, cross_keys, cross_mixed, cross_mix, cross_logsum, first_low, first_pre,
        second_grad, mixed, sums, both, cross_query, self_out, cross_key, cross_value, vecs, owned_rows,
    )
    mix, enc_part = receive(feed_chains, mix, enc_part)
    cross_chains = [
        Scatter(moves, [query_pair], x_first),
        Scatter(moves, [key_pair], y_first),
    ]
    enc_half = encoder.shape[0]
    enc_there = swap_seq(enc_part[enc_half:], 1)
    enc_rows = enc_out.shape[1]
    mix = depart(cross_chains + feed_chains, mix)
    halfway = HEADS // 4
    one = self_backward(ids, queries, own, other, mixed, mix, logsum, 0, halfway)
    tied = receive(cross_chains, enc_there, outer_chain.got, inner_chain.got, mix, *one)
    enc_there, outer_chain.got, inner_chain.got, mix = tied[:4]
    one = tied[4:]
    enc_back = low(widen(enc_part[:enc_half]) + widen(enc_there))
    enc_sent, mix = tie(enc_back[enc_rows:], mix)
    enc_got = swap_seq(enc_sent, 3)
    rest = jnp.concatenate([c.total() for c in feed_chains], axis=-2)
    rest = rest.reshape((-1,) + rest.shape[-2:])
    lines = [[i for i in range(blocks) if i % 2 == side] for side in range(2)]
    rest = lax.psum_scatter(
        rest, "dp", scatter_dimension=0, axis_index_groups=lines, tiled=True
    )[0]
    mix = depart(cross_chains, mix)
    two = self_backward(ids, queries, own, other, mixed, mix, logsum, halfway, HEADS // 2)
    tied = receive(cross_chains, enc_got, *two)
    enc_got, two = tied[0], tied[1:]
    sent = [tie(h[2], *[c.away for c in cross_chains])[0] for h in (one, two)]
    got_one, got_two = [swap_seq(v, 1) for v in sent]
    part, sums, self_query_pair = query_backward(
        ids, tokens, (one[0], two[0]), (one[3], two[3]), sums, first_grad, self_query, owned_rows
    )
    got_one, got_two, part = tie(got_one, got_two, part)
    bias_sums = sums[INNER_B : INNER_B + chunks].reshape(owners, hidden_rows)
    sums = sums[:13].reshape(13, owners, owned_rows).transpose(1, 0, 2).reshape(owners, counts)
    sums = low(jnp.concatenate([sums, bias_sums], axis=1))
    sums = jnp.pad(sums[:, None, :], ((0, 0), (0, 7), (0, width - counts - hidden_rows)))
    sums = sums.reshape(-1, 2, 8, width)
    sums_pair = (
        lax.dynamic_index_in_dim(sums, seq & 1, 1, keepdims=False),
        lax.dynamic_index_in_dim(sums, 1 - (seq & 1), 1, keepdims=False),
    )
    query_chain = Scatter(moves, [self_query_pair, sums_pair], x_first)
    got_one = depart(cross_chains + [query_chain], got_one)
    total, key_pair, value_pair = key_weights(
        ids, tokens, (one[1], two[1]), (got_one, got_two), owned_rows
    )
    key_chains = [Scatter(moves, [key_pair], x_first), Scatter(moves, [value_pair], y_first)]
    total = receive(cross_chains + [query_chain], total)
    cross_last = joined(cross_chains)
    total = depart(key_chains + [query_chain, cross_last], total)
    token_grad = token_backward(total, part, self_key, self_value)
    token_grad = receive(key_chains + [query_chain, cross_last], token_grad)
    depart(key_chains + [query_chain, cross_last])
    cross_last.got = receive(key_chains, cross_last.got)
    depart(key_chains)
    totals = [query_chain.total()]
    key_chains[0].got, key_chains[1].got, totals[0] = tie(
        key_chains[0].got, key_chains[1].got, totals[0]
    )
    totals = jnp.concatenate([c.total() for c in key_chains] + totals, axis=-2)
    totals = totals.reshape((-1,) + totals.shape[-2:])
    token_grad, token_back, totals = send_back(token_grad, totals)
    if totals.shape[0] <= 4:
        keep, gots = line_sends(moves, totals, 1)
        tied = tie(*gots, token_back)
        gots, token_back = tied[:-1], tied[-1]
        tail_held = widen(keep) + sum(widen(g) for g in gots)
    else:
        tail_held = widen(
            lax.psum_scatter(totals, "dp", scatter_dimension=0, axis_index_groups=lines, tiled=True)[0]
        )
    while cross_last.got is not None:
        receive([cross_last])
        if cross_last.order:
            cross_last.ship()

    def cut_rows(held, sizes):
        ends = [sum(sizes[: i + 1]) for i in range(len(sizes))]
        return [held[e - n : e] for e, n in zip(ends, sizes)]

    self_key_grad, self_value_grad, self_query_grad, vec = cut_rows(
        tail_held, [owned_rows, owned_rows, owned_rows, 8]
    )
    cross_held = cross_last.held.reshape(-1, owned_rows, width)
    vec = vec[0]
    prompt_grad, cont_grad = place(token_grad, token_back)
    enc_grad = jnp.where(
        group == 0,
        jnp.stack([enc_back[:enc_rows], enc_got]),
        jnp.stack([enc_got, enc_back[:enc_rows]]),
    )

    rest = widen(rest)
    outer_mat_grad = rest[:hidden_rows]
    inner_mat_grad = jnp.concatenate(
        [rest[hidden_rows + i * owned_rows : hidden_rows + (i + 1) * owned_rows] for i in range(chunks)],
        axis=1,
    )
    vec_out = [vec[i * owned_rows : (i + 1) * owned_rows] for i in range(13)]
    inner_bias_out = vec[counts : counts + hidden_rows]
    return (
        prompt_out,
        cont_out,
        prompt_grad,
        cont_grad,
        enc_grad,
        self_query_grad,
        vec_out[0],
        self_key_grad,
        self_value_grad,
        vec_out[1],
        cross_held[1],
        vec_out[2],
        vec_out[3],
        vec_out[4],
        cross_held[0],
        vec_out[5],
        cross_held[2],
        cross_held[3],
        vec_out[6],
        cross_held[4],
        vec_out[7],
        vec_out[8],
        vec_out[9],
        inner_mat_grad,
        inner_bias_out,
        outer_mat_grad,
        vec_out[10],
        vec_out[11],
        vec_out[12],
    )


def solution(mesh):
    rows_spec = P("dp", "seq", None)
    mat, vec = P(("dp", "seq"), None), P(("dp", "seq"))
    weights = (
        mat,
        vec,
        mat,
        mat,
        vec,
        mat,
        vec,
        vec,
        vec,
        mat,
        vec,
        mat,
        mat,
        vec,
        mat,
        vec,
        vec,
        vec,
        mat,
        vec,
        mat,
        vec,
        vec,
        vec,
    )
    in_specs = (rows_spec, rows_spec, rows_spec, P("dp"), rows_spec, rows_spec) + weights
    out_specs = (rows_spec,) * 5 + weights
    return jax.shard_map(body, mesh=mesh, in_specs=in_specs, out_specs=out_specs, check_vma=False)
```
